32 devices in a mesh: fsdp: 8 (over z, y), seq: 4 (over x, core).
Axes of the slice: x: 2, y: 2, z: 4, core: 2. Of those that a mesh axis runs over, the one named last changes fastest.
Arguments:
- tokens: bfloat16 [8, 1024, 2048], P(None, 'fsdp', 'seq'), may hold values from -6 to 6
- cotangent: bfloat16 [8, 1024, 2048], P(None, 'fsdp', 'seq'), may hold values from -6 to 6
- query_weight: bfloat16 [2048, 2048], P('fsdp'), may hold values from -0.125 to 0.125
- key_matrix: bfloat16 [2048, 1024], P('fsdp'), may hold values from -0.125 to 0.125
- value_matrix: bfloat16 [2048, 1024], P('fsdp'), may hold values from -0.125 to 0.125
- output_weight: bfloat16 [2048, 2048], P('fsdp'), may hold values from -1 to 1
- gate_weight: bfloat16 [2048, 8192], P('fsdp'), may hold values from -0.125 to 0.125
- up_weight: bfloat16 [2048, 8192], P('fsdp'), may hold values from -0.125 to 0.125
- down_weight: bfloat16 [8192, 2048], P('fsdp'), may hold values from -0.0625 to 0.0625
- prenorm_gain: bfloat16 [2048], P('fsdp'), may hold values from 0.5 to 1.5
- midnorm_gain: bfloat16 [2048], P('fsdp'), may hold values from 0.5 to 1.5
- seq_len: int32 [8], replicated, may hold values from 512 to 1024, as said below
- stream_order: int32 [8], replicated, may hold values from 0 to 7, each once
Outputs:
- block_output: bfloat16 [8, 1024, 2048], P(None, 'fsdp', 'seq')
- token_gradient: bfloat16 [8, 1024, 2048], P(None, 'fsdp', 'seq')
- query_gradient: float32 [2048, 2048], P('fsdp')
- key_gradient: float32 [2048, 1024], P('fsdp')
- value_gradient: float32 [2048, 1024], P('fsdp')
- output_gradient: float32 [2048, 2048], P('fsdp')
- gate_gradient: float32 [2048, 8192], P('fsdp')
- up_gradient: float32 [2048, 8192], P('fsdp')
- down_gradient: float32 [8192, 2048], P('fsdp')
- prenorm_gradient: float32 [2048], P('fsdp')
- midnorm_gradient: float32 [2048], P('fsdp')
The draws below stay inside these ranges and needn't reach their ends.
Inputs may be any that keep to these rules, and one draw needn't show every extreme that they name: `seq_len`: in every draw one sequence has 1024 tokens and another 512. `stream_order`: a permutation of the groups.
All inputs are finite; a program needn't handle non-finite values.
Results may differ from the reference program's by a relative error of at most 0.02.
Values may be sent and summed in bfloat16 or wider, within the bound.
No kernel may reach another device: no remote copies, remote signals or barrier semaphores. Data moves between devices by JAX's collectives and lax.ppermute only.
A program may use at most 512 MiB of HBM per device.

```python
import math
import jax
import jax.numpy as jnp
from jax import lax

D = 2048
QUERY_HEADS = 8
KEY_VALUE_HEADS = 4
HEAD_SIZE = 256
FF = 8192
BLK = 128
QBLK = 512
SEQS = 8
PADDED_ROWS = 1024
MIN_LEN = 512
SLOTS = 8
KVW = 1024


def draw_seq_len(key, part):
    length_key = jax.random.fold_in(key, 11)
    order_key = jax.random.fold_in(key, 12)
    lengths = jax.random.randint(length_key, (SEQS,), MIN_LEN, PADDED_ROWS + 1, dtype=jnp.int32)
    chosen = jax.random.permutation(order_key, SEQS)
    lengths = lengths.at[chosen[0]].set(PADDED_ROWS)
    return lengths.at[chosen[1]].set(MIN_LEN)


def with_spikes(values, key, source, target, blocks, factor):
    def block_of(axis_at):
        return (jnp.arange(values.shape[axis_at]) // (values.shape[axis_at] // blocks)).reshape((-1,) + (1,) * (values.ndim - 1 - axis_at))

    near = jax.random.permutation(key, blocks)[block_of(target)]
    far = (block_of(target) + blocks // 2) % blocks
    return jnp.where((block_of(source) == near) | (block_of(source) == far), factor * values, values)


def shard_levels(own_key, shape, shards, smallest, top_value):
    def one(position, parts):
        steps = jax.random.uniform(jax.random.fold_in(jax.random.fold_in(own_key, 6), position), (parts,), jnp.float32, smallest / len(shards), top_value / len(shards))
        return jnp.repeat(jnp.exp(steps), shape[position] // parts).reshape((-1,) + (1,) * (len(shape) - position - 1))

    gain = one(*shards[0])
    for cut in shards[1:]:
        gain = gain * one(*cut)
    return gain


def gaussian(stream_key, extent, width, most, cuts=(), kind=jnp.bfloat16):
    values = jax.random.normal(stream_key, extent, jnp.float32) * width
    if len(cuts) > 0:
        values = shard_levels(stream_key, extent, cuts, -0.22, 0.18) * values
    return jnp.clip(values, min=-most, max=most).astype(kind)


def noise_with(own_key, shape, deviation, limit, split, heavy, kind=jnp.bfloat16):
    entries = deviation * jax.random.normal(own_key, shape, jnp.float32)
    if split:
        entries = entries * shard_levels(own_key, shape, split, -0.22, 0.18)
    return jnp.clip(with_spikes(entries, jax.random.fold_in(own_key, 3), *heavy), -limit, limit).astype(kind)


def setup_inputs(seed: int = 0) -> dict:
    splits = jax.random.split(jax.random.key(seed), 14)
    return {
        "tokens": noise_with(splits[0], (SLOTS, SEQS * BLK, D), 1.0, 6.0, ((1, 8), (2, 4)), (1, 2, 8, 2.0)),
        "cotangent": gaussian(splits[1], (SLOTS, SEQS * BLK, D), 1.0, 6.0, ((1, 8), (2, 4))),
        "query_weight": gaussian(splits[2], (D, D), D ** -0.5, 0.125, ((0, 8),)),
        "key_matrix": gaussian(splits[3], (D, KVW), D ** -0.5, 0.125, ((0, 8),)),
        "value_matrix": gaussian(splits[4], (D, KVW), D ** -0.5, 0.125, ((0, 8),)),
        "output_weight": gaussian(splits[5], (D, D), (D // 64) ** -0.5, 1.0, ((0, 8),)),
        "gate_weight": gaussian(splits[6], (D, FF), D ** -0.5, 0.125, ((0, 8),)),
        "up_weight": gaussian(splits[7], (D, FF), D ** -0.5, 0.125, ((0, 8),)),
        "down_weight": gaussian(splits[8], (FF, D), FF ** -0.5, 0.0625, ((0, 8),)),
        "prenorm_gain": jnp.clip(0.5 + 1.0 * jax.random.uniform(splits[9], (D,), jnp.float32) ** shard_levels(splits[9], (D,), ((0, 8),), -0.2, 0.2), 0.5, 1.5).astype(jnp.bfloat16),
        "midnorm_gain": jnp.clip(0.5 + 1.0 * jax.random.uniform(splits[10], (D,), jnp.float32) ** shard_levels(splits[10], (D,), ((0, 8),), -0.2, 0.2), 0.5, 1.5).astype(jnp.bfloat16),
        "seq_len": draw_seq_len(jax.random.fold_in(splits[13], 71), 0),
        "stream_order": jax.random.permutation(splits[12], SEQS).astype(jnp.int32),
    }


EPS_NORM = 1e-06
ROPE_BASE = 1000042.0
MASK_FILL = -1e+30

@jax.custom_vjp
def reduced_precision(v):
    return lax.optimization_barrier(v.astype(jnp.bfloat16)).astype(jnp.float32)

@jax.custom_vjp
def reduced_precision_back(v):
    return v

def low_keep(v):
    return (reduced_precision(v), None)

def low_pass(kept, grad):
    return (grad,)

def back_keep(v):
    return (v, None)

def back_low(kept, grad):
    return (reduced_precision(grad),)
reduced_precision.defvjp(low_keep, low_pass)
reduced_precision_back.defvjp(back_keep, back_low)

def matrix_product(left_arg, right_arg):
    return jnp.dot(left_arg, right_arg, precision=lax.Precision.HIGHEST)

def rms_norm(hidden, gain_vec):
    factor = lax.rsqrt(lax.optimization_barrier(jnp.mean(hidden * hidden, axis=-1, keepdims=True)) + EPS_NORM)
    return hidden * factor * gain_vec

def rope_tables(positions):
    half_dim = HEAD_SIZE // 2
    frequency = jnp.exp(jnp.arange(half_dim, dtype=jnp.float32) * (-2.0 * math.log(ROPE_BASE) / HEAD_SIZE))
    angles = positions[:, None] * frequency[None, :]
    return (jnp.cos(angles)[:, None, :], jnp.sin(angles)[:, None, :])

def rotate(vectors, cos_t, sin_t):
    half_dim = vectors.shape[-1] // 2
    front_half = vectors[..., :half_dim]
    behind = vectors[..., half_dim:]
    return jnp.concatenate([front_half * cos_t - behind * sin_t, behind * cos_t + front_half * sin_t], axis=-1)

def attention(queries, keys_rot, value_rows, valid_rows):
    heads_per_group = QUERY_HEADS // KEY_VALUE_HEADS
    keys_all = jnp.repeat(keys_rot, heads_per_group, axis=1)
    values_all = jnp.repeat(value_rows, heads_per_group, axis=1)
    key_pos = jnp.arange(PADDED_ROWS, dtype=jnp.int32)
    factor = 1.0 / math.sqrt(HEAD_SIZE)

    def one_block(first_row):
        query_rows = lax.dynamic_slice_in_dim(queries, first_row, QBLK, 0)
        scores = reduced_precision_back(jnp.einsum('qhd,khd->hqk', query_rows, keys_all, precision=lax.Precision.HIGHEST) * factor)
        query_pos = first_row + jnp.arange(QBLK, dtype=jnp.int32)
        allowed = (key_pos[None, :] <= query_pos[:, None]) & (valid_rows[None, :] > 0.5)
        scores = jnp.where(allowed[None, :, :], scores, MASK_FILL)
        prob_rows = reduced_precision(jax.nn.softmax(scores, axis=-1))
        return jnp.einsum('hqk,khd->qhd', prob_rows, values_all, precision=lax.Precision.HIGHEST)
    block_firsts = jnp.arange(PADDED_ROWS // QBLK, dtype=jnp.int32) * QBLK
    blocks = lax.map(jax.checkpoint(one_block), block_firsts)
    return blocks.reshape(PADDED_ROWS, QUERY_HEADS * HEAD_SIZE)

def block_layer(hidden_in, query_weight, key_matrix, value_matrix, output_weight, gate_weight, up_weight, down_weight, prenorm_gain, midnorm_gain, valid_rows, cos_t, sin_t):
    hidden_zero = hidden_in * valid_rows[:, None]
    normalized_rows = reduced_precision(rms_norm(hidden_zero, prenorm_gain))
    query_pre = reduced_precision_back(matrix_product(normalized_rows, query_weight)).reshape(PADDED_ROWS, QUERY_HEADS, HEAD_SIZE)
    key_before_rotation = reduced_precision_back(matrix_product(normalized_rows, key_matrix)).reshape(PADDED_ROWS, KEY_VALUE_HEADS, HEAD_SIZE)
    queries = reduced_precision(reduced_precision_back(rotate(query_pre, cos_t, sin_t)))
    keys_rot = reduced_precision(reduced_precision_back(rotate(key_before_rotation, cos_t, sin_t)))
    value_rows = reduced_precision(reduced_precision_back(matrix_product(normalized_rows, value_matrix))).reshape(PADDED_ROWS, KEY_VALUE_HEADS, HEAD_SIZE)
    mixed_heads = reduced_precision(reduced_precision_back(attention(queries, keys_rot, value_rows, valid_rows)))
    hidden_one = hidden_zero + reduced_precision_back(matrix_product(mixed_heads, output_weight))
    normed_two = reduced_precision(rms_norm(hidden_one, midnorm_gain))
    gate_pre = reduced_precision_back(matrix_product(normed_two, gate_weight))
    up_pre = reduced_precision_back(matrix_product(normed_two, up_weight))
    activated = reduced_precision(jax.nn.silu(gate_pre) * up_pre)
    return (hidden_one + reduced_precision_back(matrix_product(activated, down_weight))) * valid_rows[:, None]

def reference(tokens, cotangent, query_weight, key_matrix, value_matrix, output_weight, gate_weight, up_weight, down_weight, prenorm_gain, midnorm_gain, seq_len, stream_order):
    total_rows = SLOTS * SEQS * BLK
    zeros_tail = jnp.zeros((PADDED_ROWS, D), jnp.float32)
    stream_in = jnp.concatenate([tokens.reshape(total_rows, D).astype(jnp.float32), zeros_tail], axis=0)
    stream_cot = jnp.concatenate([cotangent.reshape(total_rows, D).astype(jnp.float32), zeros_tail], axis=0)
    block_count = ((seq_len + BLK - 1) // BLK).astype(jnp.int32)
    ordered = block_count[stream_order]
    firsts = (jnp.cumsum(ordered) - ordered).astype(jnp.int32)
    seq_start = jnp.zeros((SEQS,), jnp.int32).at[stream_order].set(firsts)
    float_weights = tuple((weight_arg.astype(jnp.float32) for weight_arg in (query_weight, key_matrix, value_matrix, output_weight, gate_weight, up_weight, down_weight, prenorm_gain, midnorm_gain)))
    cos_t, sin_t = rope_tables(jnp.arange(PADDED_ROWS, dtype=jnp.float32))
    row_index = jnp.arange(PADDED_ROWS, dtype=jnp.int32)

    def one_group(state_carry, group_id):
        out_stream, back_stream, sums_now = state_carry
        row_zero = (seq_start[group_id] * BLK).astype(jnp.int32)
        seq_in = lax.dynamic_slice_in_dim(stream_in, row_zero, PADDED_ROWS, 0)
        seq_cot = lax.dynamic_slice_in_dim(stream_cot, row_zero, PADDED_ROWS, 0)
        valid_rows = (row_index < seq_len[group_id]).astype(jnp.float32)

        def forward(hidden_in, *weight_args):
            return block_layer(hidden_in, *weight_args, valid_rows, cos_t, sin_t)
        result, pullback = jax.vjp(forward, seq_in, *float_weights)
        gradients = pullback(seq_cot)
        old_out = lax.dynamic_slice_in_dim(out_stream, row_zero, PADDED_ROWS, 0)
        out_stream = lax.dynamic_update_slice_in_dim(out_stream, old_out + result, row_zero, 0)
        old_back = lax.dynamic_slice_in_dim(back_stream, row_zero, PADDED_ROWS, 0)
        back_stream = lax.dynamic_update_slice_in_dim(back_stream, old_back + gradients[0], row_zero, 0)
        sums_now = tuple((total_old + total_new for total_old, total_new in zip(sums_now, gradients[1:])))
        return ((out_stream, back_stream, sums_now), None)
    start_state = (jnp.zeros((total_rows + PADDED_ROWS, D), jnp.float32), jnp.zeros((total_rows + PADDED_ROWS, D), jnp.float32), tuple((jnp.zeros(weight_arg.shape, jnp.float32) for weight_arg in float_weights)))
    final_state, unused = lax.scan(one_group, start_state, jnp.arange(SEQS, dtype=jnp.int32))
    out_stream, back_stream, totals = final_state
    block_output = out_stream[:total_rows].reshape(SLOTS, SEQS * BLK, D).astype(jnp.bfloat16)
    token_gradient = back_stream[:total_rows].reshape(SLOTS, SEQS * BLK, D).astype(jnp.bfloat16)
    return (block_output, token_gradient, totals[0], totals[1], totals[2], totals[3], totals[4], totals[5], totals[6], totals[7], totals[8])
```

```python
import math

import jax
import jax.numpy as jnp
from jax import lax
from jax.sharding import Mesh
from jax.sharding import PartitionSpec as P

QUERY_HEADS = 8
KEY_VALUE_HEADS = 4
HEAD_SIZE = 256

EPS_NORM = 1e-06
ROPE_BASE = 1000042.0
MASK_FILL = -1e30
AXES = ("z", "y", "x", "c")
F32 = jnp.float32
BF16 = jnp.bfloat16


def dot(a, b, dims):
    return lax.dot_general(a, b, (dims, ((), ())), preferred_element_type=F32)


def mm(a, b):
    return dot(a, b, ((1,), (0,)))


def mm_nt(a, b):
    return dot(a, b, ((1,), (1,)))


def mm_tn(a, b):
    return dot(a, b, ((0,), (0,)))


class Links:
    def __init__(self, planes):
        self.planes = planes

        def pairs(move):
            out = []
            for z in range(planes):
                for y in range(2):
                    for x in range(2):
                        for c in range(2):
                            a, b, d, e = move(z, y, x, c)
                            out.append((((z * 2 + y) * 2 + x) * 2 + c, ((a * 2 + b) * 2 + d) * 2 + e))
            return out

        self.px = pairs(lambda z, y, x, c: (z, y, 1 - x, c))
        self.py = pairs(lambda z, y, x, c: (z, 1 - y, x, c))
        self.pc = pairs(lambda z, y, x, c: (z, y, x, 1 - c))
        self.pz = pairs(lambda z, y, x, c: ((z + 1) % planes, y, x, c))

    def x(self, a):
        return lax.ppermute(a, AXES, self.px)

    def y(self, a):
        return lax.ppermute(a, AXES, self.py)

    def c(self, a):
        return lax.ppermute(a, AXES, self.pc)

    def z(self, a):
        return lax.ppermute(a, AXES, self.pz)

    def gather_rows(self, a):
        n = a.shape[0]
        ax = self.x(a)
        ay = self.y(a)
        dx = self.x(ay[: n // 2])
        dy = self.y(ax[n // 2 :])
        return jnp.concatenate([a, ax, ay, dx, dy], axis=0)

    def scatter_rows(self, part):
        n, d = part.shape[0] // 4, part.shape[1]
        h = d // 2
        p = part.reshape(4, n, d)
        left, right = p[:, :, :h], p[:, :, h:]
        gl = self.x(jnp.stack([left[1], left[3]]).astype(BF16))
        gr = self.y(jnp.stack([right[2], right[3]]).astype(BF16))
        l_far = self.y((left[2] + gl[1]).astype(BF16))
        r_far = self.x((right[1] + gr[1]).astype(BF16))
        l_own = left[0] + gl[0] + l_far
        r_own = right[0] + gr[0] + r_far
        return jnp.concatenate([l_own, r_own], axis=1)

    def gather_planes(self, a):
        if self.planes > 4:
            return lax.all_gather(a, "z", axis=0, tiled=True)
        me = lax.axis_index("z")
        out = jnp.zeros((self.planes,) + a.shape, a.dtype)
        now = a
        for k in range(self.planes):
            if k:
                now = self.z(now)
            out = lax.dynamic_update_slice(
                out, now[None], (lax.rem(me - k + self.planes, self.planes), 0, 0)
            )
        return out.reshape(self.planes * a.shape[0], a.shape[1])


def pair(bit, own, other):
    return jnp.stack([jnp.where(bit == 0, own, other), jnp.where(bit == 0, other, own)])


def rope_tables(positions):
    half_dim = HEAD_SIZE // 2
    frequency = jnp.exp(jnp.arange(half_dim, dtype=F32) * (-2.0 * math.log(ROPE_BASE) / HEAD_SIZE))
    angles = positions.astype(F32)[:, None] * frequency[None, :]
    return jnp.cos(angles), jnp.sin(angles)


def rotate(v, cos_t, sin_t):
    h = HEAD_SIZE // 2
    a, b = v[:, :h], v[:, h:]
    return jnp.concatenate([a * cos_t - b * sin_t, b * cos_t + a * sin_t], axis=-1).astype(BF16)


def unrotate(v, cos_t, sin_t):
    h = HEAD_SIZE // 2
    a, b = v[:, :h], v[:, h:]
    return jnp.concatenate([a * cos_t + b * sin_t, b * cos_t - a * sin_t], axis=-1).astype(BF16)


def norm_factor(hidden):
    return lax.rsqrt(jnp.mean(hidden * hidden, axis=-1, keepdims=True) + EPS_NORM)


def norm_backward(upstream, hidden, factor, gain_vec):
    scaled = upstream * gain_vec
    gain_part = jnp.sum(upstream * hidden * factor, axis=0)
    inner_sum = jnp.mean(scaled * hidden, axis=-1, keepdims=True)
    return (factor * scaled - hidden * (factor * factor * factor) * inner_sum, gain_part)


def make_body(planes):
    links = Links(planes)

    def body(
        tokens,
        cotangent,
        query_weight,
        key_matrix,
        value_matrix,
        output_weight,
        gate_weight,
        up_weight,
        down_weight,
        prenorm_gain,
        midnorm_gain,
        seq_len,
        stream_order,
    ):
        groups = 2 * planes
        z_me = lax.axis_index("z")
        y_me = lax.axis_index("y")
        x_me = lax.axis_index("x")
        c_me = lax.axis_index("c")
        slots, blk, quarter = tokens.shape
        width = 4 * quarter
        rank = 4 * y_me + 2 * x_me + c_me
        head = 2 * y_me + x_me
        shard = query_weight.shape[0]
        ff = gate_weight.shape[1]
        piece = ff // groups // 4

        nblk = (seq_len + blk - 1) // blk
        member = (stream_order[:, None] == jnp.arange(groups, dtype=jnp.int32)[None, :]).astype(
            jnp.int32
        )
        ordered = jnp.sum(member * nblk[None, :], axis=1)
        firsts = jnp.cumsum(ordered) - ordered
        seq_start = jnp.sum(member * firsts[:, None], axis=0)
        group_me = 2 * z_me + y_me
        offset = lax.rem(group_me - lax.rem(seq_start, groups) + groups, groups)
        has = offset < nblk
        slot_of = jnp.where(has, (seq_start + offset) // groups, -1)
        routes = (jnp.arange(slots, dtype=jnp.int32)[:, None] == slot_of[None, :]).astype(BF16)

        mine = 2 * z_me + c_me
        picked = jnp.arange(groups, dtype=jnp.int32) == mine
        my_start = jnp.sum(jnp.where(picked, seq_start, 0))
        my_len = jnp.sum(jnp.where(picked, seq_len, 0))

        def block_places(y):
            first = lax.rem(y + my_start, 2)
            plane = lax.rem((my_start + first) // 2, planes)
            k = jnp.arange(4, dtype=jnp.int32)
            if planes == 4:
                k = lax.rem(k - plane + planes, planes)
            return first + 2 * k, plane

        places_own, plane_own = block_places(y_me)
        places_far, _ = block_places(1 - y_me)

        def row_positions(places, x):
            two = lax.dynamic_slice(places, (2 * x,), (2,))
            return (two[:, None] * blk + jnp.arange(blk, dtype=jnp.int32)[None, :]).reshape(-1)

        positions = row_positions(places_own, x_me)
        positions_all = jnp.concatenate(
            [
                positions,
                row_positions(places_own, 1 - x_me),
                row_positions(places_far, x_me),
                row_positions(places_far, 1 - x_me),
            ]
        )
        valid = (positions < my_len).astype(F32)[:, None]
        seq_rows = 8 * blk
        rows = 2 * blk

        def route_in(stream):
            send = jnp.einsum("jg,jrf->grf", routes, stream, preferred_element_type=F32).astype(BF16)
            got = lax.all_to_all(send, ("z", "c"), split_axis=0, concat_axis=0, tiled=True)
            got = got.reshape(planes, 2, blk, quarter)
            if planes > 4:
                got = jnp.roll(got, -plane_own, axis=0)[:4]
            got = lax.all_to_all(got, "x", split_axis=0, concat_axis=1, tiled=True)
            return jnp.transpose(got, (0, 2, 1, 3)).reshape(rows, width)

        def route_out(out_rows):
            send = lax.all_to_all(
                out_rows.reshape(2, blk, width), "x", split_axis=2, concat_axis=0, tiled=True
            )
            send = jnp.transpose(send.reshape(4, blk, 2, quarter), (0, 2, 1, 3))
            if planes > 4:
                send = jnp.pad(send, ((0, planes - 4), (0, 0), (0, 0), (0, 0)))
                send = jnp.roll(send, plane_own, axis=0)
            send = send.reshape(groups, blk, quarter)
            got = lax.all_to_all(send, ("z", "c"), split_axis=0, concat_axis=0, tiled=True)
            return jnp.einsum("jg,grf->jrf", routes, got, preferred_element_type=F32).astype(BF16)

        def plane_rows(own_part, far_part):
            got = links.y(far_part)
            both = pair(y_me, own_part, got)
            return both.reshape(2 * own_part.shape[0], own_part.shape[1])

        def attn_columns(r):
            q = lax.dynamic_slice(query_weight, (0, r * HEAD_SIZE), (shard, HEAD_SIZE))
            j = r // 2
            k = lax.dynamic_slice(key_matrix, (0, j * HEAD_SIZE), (shard, HEAD_SIZE))
            v = lax.dynamic_slice(value_matrix, (0, j * HEAD_SIZE), (shard, HEAD_SIZE))
            return jnp.concatenate([q, jnp.where(c_me == 0, k, v)], axis=1)

        def out_columns(r):
            at = lax.rem(r, 2) * (width // 2) + (r // 2) * (width // 8)
            return lax.dynamic_slice(output_weight, (0, at), (output_weight.shape[0], width // 8))

        def ff_columns(w, r):
            return jnp.concatenate(
                [
                    lax.dynamic_slice(w, (0, p * 8 * piece + r * piece), (shard, piece))
                    for p in range(planes)
                ],
                axis=1,
            )

        far = rank + 4 - 8 * y_me
        gain_rows = jnp.stack([prenorm_gain, midnorm_gain])
        gains = lax.all_gather(gain_rows, ("z", "y"), axis=1, tiled=True).astype(F32)
        gain_pre, gain_mid = gains[0], gains[1]

        rows_in = route_in(tokens)
        w_qkv = links.gather_planes(plane_rows(attn_columns(rank), attn_columns(far)))
        w_qkv_far = links.c(w_qkv)
        w_o_cols = links.gather_planes(plane_rows(out_columns(rank), out_columns(far)))
        w_o = lax.all_to_all(w_o_cols, ("y", "x"), split_axis=0, concat_axis=1, tiled=True)
        w_o_far = links.c(w_o)
        rows_cot = route_in(cotangent)
        w_gate = links.gather_planes(plane_rows(ff_columns(gate_weight, rank), ff_columns(gate_weight, far)))
        w_gate_far = links.c(w_gate)
        w_up = links.gather_planes(plane_rows(ff_columns(up_weight, rank), ff_columns(up_weight, far)))
        w_up_far = links.c(w_up)
        w_down = links.gather_planes(
            lax.dynamic_slice(down_weight, ((2 * x_me + c_me) * piece, 0), (piece, width))
        )
        w_down_far = links.c(w_down)

        hidden_zero = rows_in.astype(F32) * valid
        factor_pre = norm_factor(hidden_zero)
        normed = links.gather_rows((hidden_zero * factor_pre * gain_pre).astype(BF16))
        cos_t, sin_t = rope_tables(positions_all)
        pre_own = mm(normed, w_qkv)
        pre_far = mm(normed, w_qkv_far)
        first = c_me == 0
        even = jnp.where(first, pre_own, pre_far)
        odd = jnp.where(first, pre_far, pre_own)
        queries = (
            rotate(even[:, :HEAD_SIZE], cos_t, sin_t),
            rotate(odd[:, :HEAD_SIZE], cos_t, sin_t),
        )
        keys = rotate(even[:, HEAD_SIZE:], cos_t, sin_t)
        values = odd[:, HEAD_SIZE:].astype(BF16)
        factor = 1.0 / math.sqrt(HEAD_SIZE)
        allowed = (positions_all[None, :] <= positions_all[:, None]) & (
            positions_all[None, :] < my_len
        )

        def head_forward(q):
            scores = jnp.where(allowed, mm_nt(q, keys) * factor, MASK_FILL)
            top = jnp.max(scores, axis=-1, keepdims=True)
            exponent = jnp.exp(scores - top)
            total = jnp.sum(exponent, axis=-1, keepdims=True)
            probs = (exponent / total).astype(BF16)
            return mm(probs, values).astype(BF16), top + jnp.log(total)

        heads = [head_forward(q) for q in queries]
        mixed = jnp.concatenate([heads[0][0], heads[1][0]], axis=1)

        out_own = mm(mixed, w_o)
        out_far = mm(mixed, w_o_far)
        attn_part = jnp.concatenate(
            [jnp.where(first, out_own, out_far), jnp.where(first, out_far, out_own)], axis=1
        ).astype(BF16)
        hidden_one = hidden_zero + links.scatter_rows(attn_part)
        factor_mid = norm_factor(hidden_one)
        normed_two = links.gather_rows((hidden_one * factor_mid * gain_mid).astype(BF16))

        upstream = rows_cot.astype(F32) * valid
        down_in = links.gather_rows(upstream.astype(BF16))

        def ff_half(wg, wu, wd):
            gate_pre = mm(normed_two, wg)
            up_pre = mm(normed_two, wu)
            sig = jax.nn.sigmoid(gate_pre)
            gate_act = gate_pre * sig
            activated = (gate_act * up_pre).astype(BF16)
            act_grad = mm_nt(down_in, wd)
            gate_in = (act_grad * up_pre * sig * (1.0 + gate_pre * (1.0 - sig))).astype(BF16)
            up_in = (act_grad * gate_act).astype(BF16)
            return activated, gate_in, up_in

        act, gate_in, up_in = ff_half(w_gate, w_up, w_down)
        act_far, gate_in_far, up_in_far = ff_half(w_gate_far, w_up_far, w_down_far)
        dn_part = (
            mm_nt(gate_in, w_gate)
            + mm_nt(up_in, w_up)
            + mm_nt(gate_in_far, w_gate_far)
            + mm_nt(up_in_far, w_up_far)
        ).astype(BF16)
        normed_two_grad = links.scatter_rows(dn_part)
        ff_part = (mm(act, w_down) + mm(act_far, w_down_far)).astype(BF16)

        def both_cores(own_left, far_left, own_right, far_right):
            got = links.c(mm_tn(far_left, far_right).astype(BF16))
            return (mm_tn(own_left, own_right) + got).astype(BF16)

        def over_planes(g):
            return lax.psum_scatter(g, "z", scatter_dimension=0, tiled=True)

        g_down = over_planes(both_cores(act, act_far, down_in, down_in))
        g_gate = over_planes(both_cores(normed_two, normed_two, gate_in, gate_in_far))
        g_up = over_planes(both_cores(normed_two, normed_two, up_in, up_in_far))

        ff_out = links.scatter_rows(ff_part)
        block_rows = ((hidden_one + ff_out) * valid).astype(BF16)
        out_tokens = route_out(block_rows)

        mid_upstream, midnorm_part = norm_backward(normed_two_grad, hidden_one, factor_mid, gain_mid)
        hidden_one_grad = upstream + mid_upstream
        attn_in = links.gather_rows(hidden_one_grad.astype(BF16))
        half = width // 2
        attn_own = jnp.where(first, attn_in[:, :half], attn_in[:, half:])
        attn_far = jnp.where(first, attn_in[:, half:], attn_in[:, :half])
        mixed_grad = (mm_nt(attn_own, w_o) + mm_nt(attn_far, w_o_far)).astype(BF16)
        g_out = both_cores(mixed, mixed, attn_own, attn_far)

        dk = 0.0
        dv = 0.0
        dq = []
        for i in range(2):
            dmix = mixed_grad[:, i * HEAD_SIZE : (i + 1) * HEAD_SIZE]
            scores = jnp.where(allowed, mm_nt(queries[i], keys) * factor, MASK_FILL)
            probs = jnp.exp(scores - heads[i][1])
            dv = dv + mm_tn(probs.astype(BF16), dmix)
            prob_grad = mm_nt(dmix, values)
            inner = jnp.sum(prob_grad * probs, axis=-1, keepdims=True)
            score_grad = (probs * (prob_grad - inner)).astype(BF16) * factor
            dq.append(mm(score_grad, keys).astype(BF16))
            dk = dk + mm_tn(score_grad, queries[i])
        dk = dk.astype(BF16)
        dv = dv.astype(BF16)
        dq = [unrotate(t.astype(F32), cos_t, sin_t) for t in dq]
        dk = unrotate(dk.astype(F32), cos_t, sin_t)
        grad_even = jnp.concatenate([dq[0], dk], axis=1)
        grad_odd = jnp.concatenate([dq[1], dv], axis=1)
        d_own = jnp.where(first, grad_even, grad_odd)
        d_far = jnp.where(first, grad_odd, grad_even)
        g_qkv = both_cores(normed, normed, d_own, d_far)
        g_o_cols = lax.all_to_all(g_out, ("y", "x"), split_axis=1, concat_axis=0, tiled=True)
        g_attn = over_planes(jnp.concatenate([g_qkv, g_o_cols], axis=1))

        normed_grad = links.scatter_rows((mm_nt(d_own, w_qkv) + mm_nt(d_far, w_qkv_far)).astype(BF16))
        pre_upstream, prenorm_part = norm_backward(normed_grad, hidden_zero, factor_pre, gain_pre)
        token_rows = ((hidden_one_grad + pre_upstream) * valid).astype(BF16)
        grad_tokens = route_out(token_rows)

        def by_rank(g):
            n = g.shape[1]
            two = g.reshape(2, shard, n)
            own = jnp.where(y_me == 0, two[0], two[1])
            other = jnp.where(y_me == 0, two[1], two[0])
            got = pair(y_me, own, links.y(other))
            got = pair(x_me, got, links.x(got))
            got = pair(c_me, got, links.c(got))
            return jnp.transpose(got, (2, 1, 0, 3, 4)).reshape(8, shard, n)

        def ff_gradient(g):
            t = by_rank(g).reshape(8, shard, planes, piece)
            return jnp.transpose(t, (1, 2, 0, 3)).reshape(shard, ff).astype(F32)

        gate_gradient = ff_gradient(g_gate)
        up_gradient = ff_gradient(g_up)
        down_all = pair(x_me, g_down, links.x(g_down))
        down_all = pair(c_me, down_all, links.c(down_all))
        down_gradient = (
            jnp.transpose(down_all, (1, 0, 2, 3)).reshape(4 * piece, width).astype(F32)
        )
        t = by_rank(g_attn)

        def columns(a):
            return jnp.transpose(a, (1, 0, 2)).reshape(shard, -1).astype(F32)

        query_gradient = columns(t[:, :, :HEAD_SIZE])
        key_gradient = columns(t[0::2, :, HEAD_SIZE : 2 * HEAD_SIZE])
        value_gradient = columns(t[1::2, :, HEAD_SIZE : 2 * HEAD_SIZE])
        out_t = t[:, :, 2 * HEAD_SIZE :].reshape(4, 2, shard, width // 8)
        output_gradient = jnp.transpose(out_t, (2, 1, 0, 3)).reshape(shard, width).astype(F32)

        norm_parts = lax.psum(jnp.stack([prenorm_part, midnorm_part]), AXES)
        norm_own = lax.dynamic_slice(
            norm_parts, (0, group_me * prenorm_gain.shape[0]), (2, prenorm_gain.shape[0])
        )
        return (
            out_tokens,
            grad_tokens,
            query_gradient,
            key_gradient,
            value_gradient,
            output_gradient,
            gate_gradient,
            up_gradient,
            down_gradient,
            norm_own[0],
            norm_own[1],
        )

    return body


def solution(mesh):
    planes = mesh.shape["fsdp"] // 2
    grid = Mesh(mesh.devices.reshape(planes, 2, 2, 2), AXES)
    rows = ("z", "y")
    stream = P(None, rows, ("x", "c"))
    weight = P(rows, None)
    gain = P(rows)
    return jax.shard_map(
        make_body(planes),
        mesh=grid,
        in_specs=(stream, stream) + (weight,) * 7 + (gain, gain, P(), P()),
        out_specs=(stream, stream) + (weight,) * 7 + (gain, gain),
        check_vma=False,
    )
```

```python
import math

import jax
import jax.numpy as jnp
from jax import lax
from jax.experimental import pallas as pl
from jax.experimental.pallas import tpu as pltpu
from jax.sharding import Mesh
from jax.sharding import PartitionSpec as P

QUERY_HEADS = 8
KEY_VALUE_HEADS = 4
HEAD_SIZE = 256

EPS_NORM = 1e-06
ROPE_BASE = 1000042.0
MASK_FILL = -1e30
AXES = ("z", "y", "x", "c")
F32 = jnp.float32
BF16 = jnp.bfloat16


def dot(a, b, dims):
    return lax.dot_general(a, b, (dims, ((), ())), preferred_element_type=F32)


def mm(a, b):
    return dot(a, b, ((1,), (0,)))


def mm_nt(a, b):
    return dot(a, b, ((1,), (1,)))


def mm_tn(a, b):
    return dot(a, b, ((0,), (0,)))


def sync(*values):
    return lax.optimization_barrier(values)


def after(value, *others):
    return lax.optimization_barrier((value,) + others)[0]


class Links:
    def __init__(self, planes):
        self.planes = planes

        def pairs(move):
            out = []
            for z in range(planes):
                for y in range(2):
                    for x in range(2):
                        for c in range(2):
                            a, b, d, e = move(z, y, x, c)
                            out.append((((z * 2 + y) * 2 + x) * 2 + c, ((a * 2 + b) * 2 + d) * 2 + e))
            return out

        self.px = pairs(lambda z, y, x, c: (z, y, 1 - x, c))
        self.py = pairs(lambda z, y, x, c: (z, 1 - y, x, c))
        self.pxy = pairs(lambda z, y, x, c: (z, 1 - y, 1 - x, c))
        self.pc = pairs(lambda z, y, x, c: (z, y, x, 1 - c))
        self.pz = [
            pairs(lambda z, y, x, c, k=k: ((z + k) % planes, y, x, c)) for k in range(planes)
        ]
        self.pz_swap = []
        k = 1
        while k < planes:
            self.pz_swap.append(pairs(lambda z, y, x, c, k=k: (z ^ k, y, x, c)))
            k *= 2

    def x(self, a):
        return lax.ppermute(a, AXES, self.px)

    def y(self, a):
        return lax.ppermute(a, AXES, self.py)

    def c(self, a):
        return lax.ppermute(a, AXES, self.pc)

    def swap_chips(self, chunks):
        return [
            chunks[0],
            self.x(chunks[1]),
            self.y(chunks[2]),
            lax.ppermute(chunks[3], AXES, self.pxy),
        ]

    def sum_plane(self, a):
        for p in (self.pc, self.px, self.py):
            a = a + lax.ppermute(a, AXES, p)
        return a

    def sum_planes(self, a):
        for p in self.pz_swap:
            a = a + lax.ppermute(a, AXES, p)
        return a

    def gather_one(self, a):
        return self.x(a), self.y(a)

    def gather_two(self, ax, ay):
        m = ax.shape[0] // 2
        return self.x(ay[:m]), self.y(ax[m:])

    def scatter_one(self, left, right):
        n = left.shape[0] // 4
        l4 = left.reshape(4, n, left.shape[1])
        return self.x(jnp.stack([l4[1], l4[3]])), self.y(right[2 * n :].reshape(2, n, right.shape[1]))

    def scatter_two(self, left, right, gl, gr):
        n = left.shape[0] // 4
        l_far = self.y((left[2 * n : 3 * n].astype(F32) + gl[1]).astype(BF16))
        r_far = self.x((right[n : 2 * n].astype(F32) + gr[1]).astype(BF16))
        return l_far, r_far

    def scatter_end(self, left, right, gl, gr, l_far, r_far):
        n = left.shape[0] // 4
        l_own = left[:n].astype(F32) + gl[0] + l_far
        r_own = right[:n].astype(F32) + gr[0] + r_far
        return jnp.concatenate([l_own, r_own], axis=1)

    def gather_planes(self, a):
        got = lax.all_gather(a, ("c", "z"), axis=0, tiled=True)
        return got.reshape(2, self.planes * a.shape[0], a.shape[1])

    def gather_gains(self, a):
        n = a.shape[1]
        y_me = lax.axis_index("y")
        z_me = lax.axis_index("z")
        two = pair(y_me, a, self.y(a))
        out = jnp.zeros((self.planes,) + two.shape, a.dtype)
        for k in range(self.planes):
            part = two if k == 0 else lax.ppermute(two, AXES, self.pz[k])
            at = lax.rem(z_me - k + self.planes, self.planes)
            out = lax.dynamic_update_slice(out, part[None], (at, 0, 0, 0))
        return jnp.transpose(out, (2, 0, 1, 3)).reshape(2, 2 * self.planes * n)


def pair(bit, own, other):
    return jnp.stack([jnp.where(bit == 0, own, other), jnp.where(bit == 0, other, own)])


def estimate(flops, bytes_accessed, transcendentals):
    return pl.CostEstimate(
        flops=flops // 16,
        bytes_accessed=bytes_accessed // 16,
        transcendentals=transcendentals // 16,
    )


def rank_scalar(rank):
    return jnp.reshape(rank, (1,)).astype(jnp.int32)


def place_columns(rank, parts, planes, piece, side):
    n = parts[0].shape[0]
    width = planes * piece
    total = 8 * width
    if piece % 128:
        parts = [t[:, side * width : (side + 1) * width] for t in parts]
        out = jnp.zeros((n, planes, 8, piece), F32)
        for p, part in enumerate(parts):
            part = part.reshape(n, planes, 1, piece).astype(F32)
            out = lax.dynamic_update_slice(out, part, (0, 0, jnp.bitwise_xor(rank, p), 0))
        return out.reshape(n, total)
    tile = min(n, 64)

    def kernel(rank_ref, *refs):
        out = refs[8]
        for p in range(8):
            t = jnp.bitwise_xor(rank_ref[0], p)
            for z in range(planes):
                at = pl.multiple_of(z * 8 * piece + t * piece, 128)
                out[:, pl.ds(at, piece)] = refs[p][:, z * piece : (z + 1) * piece].astype(F32)

    return pl.pallas_call(
        kernel,
        out_shape=jax.ShapeDtypeStruct((n, total), F32),
        grid_spec=pltpu.PrefetchScalarGridSpec(
            num_scalar_prefetch=1,
            grid=(n // tile,),
            in_specs=[pl.BlockSpec((tile, width), lambda i, r: (i, side))] * 8,
            out_specs=pl.BlockSpec((tile, total), lambda i, r: (i, 0)),
        ),
        cost_estimate=estimate(flops=0, bytes_accessed=6 * n * total, transcendentals=0),
    )(rank_scalar(rank), *parts)


def place_rows(order, parts):
    n, d = parts[0].shape
    tile = min(d, 256)

    def kernel(order_ref, *refs):
        out = refs[4]
        for p in range(4):
            t = jnp.bitwise_xor(order_ref[0], p)
            out[pl.ds(pl.multiple_of(t * n, 8), n), :] = refs[p][...].astype(F32)

    return pl.pallas_call(
        kernel,
        out_shape=jax.ShapeDtypeStruct((4 * n, d), F32),
        grid_spec=pltpu.PrefetchScalarGridSpec(
            num_scalar_prefetch=1,
            grid=(d // tile,),
            in_specs=[pl.BlockSpec((n, tile), lambda i, r: (0, i))] * 4,
            out_specs=pl.BlockSpec((4 * n, tile), lambda i, r: (0, i)),
        ),
        cost_estimate=estimate(flops=0, bytes_accessed=24 * n * d, transcendentals=0),
    )(rank_scalar(order), *parts)


def place_attention(rank, parts):
    n, width = parts[0].shape
    h = HEAD_SIZE
    o = width - 2 * h
    tile = min(n, 64)

    def kernel(rank_ref, *refs):
        q_out, k_out, v_out, o_out = refs[8:]
        for p in range(8):
            t = jnp.bitwise_xor(rank_ref[0], p)
            j = t // 2
            core = t - 2 * j
            q_out[:, pl.ds(pl.multiple_of(t * h, 128), h)] = refs[p][:, :h].astype(F32)
            at = pl.ds(pl.multiple_of(j * h, 128), h)

            @pl.when(core == 0)
            def _():
                k_out[:, at] = refs[p][:, h : 2 * h].astype(F32)

            @pl.when(core == 1)
            def _():
                v_out[:, at] = refs[p][:, h : 2 * h].astype(F32)

            to = pl.multiple_of(core * 4 * o + j * o, 128)
            o_out[:, pl.ds(to, o)] = refs[p][:, 2 * h :].astype(F32)

    widths = (8 * h, 4 * h, 4 * h, 8 * o)
    return pl.pallas_call(
        kernel,
        out_shape=tuple(jax.ShapeDtypeStruct((n, w), F32) for w in widths),
        grid_spec=pltpu.PrefetchScalarGridSpec(
            num_scalar_prefetch=1,
            grid=(n // tile,),
            in_specs=[pl.BlockSpec((tile, width), lambda i, r: (i, 0))] * 8,
            out_specs=tuple(pl.BlockSpec((tile, w), lambda i, r: (i, 0)) for w in widths),
        ),
        cost_estimate=estimate(flops=0, bytes_accessed=48 * n * width, transcendentals=0),
    )(rank_scalar(rank), *parts)


def back_product(core, lefts, weight):
    m, k = lefts[0].shape
    n = weight.shape[1]
    tile = min(n // 2, 256)
    steps = n // 2 // tile

    def kernel(core_ref, a0, a1, l0, l1, r0, r1, left, right):
        left[...] = (mm_nt(a0[...], l0[...]) + mm_nt(a1[...], l1[...])).astype(BF16)
        right[...] = (mm_nt(a0[...], r0[...]) + mm_nt(a1[...], r1[...])).astype(BF16)

    whole = pl.BlockSpec((m, k), lambda i, r: (0, 0))
    out = pl.BlockSpec((m, tile), lambda i, r: (0, i))
    return pl.pallas_call(
        kernel,
        out_shape=(jax.ShapeDtypeStruct((m, n // 2), BF16),) * 2,
        grid_spec=pltpu.PrefetchScalarGridSpec(
            num_scalar_prefetch=1,
            grid=(steps,),
            in_specs=[
                whole,
                whole,
                pl.BlockSpec((None, tile, k), lambda i, r: (r[0], i, 0)),
                pl.BlockSpec((None, tile, k), lambda i, r: (1 - r[0], i, 0)),
                pl.BlockSpec((None, tile, k), lambda i, r: (r[0], i + steps, 0)),
                pl.BlockSpec((None, tile, k), lambda i, r: (1 - r[0], i + steps, 0)),
            ],
            out_specs=(out, out),
        ),
        compiler_params=pltpu.CompilerParams(vmem_limit_bytes=48 << 20),
        cost_estimate=estimate(
            flops=4 * m * k * n, bytes_accessed=4 * (m + n) * k + 2 * m * n, transcendentals=0
        ),
    )(rank_scalar(core), *lefts, weight, weight, weight, weight)


def ff_front(half, n2, weight):
    m, d = n2.shape
    f = weight.shape[2] // 2
    tile = 256
    steps = f // tile

    def kernel(half_ref, x, wg, wu, gate_out, up_out, act_out):
        gate = mm(x[...], wg[...])
        up = mm(x[...], wu[...])
        gate_out[...] = gate
        up_out[...] = up
        act_out[...] = (gate * jax.nn.sigmoid(gate) * up).astype(BF16)

    out = pl.BlockSpec((m, tile), lambda i, r: (0, i))
    return pl.pallas_call(
        kernel,
        out_shape=(
            jax.ShapeDtypeStruct((m, f), F32),
            jax.ShapeDtypeStruct((m, f), F32),
            jax.ShapeDtypeStruct((m, f), BF16),
        ),
        grid_spec=pltpu.PrefetchScalarGridSpec(
            num_scalar_prefetch=1,
            grid=(steps,),
            in_specs=[
                pl.BlockSpec((m, d), lambda i, r: (0, 0)),
                pl.BlockSpec((None, d, tile), lambda i, r: (r[0], 0, i)),
                pl.BlockSpec((None, d, tile), lambda i, r: (r[0], 0, i + steps)),
            ],
            out_specs=(out, out, out),
        ),
        compiler_params=pltpu.CompilerParams(vmem_limit_bytes=48 << 20),
        cost_estimate=estimate(
            flops=4 * m * d * f, bytes_accessed=2 * m * d + 4 * d * f + 10 * m * f, transcendentals=m * f
        ),
    )(rank_scalar(half), n2, weight, weight)


def ff_back(half, d_in, weight, gate_pre, up_pre):
    m, d = d_in.shape
    f = weight.shape[1]
    tile = 256
    steps = f // tile

    def kernel(half_ref, g, w, gate_ref, up_ref, out, kept):
        i = pl.program_id(0)

        @pl.when(i < steps)
        def _():
            act_grad = mm_nt(g[...], w[...])
            gate = gate_ref[...]
            sig = jax.nn.sigmoid(gate)
            out[...] = (act_grad * up_ref[...] * sig * (1.0 + gate * (1.0 - sig))).astype(BF16)
            kept[i] = (act_grad * (gate * sig)).astype(BF16)

        @pl.when(i >= steps)
        def _():
            out[...] = kept[i - steps]

    last = steps - 1
    pre = pl.BlockSpec((m, tile), lambda i, r: (0, jnp.minimum(i, last)))
    return pl.pallas_call(
        kernel,
        out_shape=jax.ShapeDtypeStruct((m, 2 * f), BF16),
        grid_spec=pltpu.PrefetchScalarGridSpec(
            num_scalar_prefetch=1,
            grid=(2 * steps,),
            in_specs=[
                pl.BlockSpec((m, d), lambda i, r: (0, 0)),
                pl.BlockSpec((None, tile, d), lambda i, r: (r[0], jnp.minimum(i, last), 0)),
                pre,
                pre,
            ],
            out_specs=pl.BlockSpec((m, tile), lambda i, r: (0, i)),
            scratch_shapes=[pltpu.VMEM((steps, m, tile), BF16)],
        ),
        compiler_params=pltpu.CompilerParams(vmem_limit_bytes=48 << 20),
        cost_estimate=estimate(
            flops=2 * m * d * f, bytes_accessed=2 * (m + f) * d + 12 * m * f, transcendentals=m * f
        ),
    )(rank_scalar(half), d_in, weight, gate_pre, up_pre)


def forward_product(core, lefts, weight):
    m, k = lefts[0].shape
    n = weight.shape[2]
    tile = 256
    steps = n // 2 // tile

    def kernel(core_ref, a0, a1, l0, l1, r0, r1, left, right):
        left[...] = (mm(a0[...], l0[...]) + mm(a1[...], l1[...])).astype(BF16)
        right[...] = (mm(a0[...], r0[...]) + mm(a1[...], r1[...])).astype(BF16)

    whole = pl.BlockSpec((m, k), lambda i, r: (0, 0))
    out = pl.BlockSpec((m, tile), lambda i, r: (0, i))
    return pl.pallas_call(
        kernel,
        out_shape=(jax.ShapeDtypeStruct((m, n // 2), BF16),) * 2,
        grid_spec=pltpu.PrefetchScalarGridSpec(
            num_scalar_prefetch=1,
            grid=(steps,),
            in_specs=[
                whole,
                whole,
                pl.BlockSpec((None, k, tile), lambda i, r: (r[0], 0, i)),
                pl.BlockSpec((None, k, tile), lambda i, r: (1 - r[0], 0, i)),
                pl.BlockSpec((None, k, tile), lambda i, r: (r[0], 0, i + steps)),
                pl.BlockSpec((None, k, tile), lambda i, r: (1 - r[0], 0, i + steps)),
            ],
            out_specs=(out, out),
        ),
        compiler_params=pltpu.CompilerParams(vmem_limit_bytes=40 << 20),
        cost_estimate=estimate(
            flops=4 * m * k * n, bytes_accessed=4 * (m + n) * k + 2 * m * n, transcendentals=0
        ),
    )(rank_scalar(core), *lefts, weight, weight, weight, weight)


def send_blocks(slot, has, streams):
    groups = slot.shape[0]
    _, r, f = streams[0].shape
    count = len(streams)

    def kernel(slot_ref, has_ref, *refs):
        keep = has_ref[pl.program_id(0)] > 0
        for i in range(count):
            v = refs[i][0]
            refs[count][0, i] = jnp.where(keep, v, jnp.zeros_like(v))

    return pl.pallas_call(
        kernel,
        out_shape=jax.ShapeDtypeStruct((groups, count, r, f), BF16),
        grid_spec=pltpu.PrefetchScalarGridSpec(
            num_scalar_prefetch=2,
            grid=(groups,),
            in_specs=[pl.BlockSpec((1, r, f), lambda g, s, h: (s[g], 0, 0))] * count,
            out_specs=pl.BlockSpec((1, count, r, f), lambda g, s, h: (g, 0, 0, 0)),
        ),
        cost_estimate=estimate(
            flops=0, bytes_accessed=4 * count * groups * r * f, transcendentals=0
        ),
    )(slot, has, *streams)


def assemble_rows(info, pieces, gain=None):
    _, _, r, f = pieces[0].shape
    width = 4 * f

    def block(i, n):
        return 2 * jnp.bitwise_xor(n[0], (i // 2) % 2) + i % 2

    def kernel(info_ref, *refs):
        own, ax, ay, dx, dy = refs[:5]
        i = pl.program_id(0)
        x = info_ref[0]
        near = i < 4
        low = block(i, info_ref) < 2
        same = jnp.where(near, own[0], ay[0])
        other = jnp.where(near, ax[0], jnp.where(low, dx[0], dy[0]))
        at = info_ref[2 + i] * r + lax.broadcasted_iota(jnp.int32, (r, f), 0)
        inside = at < info_ref[1]
        parts = []
        for h, v in ((x, same), (1 - x, other)):
            for c in range(2):
                t = jnp.where(inside, v[c].astype(F32), 0.0)
                parts.append((2 * h + c, t))
        if gain is None:
            for q, t in parts:
                refs[5][:, pl.ds(pl.multiple_of(q * f, 128), f)] = t.astype(BF16)
            return
        gain_ref, normed, rows = refs[5:]
        total = sum(jnp.sum(t * t, axis=1, keepdims=True) for _, t in parts)
        factor = lax.rsqrt(total * (1.0 / width) + EPS_NORM)
        for q, t in parts:
            g = gain_ref[pl.ds(q, 1), :]
            normed[:, pl.ds(pl.multiple_of(q * f, 128), f)] = (t * factor * g).astype(BF16)

        @pl.when(i < 2)
        def _():
            for q, t in parts:
                rows[:, pl.ds(pl.multiple_of(q * f, 128), f)] = t.astype(BF16)

    whole = pl.BlockSpec((1, 2, r, f), lambda i, n: (block(i, n), 0, 0, 0))
    specs = [
        whole,
        whole,
        whole,
        pl.BlockSpec((1, 2, r, f), lambda i, n: (jnp.minimum(block(i, n), 1), 0, 0, 0)),
        pl.BlockSpec((1, 2, r, f), lambda i, n: (jnp.maximum(block(i, n) - 2, 0), 0, 0, 0)),
    ]
    shape = [jax.ShapeDtypeStruct((8 * r, width), BF16)]
    outs = [pl.BlockSpec((r, width), lambda i, n: (i, 0))]
    args = list(pieces)
    if gain is not None:
        specs.append(pl.BlockSpec((4, f), lambda i, n: (0, 0)))
        args.append(gain)
        shape.append(jax.ShapeDtypeStruct((2 * r, width), BF16))
        outs.append(pl.BlockSpec((r, width), lambda i, n: (jnp.minimum(i, 1), 0)))
    got = pl.pallas_call(
        kernel,
        out_shape=tuple(shape),
        grid_spec=pltpu.PrefetchScalarGridSpec(
            num_scalar_prefetch=1, grid=(8,), in_specs=specs, out_specs=tuple(outs)
        ),
        cost_estimate=estimate(
            flops=16 * r * width, bytes_accessed=40 * r * width, transcendentals=0
        ),
    )(info, *args)
    return got[0] if gain is None else got


def turn(v, cos_t, sin_t, sign):
    h = v.shape[-1] // 2
    a, b = v[:, :h], v[:, h:]
    s = sin_t * sign
    return jnp.concatenate([a * cos_t - b * s, b * cos_t + a * s], axis=-1).astype(BF16)


def project(normed, w_attn, cos_t, sin_t):
    rows, width = normed.shape
    h = HEAD_SIZE
    tile = 256

    def kernel(x_ref, w_ref, c_ref, s_ref, q0, q1, k, v):
        even = mm(x_ref[...], w_ref[0])
        odd = mm(x_ref[...], w_ref[1])
        cos_t, sin_t = c_ref[...], s_ref[...]
        q0[...] = turn(even[:, :h], cos_t, sin_t, 1.0)
        k[...] = turn(even[:, h:], cos_t, sin_t, 1.0)
        q1[...] = turn(odd[:, :h], cos_t, sin_t, 1.0)
        v[...] = odd[:, h:].astype(BF16)

    out = pl.BlockSpec((tile, h), lambda i: (i, 0))
    table = pl.BlockSpec((tile, h // 2), lambda i: (i, 0))
    return pl.pallas_call(
        kernel,
        out_shape=(jax.ShapeDtypeStruct((rows, h), BF16),) * 4,
        grid=(rows // tile,),
        in_specs=[
            pl.BlockSpec((tile, width), lambda i: (i, 0)),
            pl.BlockSpec((2, width, 2 * h), lambda i: (0, 0, 0)),
            table,
            table,
        ],
        out_specs=(out,) * 4,
        compiler_params=pltpu.CompilerParams(vmem_limit_bytes=40 << 20),
        cost_estimate=estimate(
            flops=8 * rows * width * h, bytes_accessed=2 * rows * width + 8 * width * h, transcendentals=0
        ),
    )(normed, w_attn, cos_t, sin_t)


def attend(q0, q1, keys, values, w_o, at_q, at_k):
    rows, h = q0.shape
    half = w_o.shape[2]
    tile = 256
    factor = 1.0 / math.sqrt(HEAD_SIZE)

    def kernel(q0_ref, q1_ref, k_ref, v_ref, w_ref, aq_ref, ak_ref, mixed, lse, left, right):
        allowed = ak_ref[...] <= aq_ref[...]
        for i, q_ref in enumerate((q0_ref, q1_ref)):
            scores = jnp.where(allowed, mm_nt(q_ref[...], k_ref[...]) * factor, MASK_FILL)
            top = jnp.max(scores, axis=-1, keepdims=True)
            e = jnp.exp(scores - top)
            total = jnp.sum(e, axis=-1, keepdims=True)
            probs = (e * (1.0 / total)).astype(BF16)
            mixed[:, i * h : (i + 1) * h] = mm(probs, v_ref[...]).astype(BF16)
            lse[i] = top + jnp.log(total)
        left[...] = mm(mixed[...], w_ref[0]).astype(BF16)
        right[...] = mm(mixed[...], w_ref[1]).astype(BF16)

    q_spec = pl.BlockSpec((tile, h), lambda i: (i, 0))
    kv_spec = pl.BlockSpec((rows, h), lambda i: (0, 0))
    out_spec = pl.BlockSpec((tile, half), lambda i: (i, 0))
    return pl.pallas_call(
        kernel,
        out_shape=(
            jax.ShapeDtypeStruct((rows, 2 * h), BF16),
            jax.ShapeDtypeStruct((2, rows, 1), F32),
            jax.ShapeDtypeStruct((rows, half), BF16),
            jax.ShapeDtypeStruct((rows, half), BF16),
        ),
        grid=(rows // tile,),
        in_specs=[
            q_spec,
            q_spec,
            kv_spec,
            kv_spec,
            pl.BlockSpec((2, 2 * h, half), lambda i: (0, 0, 0)),
            pl.BlockSpec((tile, 1), lambda i: (i, 0)),
            pl.BlockSpec((1, rows), lambda i: (0, 0)),
        ],
        out_specs=(
            pl.BlockSpec((tile, 2 * h), lambda i: (i, 0)),
            pl.BlockSpec((2, tile, 1), lambda i: (0, i, 0)),
            out_spec,
            out_spec,
        ),
        compiler_params=pltpu.CompilerParams(vmem_limit_bytes=40 << 20),
        cost_estimate=estimate(
            flops=8 * rows * rows * h + 8 * rows * h * half,
            bytes_accessed=12 * rows * h + 8 * h * half + 4 * rows * half,
            transcendentals=2 * rows * rows,
        ),
    )(q0, q1, keys, values, w_o, at_q, at_k)


def attend_back(attn_in, w_o, q0, q1, keys, values, lse, at_q, at_k, cos_t, sin_t):
    rows, h = q0.shape
    half = w_o.shape[2]
    tile = 256
    steps = rows // tile
    factor = 1.0 / math.sqrt(HEAD_SIZE)

    def kernel(
        g_ref, w_ref, q0_ref, q1_ref, k_ref, v_ref, lse_ref, aq_ref, ak_ref, c_ref, s_ref, ca_ref,
        sa_ref, dq0, dq1, dk, dv, k_sum, v_sum,
    ):
        step = pl.program_id(0)

        @pl.when(step == 0)
        def _():
            k_sum[...] = jnp.zeros_like(k_sum)
            v_sum[...] = jnp.zeros_like(v_sum)

        g = g_ref[...]
        dmix = (mm_nt(g[:, :half], w_ref[0]) + mm_nt(g[:, half:], w_ref[1])).astype(BF16)
        allowed = ak_ref[...] <= aq_ref[...]
        for i, (q_ref, dq) in enumerate(((q0_ref, dq0), (q1_ref, dq1))):
            d = dmix[:, i * h : (i + 1) * h]
            scores = jnp.where(allowed, mm_nt(q_ref[...], k_ref[...]) * factor, MASK_FILL)
            probs = jnp.exp(scores - lse_ref[i])
            v_sum[...] += mm_tn(probs.astype(BF16), d)
            prob_grad = mm_nt(d, v_ref[...])
            inner = jnp.sum(prob_grad * probs, axis=-1, keepdims=True)
            score_grad = (probs * (prob_grad - inner)).astype(BF16)
            k_sum[...] += mm_tn(score_grad, q_ref[...])
            rot = (mm(score_grad, k_ref[...]) * factor).astype(BF16).astype(F32)
            dq[...] = turn(rot, c_ref[...], s_ref[...], -1.0)

        @pl.when(step == steps - 1)
        def _():
            rot = (k_sum[...] * factor).astype(BF16).astype(F32)
            dk[...] = turn(rot, ca_ref[...], sa_ref[...], -1.0)
            dv[...] = v_sum[...].astype(BF16)

    q_spec = pl.BlockSpec((tile, h), lambda i: (i, 0))
    kv_spec = pl.BlockSpec((rows, h), lambda i: (0, 0))
    table = pl.BlockSpec((tile, h // 2), lambda i: (i, 0))
    all_table = pl.BlockSpec((rows, h // 2), lambda i: (0, 0))
    return pl.pallas_call(
        kernel,
        out_shape=(jax.ShapeDtypeStruct((rows, h), BF16),) * 4,
        grid=(steps,),
        in_specs=[
            pl.BlockSpec((tile, 2 * half), lambda i: (i, 0)),
            pl.BlockSpec((2, 2 * h, half), lambda i: (0, 0, 0)),
            q_spec,
            q_spec,
            kv_spec,
            kv_spec,
            pl.BlockSpec((2, tile, 1), lambda i: (0, i, 0)),
            pl.BlockSpec((tile, 1), lambda i: (i, 0)),
            pl.BlockSpec((1, rows), lambda i: (0, 0)),
            table,
            table,
            all_table,
            all_table,
        ],
        out_specs=(q_spec, q_spec, kv_spec, kv_spec),
        scratch_shapes=[pltpu.VMEM((rows, h), F32), pltpu.VMEM((rows, h), F32)],
        compiler_params=pltpu.CompilerParams(vmem_limit_bytes=48 << 20),
        cost_estimate=estimate(
            flops=20 * rows * rows * h + 8 * rows * h * half,
            bytes_accessed=20 * rows * h + 8 * h * half + 4 * rows * half,
            transcendentals=2 * rows * rows,
        ),
    )(attn_in, w_o, q0, q1, keys, values, lse, at_q, at_k, cos_t, sin_t, cos_t, sin_t)


def rope_tables(positions):
    half_dim = HEAD_SIZE // 2
    frequency = jnp.exp(jnp.arange(half_dim, dtype=F32) * (-2.0 * math.log(ROPE_BASE) / HEAD_SIZE))
    angles = positions.astype(F32)[:, None] * frequency[None, :]
    return jnp.cos(angles), jnp.sin(angles)


def norm_factor(hidden):
    return lax.rsqrt(jnp.mean(hidden * hidden, axis=-1, keepdims=True) + EPS_NORM)


def norm_backward(upstream, hidden, factor, gain_vec):
    scaled = upstream * gain_vec
    gain_part = jnp.sum(upstream * hidden * factor, axis=0)
    inner_sum = jnp.mean(scaled * hidden, axis=-1, keepdims=True)
    return (factor * scaled - hidden * (factor * factor * factor) * inner_sum, gain_part)


def make_body(planes):
    links = Links(planes)

    def body(
        tokens,
        cotangent,
        query_weight,
        key_matrix,
        value_matrix,
        output_weight,
        gate_weight,
        up_weight,
        down_weight,
        prenorm_gain,
        midnorm_gain,
        seq_len,
        stream_order,
    ):
        groups = 2 * planes
        z_me = lax.axis_index("z")
        y_me = lax.axis_index("y")
        x_me = lax.axis_index("x")
        c_me = lax.axis_index("c")
        slots, blk, quarter = tokens.shape
        width = 4 * quarter
        rank = 4 * y_me + 2 * x_me + c_me
        head = 2 * y_me + x_me
        shard = query_weight.shape[0]
        ff = gate_weight.shape[1]
        piece = ff // groups // 4

        nblk = (seq_len + blk - 1) // blk
        member = (stream_order[:, None] == jnp.arange(groups, dtype=jnp.int32)[None, :]).astype(
            jnp.int32
        )
        ordered = jnp.sum(member * nblk[None, :], axis=1)
        firsts = jnp.cumsum(ordered) - ordered
        seq_start = jnp.sum(member * firsts[:, None], axis=0)
        group_me = 2 * z_me + y_me
        offset = lax.rem(group_me - lax.rem(seq_start, groups) + groups, groups)
        has = offset < nblk
        slot_of = jnp.where(has, (seq_start + offset) // groups, 0)
        block_ids = jnp.arange(slots, dtype=jnp.int32) * groups + group_me
        ahead = block_ids[:, None] - seq_start[None, :]
        covers = ((ahead >= 0) & (ahead < nblk[None, :])).astype(jnp.int32)
        seq_of = jnp.sum(covers * jnp.arange(groups, dtype=jnp.int32)[None, :], axis=1)
        taken = jnp.sum(covers, axis=1)

        mine = 2 * z_me + c_me
        picked = jnp.arange(groups, dtype=jnp.int32) == mine
        my_start = jnp.sum(jnp.where(picked, seq_start, 0))
        my_len = jnp.sum(jnp.where(picked, seq_len, 0))

        def block_places(y):
            first = lax.rem(y + my_start, 2)
            plane = lax.rem((my_start + first) // 2, planes)
            k = jnp.arange(4, dtype=jnp.int32)
            if planes == 4:
                k = lax.rem(k - plane + planes, planes)
            return first + 2 * k, plane

        places_own, plane_own = block_places(y_me)
        places_far, _ = block_places(1 - y_me)

        def two_places(places, x):
            return lax.dynamic_slice(places, (2 * x,), (2,))

        places = jnp.concatenate(
            [
                two_places(places_own, x_me),
                two_places(places_own, 1 - x_me),
                two_places(places_far, x_me),
                two_places(places_far, 1 - x_me),
            ]
        )
        info = jnp.concatenate([jnp.stack([x_me, my_len]), places]).astype(jnp.int32)
        positions = (places[:, None] * blk + jnp.arange(blk, dtype=jnp.int32)[None, :]).reshape(-1)
        at_q = positions[:, None]
        at_k = jnp.where(positions < my_len, positions, 1 << 30)[None, :]
        rows = 2 * blk
        valid = (positions[:rows] < my_len).astype(F32)[:, None]

        def send_layout(out_rows):
            left, right = out_rows[:, : 2 * quarter], out_rows[:, 2 * quarter :]
            keep = jnp.where(x_me == 0, left, right)
            got = links.x(jnp.where(x_me == 0, right, left))
            send = pair(x_me, keep, got).reshape(4, blk, 2, quarter)
            send = jnp.transpose(send, (0, 2, 1, 3))
            if planes > 4:
                send = jnp.pad(send, ((0, planes - 4), (0, 0), (0, 0), (0, 0)))
                send = jnp.roll(send, plane_own, axis=0)
            return send.reshape(groups, blk, quarter)

        def to_stream(got):
            return send_blocks(seq_of, taken, [got])[:, 0]

        def by_rank(g):
            n = g.shape[1]
            own = lax.dynamic_slice(g, (y_me * shard, 0), (shard, n))
            other = lax.dynamic_slice(g, ((1 - y_me) * shard, 0), (shard, n))
            parts = links.swap_chips([own, own, other, other])
            return [links.c(parts[p // 2]) if p % 2 else parts[p // 2] for p in range(8)]

        def plane_rows(own_part, far_part):
            got = links.y(far_part)
            both = pair(y_me, own_part, got)
            return both.reshape(2 * own_part.shape[0], own_part.shape[1])

        def ff_columns(w, r):
            return jnp.concatenate(
                [
                    lax.dynamic_slice(w, (0, p * 8 * piece + r * piece), (shard, piece))
                    for p in range(planes)
                ],
                axis=1,
            )

        far = rank + 4 - 8 * y_me
        def attn_columns(r, ws):
            q = lax.dynamic_slice(ws[0], (0, r * HEAD_SIZE), (shard, HEAD_SIZE))
            j = r // 2
            k = lax.dynamic_slice(ws[1], (0, j * HEAD_SIZE), (shard, HEAD_SIZE))
            v = lax.dynamic_slice(ws[2], (0, j * HEAD_SIZE), (shard, HEAD_SIZE))
            at = lax.rem(r, 2) * (width // 2) + (r // 2) * (width // 8)
            o = lax.dynamic_slice(ws[3], (0, at), (shard, width // 8))
            return jnp.concatenate([q, jnp.where(c_me == 0, k, v), o], axis=1)

        gains = links.gather_gains(jnp.stack([prenorm_gain, midnorm_gain])).astype(F32)

        def to_sequences(stream):
            send = send_blocks(slot_of, has.astype(jnp.int32), [stream])
            return send[:, 0]

        def arranged(got):
            got = got.reshape(planes, 2, blk, quarter)
            if planes > 4:
                got = jnp.roll(got, -plane_own, axis=0)[:4]
            return got

        def exchange(send):
            return lax.all_to_all(send, ("z", "c"), split_axis=0, concat_axis=0, tiled=True)

        send_tokens = to_sequences(tokens)
        got_tokens = exchange(send_tokens)
        *attn_ws, gate_weight, up_weight, down_weight, _ = sync(
            query_weight,
            key_matrix,
            value_matrix,
            output_weight,
            gate_weight,
            up_weight,
            down_weight,
            send_tokens,
        )
        attn_share = plane_rows(attn_columns(rank, attn_ws), attn_columns(far, attn_ws))

        def ff_share(r):
            return jnp.concatenate([ff_columns(gate_weight, r), ff_columns(up_weight, r)], axis=1)

        ff_own, ff_far_rows = ff_share(rank), ff_share(far)
        down_share = lax.dynamic_slice(
            down_weight, ((2 * x_me + c_me) * piece, 0), (piece, width)
        )
        got_tokens, attn_share, ff_own, ff_far_rows, down_share, gains = sync(
            got_tokens, attn_share, ff_own, ff_far_rows, down_share, gains
        )
        w_attn = links.gather_planes(attn_share)
        own = arranged(got_tokens)
        ax, ay = sync(*links.gather_one(own))
        ff_two = plane_rows(ff_own, after(ff_far_rows, own))
        gain_pre, gain_mid = gains[0], gains[1]
        eighth = width // 8

        def spread(chunk_of):
            return links.swap_chips([chunk_of(jnp.bitwise_xor(head, p)) for p in range(4)])

        cos_t, sin_t = rope_tables(positions)
        dx, dy, cos_t, sin_t, ff_two = sync(*links.gather_two(ax, ay), cos_t, sin_t, ff_two)
        w_ff = links.gather_planes(ff_two)
        w_down = links.gather_planes(after(down_share, ff_two))
        normed, rows_in = assemble_rows(info, (own, ax, ay, dx, dy), gain_pre.reshape(4, quarter))
        send_cot = to_sequences(after(cotangent, dx))
        w_attn, normed, send_cot = sync(w_attn, normed, send_cot)
        got_cot = exchange(send_cot)
        w_o_cols = lax.dynamic_index_in_dim(w_attn, c_me, 0, keepdims=False)[:, 2 * HEAD_SIZE :]
        w_o = jnp.zeros((2 * HEAD_SIZE, 4 * eighth), BF16)
        for p, part in enumerate(
            spread(
                lambda t: lax.dynamic_slice(
                    w_o_cols, (t * 2 * HEAD_SIZE, 0), (2 * HEAD_SIZE, eighth)
                )
            )
        ):
            w_o = lax.dynamic_update_slice(w_o, part, (0, jnp.bitwise_xor(head, p) * eighth))
        w_o = pair(c_me, w_o, links.c(w_o))

        q0, q1, keys, values = project(normed, w_attn, cos_t, sin_t)
        mixed, lse, attn_left, attn_right = attend(q0, q1, keys, values, w_o, at_q, at_k)
        hidden_zero = rows_in.astype(F32)
        factor_pre = norm_factor(hidden_zero)
        gl, gr = sync(*links.scatter_one(attn_left, attn_right))
        l_far, r_far = sync(*links.scatter_two(attn_left, attn_right, gl, gr))
        hidden_one = hidden_zero + links.scatter_end(attn_left, attn_right, gl, gr, l_far, r_far)
        factor_mid = norm_factor(hidden_one)
        n_own = (hidden_one * factor_mid * gain_mid).astype(BF16)
        ax, ay, got_cot = sync(*links.gather_one(n_own), got_cot)
        dx, dy = sync(*links.gather_two(ax, ay))
        normed_two = jnp.concatenate([n_own, ax, ay, dx, dy], axis=0)
        own = after(arranged(got_cot), normed_two)
        n_ff = w_ff.shape[2] // 2
        far_gate, far_up, act_far = ff_front(1 - c_me, normed_two, w_ff)
        ax, ay, act_far = sync(*links.gather_one(own), act_far)
        own_gate, own_up, act_own = ff_front(c_me, after(normed_two, ax), w_ff)
        turned = sync(jnp.transpose(after(normed_two, act_own)))[0]
        dx, dy, act_own, turned = sync(*links.gather_two(ax, ay), act_own, turned)
        down_in = assemble_rows(info, (own, ax, ay, dx, dy))

        def far_part(left, right):
            return mm_tn(left, right).astype(BF16)

        def both_cores(left, right, got):
            return (mm_tn(left, right) + got).astype(BF16)

        def over_planes(g):
            return lax.psum_scatter(g, "z", scatter_dimension=0, tiled=True)

        half = width // 2
        down_far = far_part(act_far, down_in)
        sum_down = both_cores(act_own, down_in, links.c(down_far))
        w_down, d_in = sync(w_down, down_in, sum_down)[:2]
        in_far = ff_back(1 - c_me, d_in, w_down, far_gate, far_up)
        ff_far = mm(turned, in_far).astype(BF16)
        in_own = ff_back(c_me, after(d_in, ff_far), w_down, own_gate, own_up)
        ff_left, ff_right = forward_product(c_me, (after(act_own, in_own), act_far), w_down)
        in_own, ff_left, ff_right, ff_got = sync(in_own, ff_left, ff_right, links.c(ff_far))
        ff_l, ff_r = links.scatter_one(ff_left, ff_right)
        sum_ff = (mm(turned, in_own) + ff_got).astype(BF16)
        g_ff = over_planes(sum_ff)
        ff_l, ff_r, in_own, sum_ff = sync(ff_l, ff_r, in_own, sum_ff)
        ff_lf, ff_rf = links.scatter_two(ff_left, ff_right, ff_l, ff_r)
        g_down = over_planes(after(sum_down, sum_ff))
        dn_left, dn_right = back_product(c_me, (in_own, in_far), w_ff)
        dn_left, dn_right, ff_lf, ff_rf = sync(dn_left, dn_right, ff_lf, ff_rf)
        out_rows = (
            (hidden_one + links.scatter_end(ff_left, ff_right, ff_l, ff_r, ff_lf, ff_rf)) * valid
        ).astype(BF16)
        dn_l, dn_r, out_rows = sync(*links.scatter_one(dn_left, dn_right), out_rows)
        dn_lf, dn_rf = sync(*links.scatter_two(dn_left, dn_right, dn_l, dn_r))
        normed_two_grad = links.scatter_end(dn_left, dn_right, dn_l, dn_r, dn_lf, dn_rf)

        mid_upstream, midnorm_part = norm_backward(normed_two_grad, hidden_one, factor_mid, gain_mid)
        hidden_one_grad = down_in[:rows].astype(F32) + mid_upstream
        a_own = hidden_one_grad.astype(BF16)
        ax, ay = sync(*links.gather_one(a_own))
        dx, dy = sync(*links.gather_two(ax, ay))
        attn_in = jnp.concatenate([a_own, ax, ay, dx, dy], axis=0)
        attn_in, out_rows = sync(attn_in, out_rows)
        out_send = send_layout(out_rows)
        ff_parts = by_rank(after(g_ff, attn_in))
        first = c_me == 0
        attn_own = jnp.where(first, attn_in[:, :half], attn_in[:, half:])
        attn_far = jnp.where(first, attn_in[:, half:], attn_in[:, :half])
        out_far = far_part(mixed, attn_far)
        dq0, dq1, dk, dv = attend_back(
            after(attn_in, out_far), w_o, q0, q1, keys, values, lse, at_q, at_k, cos_t, sin_t
        )
        g_out = both_cores(mixed, after(attn_own, dq0), links.c(out_far))
        grad_even = jnp.concatenate([dq0, dk], axis=1)
        grad_odd = jnp.concatenate([dq1, dv], axis=1)
        normed_part = (
            mm_nt(after(grad_even, g_out), w_attn[0, :, : 2 * HEAD_SIZE])
            + mm_nt(grad_odd, w_attn[1, :, : 2 * HEAD_SIZE])
        ).astype(BF16)
        o_parts = spread(lambda t: lax.dynamic_slice(g_out, (0, t * eighth), (2 * HEAD_SIZE, eighth)))
        normed_part, out_send, grad_even, grad_odd, *o_parts = sync(
            normed_part, out_send, grad_even, grad_odd, *o_parts
        )
        np_left, np_right = normed_part[:, :half], normed_part[:, half:]
        np_l, np_r = links.scatter_one(np_left, np_right)
        got_out = exchange(out_send)
        g_o_cols = jnp.zeros((8 * HEAD_SIZE, eighth), BF16)
        for p, part in enumerate(o_parts):
            g_o_cols = lax.dynamic_update_slice(
                g_o_cols, part, (jnp.bitwise_xor(head, p) * 2 * HEAD_SIZE, 0)
            )
        d_own = jnp.where(first, grad_even, grad_odd)
        d_far = jnp.where(first, grad_odd, grad_even)
        g_qkv = both_cores(normed, d_own, links.c(far_part(normed, d_far)))
        attn_sum = jnp.concatenate([g_qkv, g_o_cols], axis=1)
        g_attn = over_planes(attn_sum)
        np_l, np_r, attn_sum, *ff_parts = sync(np_l, np_r, attn_sum, *ff_parts)
        np_lf, np_rf, got_out = sync(*links.scatter_two(np_left, np_right, np_l, np_r), got_out)
        normed_grad = links.scatter_end(np_left, np_right, np_l, np_r, np_lf, np_rf)
        pre_upstream, prenorm_part = norm_backward(normed_grad, hidden_zero, factor_pre, gain_pre)
        token_rows = ((hidden_one_grad + pre_upstream) * valid).astype(BF16)
        norm_plane = links.sum_plane(jnp.stack([prenorm_part, midnorm_part]))
        token_send, norm_plane = sync(send_layout(token_rows), norm_plane)
        got_grad = exchange(token_send)
        g_down = after(g_down, token_send)
        down_x = links.x(g_down)
        gate_gradient = place_columns(rank, ff_parts, planes, piece, 0)
        up_gradient = place_columns(rank, ff_parts, planes, piece, 1)
        out_tokens = to_stream(got_out)
        g_attn, down_x, gate_gradient, up_gradient, out_tokens = sync(
            g_attn, down_x, gate_gradient, up_gradient, out_tokens
        )
        attn_parts = by_rank(g_attn)
        norm_parts = links.sum_planes(norm_plane)
        down_gradient = place_rows(
            2 * x_me + c_me, [g_down, links.c(g_down), down_x, links.c(down_x)]
        )
        query_gradient, key_gradient, value_gradient, output_gradient = place_attention(
            rank, attn_parts
        )
        grad_tokens = to_stream(after(got_grad, down_gradient))
        norm_own = lax.dynamic_slice(
            norm_parts, (0, group_me * prenorm_gain.shape[0]), (2, prenorm_gain.shape[0])
        )
        return (
            out_tokens,
            grad_tokens,
            query_gradient,
            key_gradient,
            value_gradient,
            output_gradient,
            gate_gradient,
            up_gradient,
            down_gradient,
            norm_own[0],
            norm_own[1],
        )

    return body


def solution(mesh):
    planes = mesh.shape["fsdp"] // 2
    grid = Mesh(mesh.devices.reshape(planes, 2, 2, 2), AXES)
    rows = ("z", "y")
    stream = P(None, rows, ("x", "c"))
    weight = P(rows, None)
    gain = P(rows)
    return jax.shard_map(
        make_body(planes),
        mesh=grid,
        in_specs=(stream, stream) + (weight,) * 7 + (gain, gain, P(), P()),
        out_specs=(stream, stream) + (weight,) * 7 + (gain, gain),
        check_vma=False,
    )
```

```python
import math

import jax
import jax.numpy as jnp
from jax import lax
from jax.experimental import pallas as pl
from jax.experimental.pallas import tpu as pltpu
from jax.sharding import Mesh
from jax.sharding import PartitionSpec as P

QUERY_HEADS = 8
KEY_VALUE_HEADS = 4
HEAD_SIZE = 256

EPS_NORM = 1e-06
ROPE_BASE = 1000042.0
MASK_FILL = -1e30
AXES = ("z", "y", "x", "c")
F32 = jnp.float32
BF16 = jnp.bfloat16


def dot(a, b, dims):
    return lax.dot_general(a, b, (dims, ((), ())), preferred_element_type=F32)


def mm(a, b):
    return dot(a, b, ((1,), (0,)))


def mm_nt(a, b):
    return dot(a, b, ((1,), (1,)))


def mm_tn(a, b):
    return dot(a, b, ((0,), (0,)))


def sync(*values):
    return lax.optimization_barrier(values)


def after(value, *others):
    return lax.optimization_barrier((value,) + others)[0]


class Links:
    def __init__(self, planes):
        self.planes = planes

        def pairs(move):
            out = []
            for z in range(planes):
                for y in range(2):
                    for x in range(2):
                        for c in range(2):
                            a, b, d, e = move(z, y, x, c)
                            out.append((((z * 2 + y) * 2 + x) * 2 + c, ((a * 2 + b) * 2 + d) * 2 + e))
            return out

        self.px = pairs(lambda z, y, x, c: (z, y, 1 - x, c))
        self.py = pairs(lambda z, y, x, c: (z, 1 - y, x, c))
        self.pxy = pairs(lambda z, y, x, c: (z, 1 - y, 1 - x, c))
        self.pc = pairs(lambda z, y, x, c: (z, y, x, 1 - c))
        self.pz = [
            pairs(lambda z, y, x, c, k=k: ((z + k) % planes, y, x, c)) for k in range(planes)
        ]
        self.pz_swap = []
        k = 1
        while k < planes:
            self.pz_swap.append(pairs(lambda z, y, x, c, k=k: (z ^ k, y, x, c)))
            k *= 2

    def x(self, a):
        return lax.ppermute(a, AXES, self.px)

    def y(self, a):
        return lax.ppermute(a, AXES, self.py)

    def c(self, a):
        return lax.ppermute(a, AXES, self.pc)

    def swap_chips(self, chunks):
        return [
            chunks[0],
            self.x(chunks[1]),
            self.y(chunks[2]),
            lax.ppermute(chunks[3], AXES, self.pxy),
        ]

    def sum_plane(self, a):
        for p in (self.pc, self.px, self.py):
            a = a + lax.ppermute(a, AXES, p)
        return a

    def sum_planes(self, a):
        for p in self.pz_swap:
            a = a + lax.ppermute(a, AXES, p)
        return a

    def gather_one(self, a):
        return self.x(a), self.y(a)

    def gather_two(self, ax, ay):
        m = ax.shape[0] // 2
        return self.x(ay[:m]), self.y(ax[m:])

    def scatter_one(self, left, right):
        n = left.shape[0] // 4
        l4 = left.reshape(4, n, left.shape[1])
        return self.x(jnp.stack([l4[1], l4[3]])), self.y(right[2 * n :].reshape(2, n, right.shape[1]))

    def scatter_two(self, left, right, gl, gr):
        n = left.shape[0] // 4
        l_far = self.y((left[2 * n : 3 * n].astype(F32) + gl[1]).astype(BF16))
        r_far = self.x((right[n : 2 * n].astype(F32) + gr[1]).astype(BF16))
        return l_far, r_far

    def scatter_end(self, left, right, gl, gr, l_far, r_far):
        n = left.shape[0] // 4
        l_own = left[:n].astype(F32) + gl[0] + l_far
        r_own = right[:n].astype(F32) + gr[0] + r_far
        return jnp.concatenate([l_own, r_own], axis=1)

    def gather_planes(self, a):
        got = lax.all_gather(a, ("c", "z"), axis=0, tiled=True)
        return got.reshape(2, self.planes * a.shape[0], a.shape[1])

    def gather_gains(self, a):
        n = a.shape[1]
        y_me = lax.axis_index("y")
        z_me = lax.axis_index("z")
        two = pair(y_me, a, self.y(a))
        out = jnp.zeros((self.planes,) + two.shape, a.dtype)
        for k in range(self.planes):
            part = two if k == 0 else lax.ppermute(two, AXES, self.pz[k])
            at = lax.rem(z_me - k + self.planes, self.planes)
            out = lax.dynamic_update_slice(out, part[None], (at, 0, 0, 0))
        return jnp.transpose(out, (2, 0, 1, 3)).reshape(2, 2 * self.planes * n)


def pair(bit, own, other):
    return jnp.stack([jnp.where(bit == 0, own, other), jnp.where(bit == 0, other, own)])


def estimate(flops, bytes_accessed, transcendentals):
    return pl.CostEstimate(
        flops=flops // 1,
        bytes_accessed=bytes_accessed // 1,
        transcendentals=transcendentals // 1,
    )


def rank_scalar(rank):
    return jnp.reshape(rank, (1,)).astype(jnp.int32)


def place_columns(rank, parts, planes, piece, side):
    n = parts[0].shape[0]
    width = planes * piece
    total = 8 * width
    if piece % 128:
        parts = [t[:, side * width : (side + 1) * width] for t in parts]
        out = jnp.zeros((n, planes, 8, piece), F32)
        for p, part in enumerate(parts):
            part = part.reshape(n, planes, 1, piece).astype(F32)
            out = lax.dynamic_update_slice(out, part, (0, 0, jnp.bitwise_xor(rank, p), 0))
        return out.reshape(n, total)
    tile = min(n, 64)

    def kernel(rank_ref, *refs):
        out = refs[8]
        for p in range(8):
            t = jnp.bitwise_xor(rank_ref[0], p)
            for z in range(planes):
                at = pl.multiple_of(z * 8 * piece + t * piece, 128)
                out[:, pl.ds(at, piece)] = refs[p][:, z * piece : (z + 1) * piece].astype(F32)

    return pl.pallas_call(
        kernel,
        out_shape=jax.ShapeDtypeStruct((n, total), F32),
        grid_spec=pltpu.PrefetchScalarGridSpec(
            num_scalar_prefetch=1,
            grid=(n // tile,),
            in_specs=[pl.BlockSpec((tile, width), lambda i, r: (i, side))] * 8,
            out_specs=pl.BlockSpec((tile, total), lambda i, r: (i, 0)),
        ),
        cost_estimate=estimate(flops=0, bytes_accessed=6 * n * total, transcendentals=0),
    )(rank_scalar(rank), *parts)


def place_rows(order, parts):
    n, d = parts[0].shape
    tile = min(d, 256)

    def kernel(order_ref, *refs):
        out = refs[4]
        for p in range(4):
            t = jnp.bitwise_xor(order_ref[0], p)
            out[pl.ds(pl.multiple_of(t * n, 8), n), :] = refs[p][...].astype(F32)

    return pl.pallas_call(
        kernel,
        out_shape=jax.ShapeDtypeStruct((4 * n, d), F32),
        grid_spec=pltpu.PrefetchScalarGridSpec(
            num_scalar_prefetch=1,
            grid=(d // tile,),
            in_specs=[pl.BlockSpec((n, tile), lambda i, r: (0, i))] * 4,
            out_specs=pl.BlockSpec((4 * n, tile), lambda i, r: (0, i)),
        ),
        cost_estimate=estimate(flops=0, bytes_accessed=24 * n * d, transcendentals=0),
    )(rank_scalar(order), *parts)


def place_attention(rank, parts):
    n, width = parts[0].shape
    h = HEAD_SIZE
    o = width - 2 * h
    tile = min(n, 64)

    def kernel(rank_ref, *refs):
        q_out, k_out, v_out, o_out = refs[8:]
        for p in range(8):
            t = jnp.bitwise_xor(rank_ref[0], p)
            j = t // 2
            core = t - 2 * j
            q_out[:, pl.ds(pl.multiple_of(t * h, 128), h)] = refs[p][:, :h].astype(F32)
            at = pl.ds(pl.multiple_of(j * h, 128), h)

            @pl.when(core == 0)
            def _():
                k_out[:, at] = refs[p][:, h : 2 * h].astype(F32)

            @pl.when(core == 1)
            def _():
                v_out[:, at] = refs[p][:, h : 2 * h].astype(F32)

            to = pl.multiple_of(core * 4 * o + j * o, 128)
            o_out[:, pl.ds(to, o)] = refs[p][:, 2 * h :].astype(F32)

    widths = (8 * h, 4 * h, 4 * h, 8 * o)
    return pl.pallas_call(
        kernel,
        out_shape=tuple(jax.ShapeDtypeStruct((n, w), F32) for w in widths),
        grid_spec=pltpu.PrefetchScalarGridSpec(
            num_scalar_prefetch=1,
            grid=(n // tile,),
            in_specs=[pl.BlockSpec((tile, width), lambda i, r: (i, 0))] * 8,
            out_specs=tuple(pl.BlockSpec((tile, w), lambda i, r: (i, 0)) for w in widths),
        ),
        cost_estimate=estimate(flops=0, bytes_accessed=48 * n * width, transcendentals=0),
    )(rank_scalar(rank), *parts)


def back_product(core, lefts, weight):
    m, k = lefts[0].shape
    n = weight.shape[1]
    tile = min(n // 2, 256)
    steps = n // 2 // tile

    def kernel(core_ref, a0, a1, l0, l1, r0, r1, left, right):
        left[...] = (mm_nt(a0[...], l0[...]) + mm_nt(a1[...], l1[...])).astype(BF16)
        right[...] = (mm_nt(a0[...], r0[...]) + mm_nt(a1[...], r1[...])).astype(BF16)

    whole = pl.BlockSpec((m, k), lambda i, r: (0, 0))
    out = pl.BlockSpec((m, tile), lambda i, r: (0, i))
    return pl.pallas_call(
        kernel,
        out_shape=(jax.ShapeDtypeStruct((m, n // 2), BF16),) * 2,
        grid_spec=pltpu.PrefetchScalarGridSpec(
            num_scalar_prefetch=1,
            grid=(steps,),
            in_specs=[
                whole,
                whole,
                pl.BlockSpec((None, tile, k), lambda i, r: (r[0], i, 0)),
                pl.BlockSpec((None, tile, k), lambda i, r: (1 - r[0], i, 0)),
                pl.BlockSpec((None, tile, k), lambda i, r: (r[0], i + steps, 0)),
                pl.BlockSpec((None, tile, k), lambda i, r: (1 - r[0], i + steps, 0)),
            ],
            out_specs=(out, out),
        ),
        cost_estimate=estimate(
            flops=4 * m * k * n, bytes_accessed=4 * (m + n) * k + 2 * m * n, transcendentals=0
        ),
    )(rank_scalar(core), *lefts, weight, weight, weight, weight)


def weight_product(left, right, other=None):
    m, k = left.shape
    n = right.shape[1]
    tile = 256

    def kernel(a, b, *refs):
        total = mm(a[...], b[...])
        if other is not None:
            total = total + refs[0][...]
        refs[-1][...] = total.astype(BF16)

    out = pl.BlockSpec((m, tile), lambda i: (0, i))
    more = () if other is None else (other,)
    return pl.pallas_call(
        kernel,
        out_shape=jax.ShapeDtypeStruct((m, n), BF16),
        grid=(n // tile,),
        in_specs=[
            pl.BlockSpec((m, k), lambda i: (0, 0)),
            pl.BlockSpec((k, tile), lambda i: (0, i)),
        ]
        + [out] * len(more),
        out_specs=out,
        cost_estimate=estimate(
            flops=2 * m * k * n,
            bytes_accessed=2 * (m * k + k * n + (1 + len(more)) * m * n),
            transcendentals=0,
        ),
    )(left, right, *more)


def ff_front(half, n2, weight):
    m, d = n2.shape
    f = weight.shape[2] // 2
    tile = 256
    steps = f // tile

    def kernel(half_ref, x, wg, wu, gate_out, up_out, act_out):
        gate = mm(x[...], wg[...])
        up = mm(x[...], wu[...])
        gate_out[...] = gate
        up_out[...] = up
        act_out[...] = (gate * jax.nn.sigmoid(gate) * up).astype(BF16)

    out = pl.BlockSpec((m, tile), lambda i, r: (0, i))
    return pl.pallas_call(
        kernel,
        out_shape=(
            jax.ShapeDtypeStruct((m, f), F32),
            jax.ShapeDtypeStruct((m, f), F32),
            jax.ShapeDtypeStruct((m, f), BF16),
        ),
        grid_spec=pltpu.PrefetchScalarGridSpec(
            num_scalar_prefetch=1,
            grid=(steps,),
            in_specs=[
                pl.BlockSpec((m, d), lambda i, r: (0, 0)),
                pl.BlockSpec((None, d, tile), lambda i, r: (r[0], 0, i)),
                pl.BlockSpec((None, d, tile), lambda i, r: (r[0], 0, i + steps)),
            ],
            out_specs=(out, out, out),
        ),
        cost_estimate=estimate(
            flops=4 * m * d * f, bytes_accessed=2 * m * d + 4 * d * f + 10 * m * f, transcendentals=m * f
        ),
    )(rank_scalar(half), n2, weight, weight)


def ff_back(half, d_in, weight, gate_pre, up_pre):
    m, d = d_in.shape
    f = weight.shape[1]
    tile = 256
    steps = f // tile

    def kernel(half_ref, g, w, gate_ref, up_ref, out, kept):
        i = pl.program_id(0)

        @pl.when(i < steps)
        def _():
            act_grad = mm_nt(g[...], w[...])
            gate = gate_ref[...]
            sig = jax.nn.sigmoid(gate)
            out[...] = (act_grad * up_ref[...] * sig * (1.0 + gate * (1.0 - sig))).astype(BF16)
            kept[i] = (act_grad * (gate * sig)).astype(BF16)

        @pl.when(i >= steps)
        def _():
            out[...] = kept[i - steps]

    last = steps - 1
    pre = pl.BlockSpec((m, tile), lambda i, r: (0, jnp.minimum(i, last)))
    return pl.pallas_call(
        kernel,
        out_shape=jax.ShapeDtypeStruct((m, 2 * f), BF16),
        grid_spec=pltpu.PrefetchScalarGridSpec(
            num_scalar_prefetch=1,
            grid=(2 * steps,),
            in_specs=[
                pl.BlockSpec((m, d), lambda i, r: (0, 0)),
                pl.BlockSpec((None, tile, d), lambda i, r: (r[0], jnp.minimum(i, last), 0)),
                pre,
                pre,
            ],
            out_specs=pl.BlockSpec((m, tile), lambda i, r: (0, i)),
            scratch_shapes=[pltpu.VMEM((steps, m, tile), BF16)],
        ),
        cost_estimate=estimate(
            flops=2 * m * d * f, bytes_accessed=2 * (m + f) * d + 12 * m * f, transcendentals=m * f
        ),
    )(rank_scalar(half), d_in, weight, gate_pre, up_pre)


def forward_product(core, lefts, weight):
    m, k = lefts[0].shape
    n = weight.shape[2]
    tile = 256
    steps = n // 2 // tile

    def kernel(core_ref, a0, a1, l0, l1, r0, r1, left, right):
        left[...] = (mm(a0[...], l0[...]) + mm(a1[...], l1[...])).astype(BF16)
        right[...] = (mm(a0[...], r0[...]) + mm(a1[...], r1[...])).astype(BF16)

    whole = pl.BlockSpec((m, k), lambda i, r: (0, 0))
    out = pl.BlockSpec((m, tile), lambda i, r: (0, i))
    return pl.pallas_call(
        kernel,
        out_shape=(jax.ShapeDtypeStruct((m, n // 2), BF16),) * 2,
        grid_spec=pltpu.PrefetchScalarGridSpec(
            num_scalar_prefetch=1,
            grid=(steps,),
            in_specs=[
                whole,
                whole,
                pl.BlockSpec((None, k, tile), lambda i, r: (r[0], 0, i)),
                pl.BlockSpec((None, k, tile), lambda i, r: (1 - r[0], 0, i)),
                pl.BlockSpec((None, k, tile), lambda i, r: (r[0], 0, i + steps)),
                pl.BlockSpec((None, k, tile), lambda i, r: (1 - r[0], 0, i + steps)),
            ],
            out_specs=(out, out),
        ),
        cost_estimate=estimate(
            flops=4 * m * k * n, bytes_accessed=4 * (m + n) * k + 2 * m * n, transcendentals=0
        ),
    )(rank_scalar(core), *lefts, weight, weight, weight, weight)


def send_blocks(slot, has, streams):
    groups = slot.shape[0]
    _, r, f = streams[0].shape
    count = len(streams)

    def kernel(slot_ref, has_ref, *refs):
        keep = has_ref[pl.program_id(0)] > 0
        for i in range(count):
            v = refs[i][0]
            refs[count][0, i] = jnp.where(keep, v, jnp.zeros_like(v))

    return pl.pallas_call(
        kernel,
        out_shape=jax.ShapeDtypeStruct((groups, count, r, f), BF16),
        grid_spec=pltpu.PrefetchScalarGridSpec(
            num_scalar_prefetch=2,
            grid=(groups,),
            in_specs=[pl.BlockSpec((1, r, f), lambda g, s, h: (s[g], 0, 0))] * count,
            out_specs=pl.BlockSpec((1, count, r, f), lambda g, s, h: (g, 0, 0, 0)),
        ),
        cost_estimate=estimate(
            flops=0, bytes_accessed=4 * count * groups * r * f, transcendentals=0
        ),
    )(slot, has, *streams)


def take_blocks(slot, has, got):
    slots = slot.shape[0]
    _, _, r, f = got.shape

    def kernel(slot_ref, has_ref, x, a, b):
        keep = has_ref[pl.program_id(0)] > 0
        for i, out in enumerate((a, b)):
            v = x[0, i]
            out[0] = jnp.where(keep, v, jnp.zeros_like(v))

    out = pl.BlockSpec((1, r, f), lambda g, s, h: (g, 0, 0))
    return pl.pallas_call(
        kernel,
        out_shape=(jax.ShapeDtypeStruct((slots, r, f), BF16),) * 2,
        grid_spec=pltpu.PrefetchScalarGridSpec(
            num_scalar_prefetch=2,
            grid=(slots,),
            in_specs=[pl.BlockSpec((1, 2, r, f), lambda g, s, h: (s[g], 0, 0, 0))],
            out_specs=(out, out),
        ),
        cost_estimate=estimate(
            flops=0, bytes_accessed=8 * slots * r * f, transcendentals=0
        ),
    )(slot, has, got)


def assemble_rows(info, pieces, gain=None):
    _, _, r, f = pieces[0].shape
    width = 4 * f

    def block(i, n):
        return 2 * jnp.bitwise_xor(n[0], (i // 2) % 2) + i % 2

    def kernel(info_ref, *refs):
        own, ax, ay, dx, dy = refs[:5]
        i = pl.program_id(0)
        x = info_ref[0]
        near = i < 4
        low = block(i, info_ref) < 2
        same = jnp.where(near, own[0], ay[0])
        other = jnp.where(near, ax[0], jnp.where(low, dx[0], dy[0]))
        at = info_ref[2 + i] * r + lax.broadcasted_iota(jnp.int32, (r, f), 0)
        inside = at < info_ref[1]
        parts = []
        for h, v in ((x, same), (1 - x, other)):
            for c in range(2):
                t = jnp.where(inside, v[c].astype(F32), 0.0)
                parts.append((2 * h + c, t))
        if gain is None:
            for q, t in parts:
                refs[5][:, pl.ds(pl.multiple_of(q * f, 128), f)] = t.astype(BF16)
            return
        gain_ref, normed, rows = refs[5:]
        total = sum(jnp.sum(t * t, axis=1, keepdims=True) for _, t in parts)
        factor = lax.rsqrt(total * (1.0 / width) + EPS_NORM)
        for q, t in parts:
            g = gain_ref[pl.ds(q, 1), :]
            normed[:, pl.ds(pl.multiple_of(q * f, 128), f)] = (t * factor * g).astype(BF16)

        @pl.when(i < 2)
        def _():
            for q, t in parts:
                rows[:, pl.ds(pl.multiple_of(q * f, 128), f)] = t.astype(BF16)

    whole = pl.BlockSpec((1, 2, r, f), lambda i, n: (block(i, n), 0, 0, 0))
    specs = [
        whole,
        whole,
        whole,
        pl.BlockSpec((1, 2, r, f), lambda i, n: (jnp.minimum(block(i, n), 1), 0, 0, 0)),
        pl.BlockSpec((1, 2, r, f), lambda i, n: (jnp.maximum(block(i, n) - 2, 0), 0, 0, 0)),
    ]
    shape = [jax.ShapeDtypeStruct((8 * r, width), BF16)]
    outs = [pl.BlockSpec((r, width), lambda i, n: (i, 0))]
    args = list(pieces)
    if gain is not None:
        specs.append(pl.BlockSpec((4, f), lambda i, n: (0, 0)))
        args.append(gain)
        shape.append(jax.ShapeDtypeStruct((2 * r, width), BF16))
        outs.append(pl.BlockSpec((r, width), lambda i, n: (jnp.minimum(i, 1), 0)))
    got = pl.pallas_call(
        kernel,
        out_shape=tuple(shape),
        grid_spec=pltpu.PrefetchScalarGridSpec(
            num_scalar_prefetch=1, grid=(8,), in_specs=specs, out_specs=tuple(outs)
        ),
        cost_estimate=estimate(
            flops=16 * r * width, bytes_accessed=40 * r * width, transcendentals=0
        ),
    )(info, *args)
    return got[0] if gain is None else got


def turn(v, cos_t, sin_t, sign):
    h = v.shape[-1] // 2
    a, b = v[:, :h], v[:, h:]
    s = sin_t * sign
    return jnp.concatenate([a * cos_t - b * s, b * cos_t + a * s], axis=-1).astype(BF16)


def project(normed, w_attn, cos_t, sin_t):
    rows, width = normed.shape
    h = HEAD_SIZE
    tile = 256

    def kernel(x_ref, w_ref, c_ref, s_ref, q0, q1, k, v):
        even = mm(x_ref[...], w_ref[0])
        odd = mm(x_ref[...], w_ref[1])
        cos_t, sin_t = c_ref[...], s_ref[...]
        q0[...] = turn(even[:, :h], cos_t, sin_t, 1.0)
        k[...] = turn(even[:, h:], cos_t, sin_t, 1.0)
        q1[...] = turn(odd[:, :h], cos_t, sin_t, 1.0)
        v[...] = odd[:, h:].astype(BF16)

    out = pl.BlockSpec((tile, h), lambda i: (i, 0))
    table = pl.BlockSpec((tile, h // 2), lambda i: (i, 0))
    return pl.pallas_call(
        kernel,
        out_shape=(jax.ShapeDtypeStruct((rows, h), BF16),) * 4,
        grid=(rows // tile,),
        in_specs=[
            pl.BlockSpec((tile, width), lambda i: (i, 0)),
            pl.BlockSpec((2, width, 2 * h), lambda i: (0, 0, 0)),
            table,
            table,
        ],
        out_specs=(out,) * 4,
        cost_estimate=estimate(
            flops=8 * rows * width * h, bytes_accessed=2 * rows * width + 8 * width * h, transcendentals=0
        ),
    )(normed, w_attn, cos_t, sin_t)


def attend(q0, q1, keys, values, w_o, at_q, at_k):
    rows, h = q0.shape
    half = w_o.shape[2]
    tile = 256
    factor = 1.0 / math.sqrt(HEAD_SIZE)

    def kernel(q0_ref, q1_ref, k_ref, v_ref, w_ref, aq_ref, ak_ref, mixed, lse, left, right):
        allowed = ak_ref[...] <= aq_ref[...]
        for i, q_ref in enumerate((q0_ref, q1_ref)):
            scores = jnp.where(allowed, mm_nt(q_ref[...], k_ref[...]) * factor, MASK_FILL)
            top = jnp.max(scores, axis=-1, keepdims=True)
            e = jnp.exp(scores - top)
            total = jnp.sum(e, axis=-1, keepdims=True)
            probs = (e * (1.0 / total)).astype(BF16)
            mixed[:, i * h : (i + 1) * h] = mm(probs, v_ref[...]).astype(BF16)
            lse[i] = top + jnp.log(total)
        left[...] = mm(mixed[...], w_ref[0]).astype(BF16)
        right[...] = mm(mixed[...], w_ref[1]).astype(BF16)

    q_spec = pl.BlockSpec((tile, h), lambda i: (i, 0))
    kv_spec = pl.BlockSpec((rows, h), lambda i: (0, 0))
    out_spec = pl.BlockSpec((tile, half), lambda i: (i, 0))
    return pl.pallas_call(
        kernel,
        out_shape=(
            jax.ShapeDtypeStruct((rows, 2 * h), BF16),
            jax.ShapeDtypeStruct((2, rows, 1), F32),
            jax.ShapeDtypeStruct((rows, half), BF16),
            jax.ShapeDtypeStruct((rows, half), BF16),
        ),
        grid=(rows // tile,),
        in_specs=[
            q_spec,
            q_spec,
            kv_spec,
            kv_spec,
            pl.BlockSpec((2, 2 * h, half), lambda i: (0, 0, 0)),
            pl.BlockSpec((tile, 1), lambda i: (i, 0)),
            pl.BlockSpec((1, rows), lambda i: (0, 0)),
        ],
        out_specs=(
            pl.BlockSpec((tile, 2 * h), lambda i: (i, 0)),
            pl.BlockSpec((2, tile, 1), lambda i: (0, i, 0)),
            out_spec,
            out_spec,
        ),
        cost_estimate=estimate(
            flops=8 * rows * rows * h + 8 * rows * h * half,
            bytes_accessed=12 * rows * h + 8 * h * half + 4 * rows * half,
            transcendentals=2 * rows * rows,
        ),
    )(q0, q1, keys, values, w_o, at_q, at_k)


def attend_back(attn_in, w_o, q0, q1, keys, values, lse, at_q, at_k, cos_t, sin_t):
    rows, h = q0.shape
    half = w_o.shape[2]
    tile = 256
    steps = rows // tile
    factor = 1.0 / math.sqrt(HEAD_SIZE)

    def kernel(
        g_ref, w_ref, q0_ref, q1_ref, k_ref, v_ref, lse_ref, aq_ref, ak_ref, c_ref, s_ref, ca_ref,
        sa_ref, dq0, dq1, dk, dv, k_sum, v_sum,
    ):
        step = pl.program_id(0)

        @pl.when(step == 0)
        def _():
            k_sum[...] = jnp.zeros_like(k_sum)
            v_sum[...] = jnp.zeros_like(v_sum)

        g = g_ref[...]
        dmix = (mm_nt(g[:, :half], w_ref[0]) + mm_nt(g[:, half:], w_ref[1])).astype(BF16)
        allowed = ak_ref[...] <= aq_ref[...]
        for i, (q_ref, dq) in enumerate(((q0_ref, dq0), (q1_ref, dq1))):
            d = dmix[:, i * h : (i + 1) * h]
            scores = jnp.where(allowed, mm_nt(q_ref[...], k_ref[...]) * factor, MASK_FILL)
            probs = jnp.exp(scores - lse_ref[i])
            v_sum[...] += mm_tn(probs.astype(BF16), d)
            prob_grad = mm_nt(d, v_ref[...])
            inner = jnp.sum(prob_grad * probs, axis=-1, keepdims=True)
            score_grad = (probs * (prob_grad - inner)).astype(BF16)
            k_sum[...] += mm_tn(score_grad, q_ref[...])
            rot = (mm(score_grad, k_ref[...]) * factor).astype(BF16).astype(F32)
            dq[...] = turn(rot, c_ref[...], s_ref[...], -1.0)

        @pl.when(step == steps - 1)
        def _():
            rot = (k_sum[...] * factor).astype(BF16).astype(F32)
            dk[...] = turn(rot, ca_ref[...], sa_ref[...], -1.0)
            dv[...] = v_sum[...].astype(BF16)

    q_spec = pl.BlockSpec((tile, h), lambda i: (i, 0))
    kv_spec = pl.BlockSpec((rows, h), lambda i: (0, 0))
    table = pl.BlockSpec((tile, h // 2), lambda i: (i, 0))
    all_table = pl.BlockSpec((rows, h // 2), lambda i: (0, 0))
    return pl.pallas_call(
        kernel,
        out_shape=(jax.ShapeDtypeStruct((rows, h), BF16),) * 4,
        grid=(steps,),
        in_specs=[
            pl.BlockSpec((tile, 2 * half), lambda i: (i, 0)),
            pl.BlockSpec((2, 2 * h, half), lambda i: (0, 0, 0)),
            q_spec,
            q_spec,
            kv_spec,
            kv_spec,
            pl.BlockSpec((2, tile, 1), lambda i: (0, i, 0)),
            pl.BlockSpec((tile, 1), lambda i: (i, 0)),
            pl.BlockSpec((1, rows), lambda i: (0, 0)),
            table,
            table,
            all_table,
            all_table,
        ],
        out_specs=(q_spec, q_spec, kv_spec, kv_spec),
        scratch_shapes=[pltpu.VMEM((rows, h), F32), pltpu.VMEM((rows, h), F32)],
        cost_estimate=estimate(
            flops=20 * rows * rows * h + 8 * rows * h * half,
            bytes_accessed=20 * rows * h + 8 * h * half + 4 * rows * half,
            transcendentals=2 * rows * rows,
        ),
    )(attn_in, w_o, q0, q1, keys, values, lse, at_q, at_k, cos_t, sin_t, cos_t, sin_t)


def rope_tables(positions):
    half_dim = HEAD_SIZE // 2
    frequency = jnp.exp(jnp.arange(half_dim, dtype=F32) * (-2.0 * math.log(ROPE_BASE) / HEAD_SIZE))
    angles = positions.astype(F32)[:, None] * frequency[None, :]
    return jnp.cos(angles), jnp.sin(angles)


def norm_factor(hidden):
    return lax.rsqrt(jnp.mean(hidden * hidden, axis=-1, keepdims=True) + EPS_NORM)


def norm_backward(upstream, hidden, factor, gain_vec):
    scaled = upstream * gain_vec
    gain_part = jnp.sum(upstream * hidden * factor, axis=0)
    inner_sum = jnp.mean(scaled * hidden, axis=-1, keepdims=True)
    return (factor * scaled - hidden * (factor * factor * factor) * inner_sum, gain_part)


def make_body(planes):
    links = Links(planes)

    def body(
        tokens,
        cotangent,
        query_weight,
        key_matrix,
        value_matrix,
        output_weight,
        gate_weight,
        up_weight,
        down_weight,
        prenorm_gain,
        midnorm_gain,
        seq_len,
        stream_order,
    ):
        groups = 2 * planes
        z_me = lax.axis_index("z")
        y_me = lax.axis_index("y")
        x_me = lax.axis_index("x")
        c_me = lax.axis_index("c")
        slots, blk, quarter = tokens.shape
        width = 4 * quarter
        rank = 4 * y_me + 2 * x_me + c_me
        head = 2 * y_me + x_me
        shard = query_weight.shape[0]
        ff = gate_weight.shape[1]
        piece = ff // groups // 4

        nblk = (seq_len + blk - 1) // blk
        member = (stream_order[:, None] == jnp.arange(groups, dtype=jnp.int32)[None, :]).astype(
            jnp.int32
        )
        ordered = jnp.sum(member * nblk[None, :], axis=1)
        firsts = jnp.cumsum(ordered) - ordered
        seq_start = jnp.sum(member * firsts[:, None], axis=0)
        group_me = 2 * z_me + y_me
        offset = lax.rem(group_me - lax.rem(seq_start, groups) + groups, groups)
        has = offset < nblk
        slot_of = jnp.where(has, (seq_start + offset) // groups, 0)
        block_ids = jnp.arange(slots, dtype=jnp.int32) * groups + group_me
        ahead = block_ids[:, None] - seq_start[None, :]
        covers = ((ahead >= 0) & (ahead < nblk[None, :])).astype(jnp.int32)
        seq_of = jnp.sum(covers * jnp.arange(groups, dtype=jnp.int32)[None, :], axis=1)
        taken = jnp.sum(covers, axis=1)

        mine = 2 * z_me + c_me
        picked = jnp.arange(groups, dtype=jnp.int32) == mine
        my_start = jnp.sum(jnp.where(picked, seq_start, 0))
        my_len = jnp.sum(jnp.where(picked, seq_len, 0))

        def block_places(y):
            first = lax.rem(y + my_start, 2)
            plane = lax.rem((my_start + first) // 2, planes)
            k = jnp.arange(4, dtype=jnp.int32)
            if planes == 4:
                k = lax.rem(k - plane + planes, planes)
            return first + 2 * k, plane

        places_own, plane_own = block_places(y_me)
        places_far, _ = block_places(1 - y_me)

        def two_places(places, x):
            return lax.dynamic_slice(places, (2 * x,), (2,))

        places = jnp.concatenate(
            [
                two_places(places_own, x_me),
                two_places(places_own, 1 - x_me),
                two_places(places_far, x_me),
                two_places(places_far, 1 - x_me),
            ]
        )
        info = jnp.concatenate([jnp.stack([x_me, my_len]), places]).astype(jnp.int32)
        positions = (places[:, None] * blk + jnp.arange(blk, dtype=jnp.int32)[None, :]).reshape(-1)
        at_q = positions[:, None]
        at_k = jnp.where(positions < my_len, positions, 1 << 30)[None, :]
        rows = 2 * blk
        valid = (positions[:rows] < my_len).astype(F32)[:, None]

        def send_layout(out_rows, count):
            left, right = out_rows[:, : 2 * quarter], out_rows[:, 2 * quarter :]
            keep = jnp.where(x_me == 0, left, right)
            got = links.x(jnp.where(x_me == 0, right, left))
            send = pair(x_me, keep, got).reshape(2, count, 2, blk, 2, quarter)
            send = jnp.transpose(send, (0, 2, 4, 1, 3, 5)).reshape(4, 2, count, blk, quarter)
            if planes > 4:
                send = jnp.pad(send, ((0, planes - 4),) + ((0, 0),) * 4)
                send = jnp.roll(send, plane_own, axis=0)
            return send.reshape(groups, count, blk, quarter)

        def by_chip(g):
            n = g.shape[1]
            own = lax.dynamic_slice(g, (y_me * shard, 0), (shard, n))
            other = lax.dynamic_slice(g, ((1 - y_me) * shard, 0), (shard, n))
            return links.swap_chips([own, own, other, other])

        def by_rank(chips):
            return [links.c(chips[p // 2]) if p % 2 else chips[p // 2] for p in range(8)]

        def plane_rows(own_part, far_part):
            got = links.y(far_part)
            both = pair(y_me, own_part, got)
            return both.reshape(2 * own_part.shape[0], own_part.shape[1])

        def ff_columns(w, r):
            return jnp.concatenate(
                [
                    lax.dynamic_slice(w, (0, p * 8 * piece + r * piece), (shard, piece))
                    for p in range(planes)
                ],
                axis=1,
            )

        far = rank + 4 - 8 * y_me
        def attn_columns(r, ws):
            q = lax.dynamic_slice(ws[0], (0, r * HEAD_SIZE), (shard, HEAD_SIZE))
            j = r // 2
            k = lax.dynamic_slice(ws[1], (0, j * HEAD_SIZE), (shard, HEAD_SIZE))
            v = lax.dynamic_slice(ws[2], (0, j * HEAD_SIZE), (shard, HEAD_SIZE))
            at = lax.rem(r, 2) * (width // 2) + (r // 2) * (width // 8)
            o = lax.dynamic_slice(ws[3], (0, at), (shard, width // 8))
            return jnp.concatenate([q, jnp.where(c_me == 0, k, v), o], axis=1)

        gains = links.gather_gains(jnp.stack([prenorm_gain, midnorm_gain])).astype(F32)

        def to_sequences(stream):
            send = send_blocks(slot_of, has.astype(jnp.int32), [stream])
            return send[:, 0]

        def arranged(got):
            got = got.reshape(planes, 2, blk, quarter)
            if planes > 4:
                got = jnp.roll(got, -plane_own, axis=0)[:4]
            return got

        def exchange(send):
            return lax.all_to_all(send, ("z", "c"), split_axis=0, concat_axis=0, tiled=True)

        send_tokens = to_sequences(tokens)
        got_tokens = exchange(send_tokens)
        *attn_ws, gate_weight, up_weight, down_weight, _ = sync(
            query_weight,
            key_matrix,
            value_matrix,
            output_weight,
            gate_weight,
            up_weight,
            down_weight,
            send_tokens,
        )
        attn_share = plane_rows(attn_columns(rank, attn_ws), attn_columns(far, attn_ws))

        def ff_share(r):
            return jnp.concatenate([ff_columns(gate_weight, r), ff_columns(up_weight, r)], axis=1)

        ff_own, ff_far_rows = ff_share(rank), ff_share(far)
        down_share = lax.dynamic_slice(
            down_weight, ((2 * x_me + c_me) * piece, 0), (piece, width)
        )
        got_tokens, attn_share, ff_own, ff_far_rows, down_share, gains = sync(
            got_tokens, attn_share, ff_own, ff_far_rows, down_share, gains
        )
        w_attn = links.gather_planes(attn_share)
        own = arranged(got_tokens)
        ax, ay = sync(*links.gather_one(own))
        ff_two = plane_rows(ff_own, after(ff_far_rows, own))
        gain_pre, gain_mid = gains[0], gains[1]
        eighth = width // 8

        def spread(chunk_of):
            return links.swap_chips([chunk_of(jnp.bitwise_xor(head, p)) for p in range(4)])

        cos_t, sin_t = rope_tables(positions)
        dx, dy, cos_t, sin_t, ff_two = sync(*links.gather_two(ax, ay), cos_t, sin_t, ff_two)
        w_ff = links.gather_planes(ff_two)
        w_down = links.gather_planes(after(down_share, ff_two))
        normed, rows_in = assemble_rows(info, (own, ax, ay, dx, dy), gain_pre.reshape(4, quarter))
        send_cot = to_sequences(after(cotangent, dx))
        w_attn, normed, send_cot = sync(w_attn, normed, send_cot)
        got_cot = exchange(send_cot)
        w_o_cols = lax.dynamic_index_in_dim(w_attn, c_me, 0, keepdims=False)[:, 2 * HEAD_SIZE :]
        w_o = jnp.zeros((2 * HEAD_SIZE, 4 * eighth), BF16)
        for p, part in enumerate(
            spread(
                lambda t: lax.dynamic_slice(
                    w_o_cols, (t * 2 * HEAD_SIZE, 0), (2 * HEAD_SIZE, eighth)
                )
            )
        ):
            w_o = lax.dynamic_update_slice(w_o, part, (0, jnp.bitwise_xor(head, p) * eighth))
        w_o = pair(c_me, w_o, links.c(w_o))

        q0, q1, keys, values = project(normed, w_attn, cos_t, sin_t)
        mixed, lse, attn_left, attn_right = attend(q0, q1, keys, values, w_o, at_q, at_k)
        hidden_zero = rows_in.astype(F32)
        factor_pre = norm_factor(hidden_zero)
        gl, gr = sync(*links.scatter_one(attn_left, attn_right))
        l_far, r_far = sync(*links.scatter_two(attn_left, attn_right, gl, gr))
        hidden_one = hidden_zero + links.scatter_end(attn_left, attn_right, gl, gr, l_far, r_far)
        factor_mid = norm_factor(hidden_one)
        n_own = (hidden_one * factor_mid * gain_mid).astype(BF16)
        ax, ay, got_cot = sync(*links.gather_one(n_own), got_cot)
        dx, dy = sync(*links.gather_two(ax, ay))
        normed_two = jnp.concatenate([n_own, ax, ay, dx, dy], axis=0)
        own = after(arranged(got_cot), normed_two)
        n_ff = w_ff.shape[2] // 2
        far_gate, far_up, act_far = ff_front(1 - c_me, normed_two, w_ff)
        ax, ay, act_far = sync(*links.gather_one(own), act_far)
        own_gate, own_up, act_own = ff_front(c_me, after(normed_two, ax), w_ff)
        turned = sync(jnp.transpose(after(normed_two, act_own)))[0]
        dx, dy, act_own, turned = sync(*links.gather_two(ax, ay), act_own, turned)
        down_in = assemble_rows(info, (own, ax, ay, dx, dy))

        def far_part(left, right):
            return mm_tn(left, right).astype(BF16)

        def both_cores(left, right, got):
            return (mm_tn(left, right) + got).astype(BF16)

        def over_planes(g):
            return lax.psum_scatter(g, "z", scatter_dimension=0, tiled=True)

        half = width // 2
        down_far = far_part(act_far, down_in)
        sum_down = both_cores(act_own, down_in, links.c(down_far))
        g_down = over_planes(sum_down)
        w_down, d_in = sync(w_down, down_in, sum_down)[:2]
        in_far = ff_back(1 - c_me, d_in, w_down, far_gate, far_up)
        ff_far = weight_product(turned, in_far)
        in_own = ff_back(c_me, after(d_in, ff_far), w_down, own_gate, own_up)
        ff_left, ff_right = forward_product(c_me, (after(act_own, in_own), act_far), w_down)
        in_own, ff_left, ff_right, ff_got = sync(in_own, ff_left, ff_right, links.c(ff_far))
        ff_l, ff_r = links.scatter_one(ff_left, ff_right)
        sum_ff = weight_product(turned, in_own, ff_got)
        g_ff = over_planes(sum_ff)
        dn_left, dn_right = back_product(c_me, (after(in_own, sum_ff), in_far), w_ff)
        dn_left, dn_right, ff_l, ff_r, g_down = sync(dn_left, dn_right, ff_l, ff_r, g_down)
        dn_l, dn_r = sync(*links.scatter_one(dn_left, dn_right))
        dn_lf, dn_rf = sync(*links.scatter_two(dn_left, dn_right, dn_l, dn_r))
        normed_two_grad = links.scatter_end(dn_left, dn_right, dn_l, dn_r, dn_lf, dn_rf)

        mid_upstream, midnorm_part = norm_backward(normed_two_grad, hidden_one, factor_mid, gain_mid)
        hidden_one_grad = down_in[:rows].astype(F32) + mid_upstream
        a_own = hidden_one_grad.astype(BF16)
        ax, ay = sync(*links.gather_one(a_own))
        dx, dy = sync(*links.gather_two(ax, ay))
        attn_in = jnp.concatenate([a_own, ax, ay, dx, dy], axis=0)
        attn_in, g_down = sync(attn_in, g_down)
        down_x = links.x(g_down)
        ff_lf, ff_rf = links.scatter_two(
            after(ff_left, attn_in), after(ff_right, attn_in), ff_l, ff_r
        )
        first = c_me == 0
        attn_own = jnp.where(first, attn_in[:, :half], attn_in[:, half:])
        attn_far = jnp.where(first, attn_in[:, half:], attn_in[:, :half])
        out_far = far_part(mixed, attn_far)
        dq0, dq1, dk, dv = attend_back(
            after(attn_in, out_far), w_o, q0, q1, keys, values, lse, at_q, at_k, cos_t, sin_t
        )
        g_out = both_cores(mixed, after(attn_own, dq0), links.c(out_far))
        grad_even = jnp.concatenate([dq0, dk], axis=1)
        grad_odd = jnp.concatenate([dq1, dv], axis=1)
        normed_part = (
            mm_nt(after(grad_even, g_out), w_attn[0, :, : 2 * HEAD_SIZE])
            + mm_nt(grad_odd, w_attn[1, :, : 2 * HEAD_SIZE])
        ).astype(BF16)
        o_parts = spread(lambda t: lax.dynamic_slice(g_out, (0, t * eighth), (2 * HEAD_SIZE, eighth)))
        normed_part, grad_even, grad_odd, ff_lf, ff_rf, down_x, *o_parts = sync(
            normed_part, grad_even, grad_odd, ff_lf, ff_rf, down_x, *o_parts
        )
        np_left, np_right = normed_part[:, :half], normed_part[:, half:]
        np_l, np_r = links.scatter_one(np_left, np_right)
        g_o_cols = jnp.zeros((8 * HEAD_SIZE, eighth), BF16)
        for p, part in enumerate(o_parts):
            g_o_cols = lax.dynamic_update_slice(
                g_o_cols, part, (jnp.bitwise_xor(head, p) * 2 * HEAD_SIZE, 0)
            )
        d_own = jnp.where(first, grad_even, grad_odd)
        d_far = jnp.where(first, grad_odd, grad_even)
        g_qkv = both_cores(normed, d_own, links.c(far_part(normed, d_far)))
        attn_sum = jnp.concatenate([g_qkv, g_o_cols], axis=1)
        g_attn = over_planes(attn_sum)
        np_l, np_r, attn_sum = sync(np_l, np_r, attn_sum)
        np_lf, np_rf = sync(*links.scatter_two(np_left, np_right, np_l, np_r))
        out_rows = (
            (hidden_one + links.scatter_end(ff_left, ff_right, ff_l, ff_r, ff_lf, ff_rf)) * valid
        ).astype(BF16)
        normed_grad = links.scatter_end(np_left, np_right, np_l, np_r, np_lf, np_rf)
        pre_upstream, prenorm_part = norm_backward(normed_grad, hidden_zero, factor_pre, gain_pre)
        token_rows = ((hidden_one_grad + pre_upstream) * valid).astype(BF16)
        norm_plane = links.sum_plane(jnp.stack([prenorm_part, midnorm_part]))
        token_send, norm_plane = sync(
            send_layout(jnp.concatenate([token_rows, out_rows], axis=0), 2), norm_plane
        )
        got = exchange(token_send)
        *ff_chips, g_attn = sync(*by_chip(after(g_ff, token_send)), g_attn)
        attn_chips = by_chip(g_attn)
        ff_parts = by_rank(ff_chips)
        down_gradient = place_rows(
            2 * x_me + c_me, [g_down, links.c(g_down), down_x, links.c(down_x)]
        )
        gate_gradient = place_columns(rank, ff_parts, planes, piece, 0)
        up_gradient = place_columns(rank, ff_parts, planes, piece, 1)
        *attn_chips, down_gradient, gate_gradient, up_gradient = sync(
            *attn_chips, down_gradient, gate_gradient, up_gradient
        )
        norm_parts = links.sum_planes(norm_plane)
        query_gradient, key_gradient, value_gradient, output_gradient = place_attention(
            rank, by_rank(attn_chips)
        )
        grad_tokens, out_tokens = take_blocks(seq_of, taken, got)
        norm_own = lax.dynamic_slice(
            norm_parts, (0, group_me * prenorm_gain.shape[0]), (2, prenorm_gain.shape[0])
        )
        return (
            out_tokens,
            grad_tokens,
            query_gradient,
            key_gradient,
            value_gradient,
            output_gradient,
            gate_gradient,
            up_gradient,
            down_gradient,
            norm_own[0],
            norm_own[1],
        )

    return body


def solution(mesh):
    planes = mesh.shape["fsdp"] // 2
    grid = Mesh(mesh.devices.reshape(planes, 2, 2, 2), AXES)
    rows = ("z", "y")
    stream = P(None, rows, ("x", "c"))
    weight = P(rows, None)
    gain = P(rows)
    return jax.shard_map(
        make_body(planes),
        mesh=grid,
        in_specs=(stream, stream) + (weight,) * 7 + (gain, gain, P(), P()),
        out_specs=(stream, stream) + (weight,) * 7 + (gain, gain),
        check_vma=False,
    )
```

```python
import math

import jax
import jax.numpy as jnp
from jax import lax
from jax.experimental import pallas as pl
from jax.experimental.pallas import tpu as pltpu
from jax.sharding import Mesh
from jax.sharding import PartitionSpec as P

QUERY_HEADS = 8
KEY_VALUE_HEADS = 4
HEAD_SIZE = 256

EPS_NORM = 1e-06
ROPE_BASE = 1000042.0
MASK_FILL = -1e30
AXES = ("z", "y", "x", "c")
F32 = jnp.float32
BF16 = jnp.bfloat16


def dot(a, b, dims):
    return lax.dot_general(a, b, (dims, ((), ())), preferred_element_type=F32)


def mm(a, b):
    return dot(a, b, ((1,), (0,)))


def mm_nt(a, b):
    return dot(a, b, ((1,), (1,)))


def mm_tn(a, b):
    return dot(a, b, ((0,), (0,)))


def sync(*values):
    return lax.optimization_barrier(values)


def after(value, *others):
    return lax.optimization_barrier((value,) + others)[0]


class Links:
    def __init__(self, planes):
        self.planes = planes

        def pairs(move):
            out = []
            for z in range(planes):
                for y in range(2):
                    for x in range(2):
                        for c in range(2):
                            a, b, d, e = move(z, y, x, c)
                            out.append((((z * 2 + y) * 2 + x) * 2 + c, ((a * 2 + b) * 2 + d) * 2 + e))
            return out

        self.px = pairs(lambda z, y, x, c: (z, y, 1 - x, c))
        self.py = pairs(lambda z, y, x, c: (z, 1 - y, x, c))
        self.pxy = pairs(lambda z, y, x, c: (z, 1 - y, 1 - x, c))
        self.pc = pairs(lambda z, y, x, c: (z, y, x, 1 - c))
        self.pz = [
            pairs(lambda z, y, x, c, k=k: ((z + k) % planes, y, x, c)) for k in range(planes)
        ]
        self.pz_swap = []
        k = 1
        while k < planes:
            self.pz_swap.append(pairs(lambda z, y, x, c, k=k: (z ^ k, y, x, c)))
            k *= 2

    def x(self, a):
        return lax.ppermute(a, AXES, self.px)

    def y(self, a):
        return lax.ppermute(a, AXES, self.py)

    def c(self, a):
        return lax.ppermute(a, AXES, self.pc)

    def swap_chips(self, chunks):
        return [
            chunks[0],
            self.x(chunks[1]),
            self.y(chunks[2]),
            lax.ppermute(chunks[3], AXES, self.pxy),
        ]

    def sum_plane(self, a):
        for p in (self.pc, self.px, self.py):
            a = a + lax.ppermute(a, AXES, p)
        return a

    def sum_planes(self, a):
        for p in self.pz_swap:
            a = a + lax.ppermute(a, AXES, p)
        return a

    def gather_one(self, a):
        return self.x(a), self.y(a)

    def gather_two(self, ax, ay):
        m = ax.shape[0] // 2
        return self.x(ay[:m]), self.y(ax[m:])

    def scatter_one(self, left, right):
        n = left.shape[0] // 4
        l4 = left.reshape(4, n, left.shape[1])
        return self.x(jnp.stack([l4[1], l4[3]])), self.y(right[2 * n :].reshape(2, n, right.shape[1]))

    def scatter_two(self, left, right, gl, gr):
        n = left.shape[0] // 4
        l_far = self.y((left[2 * n : 3 * n].astype(F32) + gl[1]).astype(BF16))
        r_far = self.x((right[n : 2 * n].astype(F32) + gr[1]).astype(BF16))
        return l_far, r_far

    def scatter_end(self, left, right, gl, gr, l_far, r_far):
        n = left.shape[0] // 4
        gl, gr, l_far, r_far = sync(gl, gr, l_far, r_far)
        l_own = left[:n].astype(F32) + gl[0] + l_far
        r_own = right[:n].astype(F32) + gr[0] + r_far
        return jnp.concatenate([l_own, r_own], axis=1)

    def gather_planes(self, a):
        got = lax.all_gather(a, ("c", "z"), axis=0, tiled=True)
        return got.reshape(2, self.planes * a.shape[0], a.shape[1])

    def gather_gains(self, a):
        n = a.shape[1]
        y_me = lax.axis_index("y")
        z_me = lax.axis_index("z")
        two = pair(y_me, a, self.y(a))
        out = jnp.zeros((self.planes,) + two.shape, a.dtype)
        for k in range(self.planes):
            part = two if k == 0 else lax.ppermute(two, AXES, self.pz[k])
            at = lax.rem(z_me - k + self.planes, self.planes)
            out = lax.dynamic_update_slice(out, part[None], (at, 0, 0, 0))
        return jnp.transpose(out, (2, 0, 1, 3)).reshape(2, 2 * self.planes * n)


def pair(bit, own, other):
    return jnp.stack([jnp.where(bit == 0, own, other), jnp.where(bit == 0, other, own)])


def estimate(flops, bytes_accessed, transcendentals):
    return pl.CostEstimate(
        flops=flops, bytes_accessed=bytes_accessed, transcendentals=transcendentals
    )


def rank_scalar(rank):
    return jnp.reshape(rank, (1,)).astype(jnp.int32)


def place_columns(rank, parts, planes, piece, side):
    n = parts[0].shape[0]
    width = planes * piece
    total = 8 * width
    if piece % 128:
        parts = [t[:, side * width : (side + 1) * width] for t in parts]
        out = jnp.zeros((n, planes, 8, piece), F32)
        for p, part in enumerate(parts):
            part = part.reshape(n, planes, 1, piece).astype(F32)
            out = lax.dynamic_update_slice(out, part, (0, 0, jnp.bitwise_xor(rank, p), 0))
        return out.reshape(n, total)
    tile = min(n, 128)

    def kernel(rank_ref, *refs):
        out = refs[8]
        for p in range(8):
            t = jnp.bitwise_xor(rank_ref[0], p)
            for z in range(planes):
                at = pl.multiple_of(z * 8 * piece + t * piece, 128)
                out[:, pl.ds(at, piece)] = refs[p][:, z * piece : (z + 1) * piece].astype(F32)

    return pl.pallas_call(
        kernel,
        out_shape=jax.ShapeDtypeStruct((n, total), F32),
        grid_spec=pltpu.PrefetchScalarGridSpec(
            num_scalar_prefetch=1,
            grid=(n // tile,),
            in_specs=[pl.BlockSpec((tile, width), lambda i, r: (i, side))] * 8,
            out_specs=pl.BlockSpec((tile, total), lambda i, r: (i, 0)),
        ),
        cost_estimate=estimate(flops=0, bytes_accessed=6 * n * total, transcendentals=0),
    )(rank_scalar(rank), *parts)


def place_rows(order, parts):
    n, d = parts[0].shape
    tile = min(n, 128)

    def kernel(order_ref, *refs):
        for p in range(4):
            refs[4][jnp.bitwise_xor(order_ref[0], p)] = refs[p][...].astype(F32)

    out = pl.pallas_call(
        kernel,
        out_shape=jax.ShapeDtypeStruct((4, n, d), F32),
        grid_spec=pltpu.PrefetchScalarGridSpec(
            num_scalar_prefetch=1,
            grid=(n // tile,),
            in_specs=[pl.BlockSpec((tile, d), lambda i, r: (i, 0))] * 4,
            out_specs=pl.BlockSpec((4, tile, d), lambda i, r: (0, i, 0)),
        ),
        cost_estimate=estimate(flops=0, bytes_accessed=24 * n * d, transcendentals=0),
    )(rank_scalar(order), *parts)
    return out.reshape(4 * n, d)


def place_attention(rank, parts):
    n, width = parts[0].shape
    h = HEAD_SIZE
    o = width - 2 * h
    tile = min(n, 128)

    def kernel(rank_ref, *refs):
        q_out, k_out, v_out, o_out = refs[8:]
        for p in range(8):
            t = jnp.bitwise_xor(rank_ref[0], p)
            j = t // 2
            core = t - 2 * j
            q_out[:, pl.ds(pl.multiple_of(t * h, 128), h)] = refs[p][:, :h].astype(F32)
            at = pl.ds(pl.multiple_of(j * h, 128), h)

            @pl.when(core == 0)
            def _():
                k_out[:, at] = refs[p][:, h : 2 * h].astype(F32)

            @pl.when(core == 1)
            def _():
                v_out[:, at] = refs[p][:, h : 2 * h].astype(F32)

            to = pl.multiple_of(core * 4 * o + j * o, 128)
            o_out[:, pl.ds(to, o)] = refs[p][:, 2 * h :].astype(F32)

    widths = (8 * h, 4 * h, 4 * h, 8 * o)
    return pl.pallas_call(
        kernel,
        out_shape=tuple(jax.ShapeDtypeStruct((n, w), F32) for w in widths),
        grid_spec=pltpu.PrefetchScalarGridSpec(
            num_scalar_prefetch=1,
            grid=(n // tile,),
            in_specs=[pl.BlockSpec((tile, width), lambda i, r: (i, 0))] * 8,
            out_specs=tuple(pl.BlockSpec((tile, w), lambda i, r: (i, 0)) for w in widths),
        ),
        cost_estimate=estimate(flops=0, bytes_accessed=48 * n * width, transcendentals=0),
    )(rank_scalar(rank), *parts)


def back_product(core, lefts, weight):
    m, k = lefts[0].shape
    n = weight.shape[1]
    tile = min(n // 2, 256)
    steps = n // 2 // tile

    def kernel(core_ref, a0, a1, l0, l1, r0, r1, left, right):
        left[...] = (mm_nt(a0[...], l0[...]) + mm_nt(a1[...], l1[...])).astype(BF16)
        right[...] = (mm_nt(a0[...], r0[...]) + mm_nt(a1[...], r1[...])).astype(BF16)

    whole = pl.BlockSpec((m, k), lambda i, r: (0, 0))
    out = pl.BlockSpec((m, tile), lambda i, r: (0, i))
    return pl.pallas_call(
        kernel,
        out_shape=(jax.ShapeDtypeStruct((m, n // 2), BF16),) * 2,
        grid_spec=pltpu.PrefetchScalarGridSpec(
            num_scalar_prefetch=1,
            grid=(steps,),
            in_specs=[
                whole,
                whole,
                pl.BlockSpec((None, tile, k), lambda i, r: (r[0], i, 0)),
                pl.BlockSpec((None, tile, k), lambda i, r: (1 - r[0], i, 0)),
                pl.BlockSpec((None, tile, k), lambda i, r: (r[0], i + steps, 0)),
                pl.BlockSpec((None, tile, k), lambda i, r: (1 - r[0], i + steps, 0)),
            ],
            out_specs=(out, out),
        ),
        cost_estimate=estimate(
            flops=4 * m * k * n, bytes_accessed=4 * (m + n) * k + 2 * m * n, transcendentals=0
        ),
    )(rank_scalar(core), *lefts, weight, weight, weight, weight)


def weight_product(left, right, other=None):
    m, k = left.shape
    n = right.shape[1]
    tile = 256

    def kernel(a, b, *refs):
        total = mm(a[...], b[...])
        if other is not None:
            total = total + refs[0][...]
        refs[-1][...] = total.astype(BF16)

    out = pl.BlockSpec((m, tile), lambda i: (0, i))
    more = () if other is None else (other,)
    return pl.pallas_call(
        kernel,
        out_shape=jax.ShapeDtypeStruct((m, n), BF16),
        grid=(n // tile,),
        in_specs=[
            pl.BlockSpec((m, k), lambda i: (0, 0)),
            pl.BlockSpec((k, tile), lambda i: (0, i)),
        ]
        + [out] * len(more),
        out_specs=out,
        cost_estimate=estimate(
            flops=2 * m * k * n,
            bytes_accessed=2 * (m * k + k * n + (1 + len(more)) * m * n),
            transcendentals=0,
        ),
    )(left, right, *more)


def ff_front(half, n2, weight):
    m, d = n2.shape
    f = weight.shape[2] // 2
    tile = 256
    steps = f // tile

    def kernel(half_ref, x, wg, wu, gate_out, up_out, act_out):
        gate = mm(x[...], wg[...])
        up = mm(x[...], wu[...])
        gate_out[...] = gate
        up_out[...] = up
        act_out[...] = (gate * jax.nn.sigmoid(gate) * up).astype(BF16)

    out = pl.BlockSpec((m, tile), lambda i, r: (0, i))
    return pl.pallas_call(
        kernel,
        out_shape=(
            jax.ShapeDtypeStruct((m, f), F32),
            jax.ShapeDtypeStruct((m, f), F32),
            jax.ShapeDtypeStruct((m, f), BF16),
        ),
        grid_spec=pltpu.PrefetchScalarGridSpec(
            num_scalar_prefetch=1,
            grid=(steps,),
            in_specs=[
                pl.BlockSpec((m, d), lambda i, r: (0, 0)),
                pl.BlockSpec((None, d, tile), lambda i, r: (r[0], 0, i)),
                pl.BlockSpec((None, d, tile), lambda i, r: (r[0], 0, i + steps)),
            ],
            out_specs=(out, out, out),
        ),
        cost_estimate=estimate(
            flops=4 * m * d * f, bytes_accessed=2 * m * d + 4 * d * f + 10 * m * f, transcendentals=m * f
        ),
    )(rank_scalar(half), n2, weight, weight)


def ff_back(half, d_in, weight, gate_pre, up_pre):
    m, d = d_in.shape
    f = weight.shape[1]
    tile = 256
    steps = f // tile

    def kernel(half_ref, g, w, gate_ref, up_ref, out, kept):
        i = pl.program_id(0)

        @pl.when(i < steps)
        def _():
            act_grad = mm_nt(g[...], w[...])
            gate = gate_ref[...]
            sig = jax.nn.sigmoid(gate)
            out[...] = (act_grad * up_ref[...] * sig * (1.0 + gate * (1.0 - sig))).astype(BF16)
            kept[i] = (act_grad * (gate * sig)).astype(BF16)

        @pl.when(i >= steps)
        def _():
            out[...] = kept[i - steps]

    last = steps - 1
    pre = pl.BlockSpec((m, tile), lambda i, r: (0, jnp.minimum(i, last)))
    return pl.pallas_call(
        kernel,
        out_shape=jax.ShapeDtypeStruct((m, 2 * f), BF16),
        grid_spec=pltpu.PrefetchScalarGridSpec(
            num_scalar_prefetch=1,
            grid=(2 * steps,),
            in_specs=[
                pl.BlockSpec((m, d), lambda i, r: (0, 0)),
                pl.BlockSpec((None, tile, d), lambda i, r: (r[0], jnp.minimum(i, last), 0)),
                pre,
                pre,
            ],
            out_specs=pl.BlockSpec((m, tile), lambda i, r: (0, i)),
            scratch_shapes=[pltpu.VMEM((steps, m, tile), BF16)],
        ),
        cost_estimate=estimate(
            flops=2 * m * d * f, bytes_accessed=2 * (m + f) * d + 12 * m * f, transcendentals=m * f
        ),
    )(rank_scalar(half), d_in, weight, gate_pre, up_pre)


def forward_product(core, lefts, weight):
    m, k = lefts[0].shape
    n = weight.shape[2]
    tile = 256
    steps = n // 2 // tile

    def kernel(core_ref, a0, a1, l0, l1, r0, r1, left, right):
        left[...] = (mm(a0[...], l0[...]) + mm(a1[...], l1[...])).astype(BF16)
        right[...] = (mm(a0[...], r0[...]) + mm(a1[...], r1[...])).astype(BF16)

    whole = pl.BlockSpec((m, k), lambda i, r: (0, 0))
    out = pl.BlockSpec((m, tile), lambda i, r: (0, i))
    return pl.pallas_call(
        kernel,
        out_shape=(jax.ShapeDtypeStruct((m, n // 2), BF16),) * 2,
        grid_spec=pltpu.PrefetchScalarGridSpec(
            num_scalar_prefetch=1,
            grid=(steps,),
            in_specs=[
                whole,
                whole,
                pl.BlockSpec((None, k, tile), lambda i, r: (r[0], 0, i)),
                pl.BlockSpec((None, k, tile), lambda i, r: (1 - r[0], 0, i)),
                pl.BlockSpec((None, k, tile), lambda i, r: (r[0], 0, i + steps)),
                pl.BlockSpec((None, k, tile), lambda i, r: (1 - r[0], 0, i + steps)),
            ],
            out_specs=(out, out),
        ),
        cost_estimate=estimate(
            flops=4 * m * k * n, bytes_accessed=4 * (m + n) * k + 2 * m * n, transcendentals=0
        ),
    )(rank_scalar(core), *lefts, weight, weight, weight, weight)


def send_blocks(slot, has, stream):
    groups = slot.shape[0]
    _, r, f = stream.shape
    count = 8

    def kernel(slot_ref, has_ref, *refs):
        for i in range(count):
            v = refs[i][0]
            keep = has_ref[pl.program_id(0) * count + i] > 0
            refs[count][i] = jnp.where(keep, v, jnp.zeros_like(v))

    return pl.pallas_call(
        kernel,
        out_shape=jax.ShapeDtypeStruct((groups, r, f), BF16),
        grid_spec=pltpu.PrefetchScalarGridSpec(
            num_scalar_prefetch=2,
            grid=(groups // count,),
            in_specs=[
                pl.BlockSpec((1, r, f), lambda g, s, h, i=i: (s[g * count + i], 0, 0))
                for i in range(count)
            ],
            out_specs=pl.BlockSpec((count, r, f), lambda g, s, h: (g, 0, 0)),
        ),
        cost_estimate=estimate(flops=0, bytes_accessed=4 * groups * r * f, transcendentals=0),
    )(slot, has, *[stream] * count)


def take_blocks(slot, has, got):
    slots = slot.shape[0]
    _, _, r, f = got.shape

    def kernel(slot_ref, has_ref, *refs):
        for i in range(slots):
            keep = has_ref[i] > 0
            for k in range(2):
                v = refs[i][0, k]
                refs[slots + k][i] = jnp.where(keep, v, jnp.zeros_like(v))

    out = pl.BlockSpec((slots, r, f), lambda g, s, h: (0, 0, 0))
    return pl.pallas_call(
        kernel,
        out_shape=(jax.ShapeDtypeStruct((slots, r, f), BF16),) * 2,
        grid_spec=pltpu.PrefetchScalarGridSpec(
            num_scalar_prefetch=2,
            grid=(1,),
            in_specs=[
                pl.BlockSpec((1, 2, r, f), lambda g, s, h, i=i: (s[i], 0, 0, 0))
                for i in range(slots)
            ],
            out_specs=(out, out),
        ),
        cost_estimate=estimate(flops=0, bytes_accessed=8 * slots * r * f, transcendentals=0),
    )(slot, has, *[got] * slots)


def assemble_rows(info, pieces, gain=None):
    _, _, r, f = pieces[0].shape
    width = 4 * f

    def block(i, n):
        return 2 * jnp.bitwise_xor(n[0], (i // 2) % 2) + i % 2

    def kernel(info_ref, *refs):
        own, ax, ay, dx, dy = refs[:5]
        i = pl.program_id(0)
        x = info_ref[0]
        near = i < 4
        low = block(i, info_ref) < 2
        same = jnp.where(near, own[0], ay[0])
        other = jnp.where(near, ax[0], jnp.where(low, dx[0], dy[0]))
        at = info_ref[2 + i] * r + lax.broadcasted_iota(jnp.int32, (r, f), 0)
        inside = at < info_ref[1]
        parts = []
        for h, v in ((x, same), (1 - x, other)):
            for c in range(2):
                t = jnp.where(inside, v[c].astype(F32), 0.0)
                parts.append((2 * h + c, t))
        if gain is None:
            for q, t in parts:
                refs[5][:, pl.ds(pl.multiple_of(q * f, 128), f)] = t.astype(BF16)
            return
        gain_ref, normed, rows = refs[5:]
        total = sum(jnp.sum(t * t, axis=1, keepdims=True) for _, t in parts)
        factor = lax.rsqrt(total * (1.0 / width) + EPS_NORM)
        for q, t in parts:
            g = gain_ref[pl.ds(q, 1), :]
            normed[:, pl.ds(pl.multiple_of(q * f, 128), f)] = (t * factor * g).astype(BF16)

        @pl.when(i < 2)
        def _():
            for q, t in parts:
                rows[:, pl.ds(pl.multiple_of(q * f, 128), f)] = t.astype(BF16)

    whole = pl.BlockSpec((1, 2, r, f), lambda i, n: (block(i, n), 0, 0, 0))
    specs = [
        whole,
        whole,
        whole,
        pl.BlockSpec((1, 2, r, f), lambda i, n: (jnp.minimum(block(i, n), 1), 0, 0, 0)),
        pl.BlockSpec((1, 2, r, f), lambda i, n: (jnp.maximum(block(i, n) - 2, 0), 0, 0, 0)),
    ]
    shape = [jax.ShapeDtypeStruct((8 * r, width), BF16)]
    outs = [pl.BlockSpec((r, width), lambda i, n: (i, 0))]
    args = list(pieces)
    if gain is not None:
        specs.append(pl.BlockSpec((4, f), lambda i, n: (0, 0)))
        args.append(gain)
        shape.append(jax.ShapeDtypeStruct((2 * r, width), BF16))
        outs.append(pl.BlockSpec((r, width), lambda i, n: (jnp.minimum(i, 1), 0)))
    got = pl.pallas_call(
        kernel,
        out_shape=tuple(shape),
        grid_spec=pltpu.PrefetchScalarGridSpec(
            num_scalar_prefetch=1, grid=(8,), in_specs=specs, out_specs=tuple(outs)
        ),
        cost_estimate=estimate(
            flops=16 * r * width, bytes_accessed=40 * r * width, transcendentals=0
        ),
    )(info, *args)
    return got[0] if gain is None else got


def turn(v, cos_t, sin_t, sign):
    h = v.shape[-1] // 2
    a, b = v[:, :h], v[:, h:]
    s = sin_t * sign
    return jnp.concatenate([a * cos_t - b * s, b * cos_t + a * s], axis=-1).astype(BF16)


def project(normed, w_attn, cos_t, sin_t):
    rows, width = normed.shape
    h = HEAD_SIZE
    tile = 256

    def kernel(x_ref, w_ref, c_ref, s_ref, q0, q1, k, v):
        even = mm(x_ref[...], w_ref[0])
        odd = mm(x_ref[...], w_ref[1])
        cos_t, sin_t = c_ref[...], s_ref[...]
        q0[...] = turn(even[:, :h], cos_t, sin_t, 1.0)
        k[...] = turn(even[:, h:], cos_t, sin_t, 1.0)
        q1[...] = turn(odd[:, :h], cos_t, sin_t, 1.0)
        v[...] = odd[:, h:].astype(BF16)

    out = pl.BlockSpec((tile, h), lambda i: (i, 0))
    table = pl.BlockSpec((tile, h // 2), lambda i: (i, 0))
    return pl.pallas_call(
        kernel,
        out_shape=(jax.ShapeDtypeStruct((rows, h), BF16),) * 4,
        grid=(rows // tile,),
        in_specs=[
            pl.BlockSpec((tile, width), lambda i: (i, 0)),
            pl.BlockSpec((2, width, 2 * h), lambda i: (0, 0, 0)),
            table,
            table,
        ],
        out_specs=(out,) * 4,
        cost_estimate=estimate(
            flops=8 * rows * width * h, bytes_accessed=2 * rows * width + 8 * width * h, transcendentals=0
        ),
    )(normed, w_attn, cos_t, sin_t)


def attend(q0, q1, keys, values, w_o, at_q, at_k):
    rows, h = q0.shape
    half = w_o.shape[2]
    tile = 256
    factor = 1.0 / math.sqrt(HEAD_SIZE)

    def kernel(q0_ref, q1_ref, k_ref, v_ref, w_ref, aq_ref, ak_ref, mixed, lse, left, right):
        allowed = ak_ref[...] <= aq_ref[...]
        for i, q_ref in enumerate((q0_ref, q1_ref)):
            scores = jnp.where(allowed, mm_nt(q_ref[...], k_ref[...]) * factor, MASK_FILL)
            top = jnp.max(scores, axis=-1, keepdims=True)
            e = jnp.exp(scores - top)
            total = jnp.sum(e, axis=-1, keepdims=True)
            probs = (e * (1.0 / total)).astype(BF16)
            mixed[:, i * h : (i + 1) * h] = mm(probs, v_ref[...]).astype(BF16)
            lse[i] = top + jnp.log(total)
        left[...] = mm(mixed[...], w_ref[0]).astype(BF16)
        right[...] = mm(mixed[...], w_ref[1]).astype(BF16)

    q_spec = pl.BlockSpec((tile, h), lambda i: (i, 0))
    kv_spec = pl.BlockSpec((rows, h), lambda i: (0, 0))
    out_spec = pl.BlockSpec((tile, half), lambda i: (i, 0))
    return pl.pallas_call(
        kernel,
        out_shape=(
            jax.ShapeDtypeStruct((rows, 2 * h), BF16),
            jax.ShapeDtypeStruct((2, rows, 1), F32),
            jax.ShapeDtypeStruct((rows, half), BF16),
            jax.ShapeDtypeStruct((rows, half), BF16),
        ),
        grid=(rows // tile,),
        in_specs=[
            q_spec,
            q_spec,
            kv_spec,
            kv_spec,
            pl.BlockSpec((2, 2 * h, half), lambda i: (0, 0, 0)),
            pl.BlockSpec((tile, 1), lambda i: (i, 0)),
            pl.BlockSpec((1, rows), lambda i: (0, 0)),
        ],
        out_specs=(
            pl.BlockSpec((tile, 2 * h), lambda i: (i, 0)),
            pl.BlockSpec((2, tile, 1), lambda i: (0, i, 0)),
            out_spec,
            out_spec,
        ),
        cost_estimate=estimate(
            flops=8 * rows * rows * h + 8 * rows * h * half,
            bytes_accessed=12 * rows * h + 8 * h * half + 4 * rows * half,
            transcendentals=2 * rows * rows,
        ),
    )(q0, q1, keys, values, w_o, at_q, at_k)


def attend_back(attn_in, w_o, q0, q1, keys, values, lse, at_q, at_k, cos_t, sin_t):
    rows, h = q0.shape
    half = w_o.shape[2]
    tile = 256
    steps = rows // tile
    factor = 1.0 / math.sqrt(HEAD_SIZE)

    def kernel(
        g_ref, w_ref, q0_ref, q1_ref, k_ref, v_ref, lse_ref, aq_ref, ak_ref, c_ref, s_ref, ca_ref,
        sa_ref, dq0, dq1, dk, dv, k_sum, v_sum,
    ):
        step = pl.program_id(0)

        @pl.when(step == 0)
        def _():
            k_sum[...] = jnp.zeros_like(k_sum)
            v_sum[...] = jnp.zeros_like(v_sum)

        g = g_ref[...]
        dmix = (mm_nt(g[:, :half], w_ref[0]) + mm_nt(g[:, half:], w_ref[1])).astype(BF16)
        allowed = ak_ref[...] <= aq_ref[...]
        for i, (q_ref, dq) in enumerate(((q0_ref, dq0), (q1_ref, dq1))):
            d = dmix[:, i * h : (i + 1) * h]
            scores = jnp.where(allowed, mm_nt(q_ref[...], k_ref[...]) * factor, MASK_FILL)
            probs = jnp.exp(scores - lse_ref[i])
            v_sum[...] += mm_tn(probs.astype(BF16), d)
            prob_grad = mm_nt(d, v_ref[...])
            inner = jnp.sum(prob_grad * probs, axis=-1, keepdims=True)
            score_grad = (probs * (prob_grad - inner)).astype(BF16)
            k_sum[...] += mm_tn(score_grad, q_ref[...])
            rot = (mm(score_grad, k_ref[...]) * factor).astype(BF16).astype(F32)
            dq[...] = turn(rot, c_ref[...], s_ref[...], -1.0)

        @pl.when(step == steps - 1)
        def _():
            rot = (k_sum[...] * factor).astype(BF16).astype(F32)
            dk[...] = turn(rot, ca_ref[...], sa_ref[...], -1.0)
            dv[...] = v_sum[...].astype(BF16)

    q_spec = pl.BlockSpec((tile, h), lambda i: (i, 0))
    kv_spec = pl.BlockSpec((rows, h), lambda i: (0, 0))
    table = pl.BlockSpec((tile, h // 2), lambda i: (i, 0))
    all_table = pl.BlockSpec((rows, h // 2), lambda i: (0, 0))
    return pl.pallas_call(
        kernel,
        out_shape=(jax.ShapeDtypeStruct((rows, h), BF16),) * 4,
        grid=(steps,),
        in_specs=[
            pl.BlockSpec((tile, 2 * half), lambda i: (i, 0)),
            pl.BlockSpec((2, 2 * h, half), lambda i: (0, 0, 0)),
            q_spec,
            q_spec,
            kv_spec,
            kv_spec,
            pl.BlockSpec((2, tile, 1), lambda i: (0, i, 0)),
            pl.BlockSpec((tile, 1), lambda i: (i, 0)),
            pl.BlockSpec((1, rows), lambda i: (0, 0)),
            table,
            table,
            all_table,
            all_table,
        ],
        out_specs=(q_spec, q_spec, kv_spec, kv_spec),
        scratch_shapes=[pltpu.VMEM((rows, h), F32), pltpu.VMEM((rows, h), F32)],
        cost_estimate=estimate(
            flops=20 * rows * rows * h + 8 * rows * h * half,
            bytes_accessed=20 * rows * h + 8 * h * half + 4 * rows * half,
            transcendentals=2 * rows * rows,
        ),
    )(attn_in, w_o, q0, q1, keys, values, lse, at_q, at_k, cos_t, sin_t, cos_t, sin_t)


def rope_tables(positions):
    half_dim = HEAD_SIZE // 2
    frequency = jnp.exp(jnp.arange(half_dim, dtype=F32) * (-2.0 * math.log(ROPE_BASE) / HEAD_SIZE))
    angles = positions.astype(F32)[:, None] * frequency[None, :]
    return jnp.cos(angles), jnp.sin(angles)


def norm_factor(hidden):
    return lax.rsqrt(jnp.mean(hidden * hidden, axis=-1, keepdims=True) + EPS_NORM)


def norm_backward(upstream, hidden, factor, gain_vec):
    scaled = upstream * gain_vec
    gain_part = jnp.sum(upstream * hidden * factor, axis=0)
    inner_sum = jnp.mean(scaled * hidden, axis=-1, keepdims=True)
    return (factor * scaled - hidden * (factor * factor * factor) * inner_sum, gain_part)


def make_body(planes):
    links = Links(planes)

    def body(
        tokens,
        cotangent,
        query_weight,
        key_matrix,
        value_matrix,
        output_weight,
        gate_weight,
        up_weight,
        down_weight,
        prenorm_gain,
        midnorm_gain,
        seq_len,
        stream_order,
    ):
        groups = 2 * planes
        z_me = lax.axis_index("z")
        y_me = lax.axis_index("y")
        x_me = lax.axis_index("x")
        c_me = lax.axis_index("c")
        slots, blk, quarter = tokens.shape
        width = 4 * quarter
        rank = 4 * y_me + 2 * x_me + c_me
        head = 2 * y_me + x_me
        shard = query_weight.shape[0]
        ff = gate_weight.shape[1]
        piece = ff // groups // 4

        nblk = (seq_len + blk - 1) // blk
        member = (stream_order[:, None] == jnp.arange(groups, dtype=jnp.int32)[None, :]).astype(
            jnp.int32
        )
        ordered = jnp.sum(member * nblk[None, :], axis=1)
        firsts = jnp.cumsum(ordered) - ordered
        seq_start = jnp.sum(member * firsts[:, None], axis=0)
        group_me = 2 * z_me + y_me
        offset = lax.rem(group_me - lax.rem(seq_start, groups) + groups, groups)
        has = offset < nblk
        slot_of = jnp.where(has, (seq_start + offset) // groups, 0)
        block_ids = jnp.arange(slots, dtype=jnp.int32) * groups + group_me
        ahead = block_ids[:, None] - seq_start[None, :]
        covers = ((ahead >= 0) & (ahead < nblk[None, :])).astype(jnp.int32)
        seq_of = jnp.sum(covers * jnp.arange(groups, dtype=jnp.int32)[None, :], axis=1)
        taken = jnp.sum(covers, axis=1)

        mine = 2 * z_me + c_me
        picked = jnp.arange(groups, dtype=jnp.int32) == mine
        my_start = jnp.sum(jnp.where(picked, seq_start, 0))
        my_len = jnp.sum(jnp.where(picked, seq_len, 0))

        def block_places(y):
            first = lax.rem(y + my_start, 2)
            plane = lax.rem((my_start + first) // 2, planes)
            k = jnp.arange(4, dtype=jnp.int32)
            if planes == 4:
                k = lax.rem(k - plane + planes, planes)
            return first + 2 * k, plane

        places_own, plane_own = block_places(y_me)
        places_far, _ = block_places(1 - y_me)

        def two_places(places, x):
            return lax.dynamic_slice(places, (2 * x,), (2,))

        places = jnp.concatenate(
            [
                two_places(places_own, x_me),
                two_places(places_own, 1 - x_me),
                two_places(places_far, x_me),
                two_places(places_far, 1 - x_me),
            ]
        )
        info = jnp.concatenate([jnp.stack([x_me, my_len]), places]).astype(jnp.int32)
        positions = (places[:, None] * blk + jnp.arange(blk, dtype=jnp.int32)[None, :]).reshape(-1)
        at_q = positions[:, None]
        at_k = jnp.where(positions < my_len, positions, 1 << 30)[None, :]
        rows = 2 * blk
        valid = (positions[:rows] < my_len).astype(F32)[:, None]

        def send_layout(out_rows):
            left, right = out_rows[:, : 2 * quarter], out_rows[:, 2 * quarter :]
            keep = jnp.where(x_me == 0, left, right)
            got = links.x(jnp.where(x_me == 0, right, left))
            send = pair(x_me, keep, got).reshape(4, blk, 2, quarter)
            send = jnp.transpose(send, (0, 2, 1, 3))
            if planes > 4:
                send = jnp.pad(send, ((0, planes - 4), (0, 0), (0, 0), (0, 0)))
                send = jnp.roll(send, plane_own, axis=0)
            return send.reshape(groups, blk, quarter)

        def own_and_other(g):
            n = g.shape[1]
            own = lax.dynamic_slice(g, (y_me * shard, 0), (shard, n))
            other = lax.dynamic_slice(g, ((1 - y_me) * shard, 0), (shard, n))
            return own, other

        def after_both(two, later):
            return sync(*two, later)[:2]

        def by_chip(own, other):
            return links.swap_chips([own, own, other, other])

        def by_rank(chips):
            return [links.c(chips[p // 2]) if p % 2 else chips[p // 2] for p in range(8)]

        def plane_rows(own_part, far_part):
            got = links.y(far_part)
            both = pair(y_me, own_part, got)
            return both.reshape(2 * own_part.shape[0], own_part.shape[1])

        def ff_columns(w, r):
            return jnp.concatenate(
                [
                    lax.dynamic_slice(w, (0, p * 8 * piece + r * piece), (shard, piece))
                    for p in range(planes)
                ],
                axis=1,
            )

        far = rank + 4 - 8 * y_me
        def attn_columns(r, ws):
            q = lax.dynamic_slice(ws[0], (0, r * HEAD_SIZE), (shard, HEAD_SIZE))
            j = r // 2
            k = lax.dynamic_slice(ws[1], (0, j * HEAD_SIZE), (shard, HEAD_SIZE))
            v = lax.dynamic_slice(ws[2], (0, j * HEAD_SIZE), (shard, HEAD_SIZE))
            at = lax.rem(r, 2) * (width // 2) + (r // 2) * (width // 8)
            o = lax.dynamic_slice(ws[3], (0, at), (shard, width // 8))
            return jnp.concatenate([q, jnp.where(c_me == 0, k, v), o], axis=1)

        gains = links.gather_gains(jnp.stack([prenorm_gain, midnorm_gain])).astype(F32)

        def to_sequences(stream):
            return send_blocks(slot_of, has.astype(jnp.int32), stream)

        def arranged(got):
            got = got.reshape(planes, 2, blk, quarter)
            if planes > 4:
                got = jnp.roll(got, -plane_own, axis=0)[:4]
            return got

        def exchange(send):
            return lax.all_to_all(send, ("z", "c"), split_axis=0, concat_axis=0, tiled=True)

        send_tokens = to_sequences(tokens)
        got_tokens = exchange(send_tokens)
        *attn_ws, gate_weight, up_weight, down_weight, _ = sync(
            query_weight,
            key_matrix,
            value_matrix,
            output_weight,
            gate_weight,
            up_weight,
            down_weight,
            send_tokens,
        )
        attn_share = plane_rows(attn_columns(rank, attn_ws), attn_columns(far, attn_ws))

        def ff_share(r):
            return jnp.concatenate([ff_columns(gate_weight, r), ff_columns(up_weight, r)], axis=1)

        ff_own, ff_far_rows = ff_share(rank), ff_share(far)
        down_share = lax.dynamic_slice(
            down_weight, ((2 * x_me + c_me) * piece, 0), (piece, width)
        )
        got_tokens, attn_share, ff_own, ff_far_rows, down_share, gains = sync(
            got_tokens, attn_share, ff_own, ff_far_rows, down_share, gains
        )
        w_attn = links.gather_planes(attn_share)
        own = arranged(got_tokens)
        ax, ay = sync(*links.gather_one(own))
        ff_two = plane_rows(ff_own, after(ff_far_rows, own))
        gain_pre, gain_mid = gains[0], gains[1]
        eighth = width // 8

        def spread(chunk_of):
            return links.swap_chips([chunk_of(jnp.bitwise_xor(head, p)) for p in range(4)])

        cos_t, sin_t = rope_tables(positions)
        dx, dy, cos_t, sin_t, ff_two = sync(*links.gather_two(ax, ay), cos_t, sin_t, ff_two)
        w_ff = links.gather_planes(ff_two)
        w_down = links.gather_planes(after(down_share, ff_two))
        normed, rows_in = assemble_rows(info, (own, ax, ay, dx, dy), gain_pre.reshape(4, quarter))
        send_cot = to_sequences(after(cotangent, dx))
        w_attn, normed, send_cot = sync(w_attn, normed, send_cot)
        got_cot = exchange(send_cot)
        w_o_cols = lax.dynamic_index_in_dim(w_attn, c_me, 0, keepdims=False)[:, 2 * HEAD_SIZE :]
        w_o = jnp.zeros((2 * HEAD_SIZE, 4 * eighth), BF16)
        for p, part in enumerate(
            spread(
                lambda t: lax.dynamic_slice(
                    w_o_cols, (t * 2 * HEAD_SIZE, 0), (2 * HEAD_SIZE, eighth)
                )
            )
        ):
            w_o = lax.dynamic_update_slice(w_o, part, (0, jnp.bitwise_xor(head, p) * eighth))
        w_o = pair(c_me, w_o, links.c(w_o))

        q0, q1, keys, values = project(normed, w_attn, cos_t, sin_t)
        mixed, lse, attn_left, attn_right = attend(q0, q1, keys, values, w_o, at_q, at_k)
        hidden_zero = rows_in.astype(F32)
        factor_pre = norm_factor(hidden_zero)
        gl, gr = sync(*links.scatter_one(attn_left, attn_right))
        l_far, r_far = sync(*links.scatter_two(attn_left, attn_right, gl, gr))
        hidden_one = hidden_zero + links.scatter_end(attn_left, attn_right, gl, gr, l_far, r_far)
        factor_mid = norm_factor(hidden_one)
        n_own = (hidden_one * factor_mid * gain_mid).astype(BF16)
        ax, ay, got_cot = sync(*links.gather_one(n_own), got_cot)
        dx, dy = sync(*links.gather_two(ax, ay))
        normed_two = jnp.concatenate([n_own, ax, ay, dx, dy], axis=0)
        own = after(arranged(got_cot), normed_two)
        n_ff = w_ff.shape[2] // 2
        far_gate, far_up, act_far = ff_front(1 - c_me, normed_two, w_ff)
        ax, ay, act_far = sync(*links.gather_one(own), act_far)
        own_gate, own_up, act_own = ff_front(c_me, after(normed_two, ax), w_ff)
        turned = sync(jnp.transpose(after(normed_two, act_own)))[0]
        dx, dy, act_own, turned = sync(*links.gather_two(ax, ay), act_own, turned)
        down_in = assemble_rows(info, (own, ax, ay, dx, dy))

        def far_part(left, right):
            return mm_tn(left, right).astype(BF16)

        def both_cores(left, right, got):
            return (mm_tn(left, right) + got).astype(BF16)

        def over_planes(g):
            return lax.psum_scatter(g, "z", scatter_dimension=0, tiled=True)

        half = width // 2
        down_far = far_part(act_far, down_in)
        sum_down = both_cores(act_own, down_in, links.c(down_far))
        g_down = over_planes(sum_down)
        w_down, d_in = sync(w_down, down_in, sum_down)[:2]
        ff_left, ff_right = forward_product(c_me, (act_own, act_far), w_down)
        ff_left, ff_right, d_in = sync(ff_left, ff_right, d_in)
        ff_l, ff_r = links.scatter_one(ff_left, ff_right)
        in_far = ff_back(1 - c_me, d_in, w_down, far_gate, far_up)
        ff_far = weight_product(turned, in_far)
        ff_l, ff_r, ff_far, in_far = sync(ff_l, ff_r, ff_far, in_far)
        ff_lf, ff_rf = links.scatter_two(ff_left, ff_right, ff_l, ff_r)
        in_own = ff_back(c_me, after(d_in, ff_far), w_down, own_gate, own_up)
        dn_left, dn_right = back_product(c_me, (in_own, in_far), w_ff)
        dn_left, dn_right, in_own, ff_lf, ff_rf, ff_got = sync(
            dn_left, dn_right, in_own, ff_lf, ff_rf, links.c(ff_far)
        )
        dn_l, dn_r = links.scatter_one(dn_left, dn_right)
        sum_ff = weight_product(turned, in_own, ff_got)
        dn_l, dn_r, sum_ff = sync(dn_l, dn_r, sum_ff)
        g_ff = over_planes(sum_ff)
        dn_lf, dn_rf = links.scatter_two(dn_left, dn_right, dn_l, dn_r)
        out_rows = (
            (hidden_one + links.scatter_end(ff_left, ff_right, ff_l, ff_r, ff_lf, ff_rf)) * valid
        ).astype(BF16)
        dn_lf, dn_rf, g_down, out_rows = sync(dn_lf, dn_rf, g_down, out_rows)
        normed_two_grad = links.scatter_end(dn_left, dn_right, dn_l, dn_r, dn_lf, dn_rf)

        mid_upstream, midnorm_part = norm_backward(normed_two_grad, hidden_one, factor_mid, gain_mid)
        hidden_one_grad = down_in[:rows].astype(F32) + mid_upstream
        a_own = hidden_one_grad.astype(BF16)
        ax, ay = sync(*links.gather_one(a_own))
        dx, dy = sync(*links.gather_two(ax, ay))
        attn_in = jnp.concatenate([a_own, ax, ay, dx, dy], axis=0)
        attn_in, g_down, out_rows = sync(attn_in, g_down, out_rows)
        out_send = send_layout(out_rows)
        down_x = links.x(g_down)
        first = c_me == 0
        g_both = mm_tn(mixed, attn_in)
        g_low, g_high = g_both[:, :half], g_both[:, half:]
        out_far = jnp.where(first, g_high, g_low).astype(BF16)
        out_own = jnp.where(first, g_low, g_high)
        dq0, dq1, dk, dv = attend_back(
            after(attn_in, out_far), w_o, q0, q1, keys, values, lse, at_q, at_k, cos_t, sin_t
        )
        g_out = (out_own + links.c(out_far)).astype(BF16)
        grad_even = jnp.concatenate([dq0, dk], axis=1)
        grad_odd = jnp.concatenate([dq1, dv], axis=1)
        normed_part = (
            mm_nt(after(grad_even, g_out), w_attn[0, :, : 2 * HEAD_SIZE])
            + mm_nt(grad_odd, w_attn[1, :, : 2 * HEAD_SIZE])
        ).astype(BF16)
        o_parts = spread(lambda t: lax.dynamic_slice(g_out, (0, t * eighth), (2 * HEAD_SIZE, eighth)))
        normed_part, grad_even, grad_odd, out_send, down_x, *o_parts = sync(
            normed_part, grad_even, grad_odd, out_send, down_x, *o_parts
        )
        np_left, np_right = normed_part[:, :half], normed_part[:, half:]
        np_l, np_r = links.scatter_one(np_left, np_right)
        g_o_cols = jnp.zeros((8 * HEAD_SIZE, eighth), BF16)
        for p, part in enumerate(o_parts):
            g_o_cols = lax.dynamic_update_slice(
                g_o_cols, part, (jnp.bitwise_xor(head, p) * 2 * HEAD_SIZE, 0)
            )
        d_own = jnp.where(first, grad_even, grad_odd)
        d_far = jnp.where(first, grad_odd, grad_even)
        g_qkv = both_cores(normed, d_own, links.c(far_part(normed, d_far)))
        attn_sum = jnp.concatenate([g_qkv, g_o_cols], axis=1)
        np_l, np_r, attn_sum = sync(np_l, np_r, attn_sum)
        g_attn = over_planes(attn_sum)
        np_lf, np_rf = sync(*links.scatter_two(np_left, np_right, np_l, np_r))
        ff_rows = own_and_other(after(g_ff, np_l))
        normed_grad = links.scatter_end(np_left, np_right, np_l, np_r, np_lf, np_rf)
        pre_upstream, prenorm_part = norm_backward(normed_grad, hidden_zero, factor_pre, gain_pre)
        token_rows = ((hidden_one_grad + pre_upstream) * valid).astype(BF16)
        norm_plane = links.sum_plane(jnp.stack([prenorm_part, midnorm_part]))
        token_send, norm_plane, *ff_rows = sync(send_layout(token_rows), norm_plane, *ff_rows)
        got = exchange(jnp.stack([token_send, out_send], axis=1))
        *ff_chips, g_attn = sync(*by_chip(*after_both(ff_rows, token_send)), g_attn)
        attn_chips = by_chip(*own_and_other(g_attn))
        ff_parts = by_rank(ff_chips)
        down_gradient = place_rows(
            2 * x_me + c_me, [g_down, links.c(g_down), down_x, links.c(down_x)]
        )
        gate_gradient = place_columns(rank, ff_parts, planes, piece, 0)
        up_gradient = place_columns(rank, ff_parts, planes, piece, 1)
        *attn_chips, down_gradient, gate_gradient, up_gradient = sync(
            *attn_chips, down_gradient, gate_gradient, up_gradient
        )
        norm_parts = links.sum_planes(after(norm_plane, attn_chips[1]))
        query_gradient, key_gradient, value_gradient, output_gradient = place_attention(
            rank, by_rank(attn_chips)
        )
        grad_tokens, out_tokens = take_blocks(seq_of, taken, got)
        norm_own = lax.dynamic_slice(
            norm_parts, (0, group_me * prenorm_gain.shape[0]), (2, prenorm_gain.shape[0])
        )
        return (
            out_tokens,
            grad_tokens,
            query_gradient,
            key_gradient,
            value_gradient,
            output_gradient,
            gate_gradient,
            up_gradient,
            down_gradient,
            norm_own[0],
            norm_own[1],
        )

    return body


def solution(mesh):
    planes = mesh.shape["fsdp"] // 2
    grid = Mesh(mesh.devices.reshape(planes, 2, 2, 2), AXES)
    rows = ("z", "y")
    stream = P(None, rows, ("x", "c"))
    weight = P(rows, None)
    gain = P(rows)
    return jax.shard_map(
        make_body(planes),
        mesh=grid,
        in_specs=(stream, stream) + (weight,) * 7 + (gain, gain, P(), P()),
        out_specs=(stream, stream) + (weight,) * 7 + (gain, gain),
        check_vma=False,
    )
```

```python
import math

import jax
import jax.numpy as jnp
from jax import lax
from jax.experimental import pallas as pl
from jax.experimental.pallas import tpu as pltpu
from jax.sharding import Mesh
from jax.sharding import PartitionSpec as P

QUERY_HEADS = 8
KEY_VALUE_HEADS = 4
HEAD_SIZE = 256

EPS_NORM = 1e-06
ROPE_BASE = 1000042.0
MASK_FILL = -1e30
AXES = ("z", "y", "x", "c")
F32 = jnp.float32
BF16 = jnp.bfloat16


def dot(a, b, dims):
    return lax.dot_general(a, b, (dims, ((), ())), preferred_element_type=F32)


def mm(a, b):
    return dot(a, b, ((1,), (0,)))


def mm_nt(a, b):
    return dot(a, b, ((1,), (1,)))


def mm_tn(a, b):
    return dot(a, b, ((0,), (0,)))


def sync(*values):
    return lax.optimization_barrier(values)


def after(value, *others):
    return lax.optimization_barrier((value,) + others)[0]


class Links:
    def __init__(self, planes):
        self.planes = planes

        def pairs(move):
            out = []
            for z in range(planes):
                for y in range(2):
                    for x in range(2):
                        for c in range(2):
                            a, b, d, e = move(z, y, x, c)
                            out.append((((z * 2 + y) * 2 + x) * 2 + c, ((a * 2 + b) * 2 + d) * 2 + e))
            return out

        self.px = pairs(lambda z, y, x, c: (z, y, 1 - x, c))
        self.py = pairs(lambda z, y, x, c: (z, 1 - y, x, c))
        self.pxy = pairs(lambda z, y, x, c: (z, 1 - y, 1 - x, c))
        self.pc = pairs(lambda z, y, x, c: (z, y, x, 1 - c))
        self.pz = [
            pairs(lambda z, y, x, c, k=k: ((z + k) % planes, y, x, c)) for k in range(planes)
        ]
        self.pz_swap = []
        k = 1
        while k < planes:
            self.pz_swap.append(pairs(lambda z, y, x, c, k=k: (z ^ k, y, x, c)))
            k *= 2

    def x(self, a):
        return lax.ppermute(a, AXES, self.px)

    def y(self, a):
        return lax.ppermute(a, AXES, self.py)

    def c(self, a):
        return lax.ppermute(a, AXES, self.pc)

    def swap_chips(self, chunks):
        return [
            chunks[0],
            self.x(chunks[1]),
            self.y(chunks[2]),
            lax.ppermute(chunks[3], AXES, self.pxy),
        ]

    def sum_plane(self, a):
        for p in (self.pc, self.px, self.py):
            a = a + lax.ppermute(a, AXES, p)
        return a

    def sum_planes(self, a):
        for p in self.pz_swap:
            a = a + lax.ppermute(a, AXES, p)
        return a

    def gather_one(self, a):
        return self.x(a), self.y(a)

    def gather_two(self, ax, ay):
        m = ax.shape[0] // 2
        return self.x(ay[:m]), self.y(ax[m:])

    def scatter_one(self, left, right):
        n = left.shape[0] // 4
        l4 = left.reshape(4, n, left.shape[1])
        return self.x(jnp.stack([l4[1], l4[3]])), self.y(right[2 * n :].reshape(2, n, right.shape[1]))

    def scatter_two(self, left, right, gl, gr):
        n = left.shape[0] // 4
        l_far = self.y((left[2 * n : 3 * n].astype(F32) + gl[1]).astype(BF16))
        r_far = self.x((right[n : 2 * n].astype(F32) + gr[1]).astype(BF16))
        return l_far, r_far

    def scatter_end(self, left, right, gl, gr, l_far, r_far):
        n = left.shape[0] // 4
        gl, gr, l_far, r_far = sync(gl, gr, l_far, r_far)
        l_own = left[:n].astype(F32) + gl[0] + l_far
        r_own = right[:n].astype(F32) + gr[0] + r_far
        return jnp.concatenate([l_own, r_own], axis=1)

    def gather_planes(self, a):
        got = lax.all_gather(a, ("c", "z"), axis=0, tiled=True)
        return got.reshape(2, self.planes * a.shape[0], a.shape[1])

    def gather_gains(self, a):
        n = a.shape[1]
        y_me = lax.axis_index("y")
        z_me = lax.axis_index("z")
        two = pair(y_me, a, self.y(a))
        out = jnp.zeros((self.planes,) + two.shape, a.dtype)
        for k in range(self.planes):
            part = two if k == 0 else lax.ppermute(two, AXES, self.pz[k])
            at = lax.rem(z_me - k + self.planes, self.planes)
            out = lax.dynamic_update_slice(out, part[None], (at, 0, 0, 0))
        return jnp.transpose(out, (2, 0, 1, 3)).reshape(2, 2 * self.planes * n)


def pair(bit, own, other):
    return jnp.stack([jnp.where(bit == 0, own, other), jnp.where(bit == 0, other, own)])


def estimate(flops, bytes_accessed, transcendentals):
    return pl.CostEstimate(
        flops=flops, bytes_accessed=bytes_accessed, transcendentals=transcendentals
    )


def rank_scalar(rank):
    return jnp.reshape(rank, (1,)).astype(jnp.int32)


def place_columns(rank, parts, planes, piece, side):
    n = parts[0].shape[0]
    width = planes * piece
    total = 8 * width
    if piece % 128:
        parts = [t[:, side * width : (side + 1) * width] for t in parts]
        out = jnp.zeros((n, planes, 8, piece), F32)
        for p, part in enumerate(parts):
            part = part.reshape(n, planes, 1, piece).astype(F32)
            out = lax.dynamic_update_slice(out, part, (0, 0, jnp.bitwise_xor(rank, p), 0))
        return out.reshape(n, total)
    tile = min(n, 128)

    def kernel(rank_ref, *refs):
        out = refs[8]
        for p in range(8):
            t = jnp.bitwise_xor(rank_ref[0], p)
            for z in range(planes):
                at = pl.multiple_of(z * 8 * piece + t * piece, 128)
                out[:, pl.ds(at, piece)] = refs[p][:, z * piece : (z + 1) * piece].astype(F32)

    return pl.pallas_call(
        kernel,
        out_shape=jax.ShapeDtypeStruct((n, total), F32),
        grid_spec=pltpu.PrefetchScalarGridSpec(
            num_scalar_prefetch=1,
            grid=(n // tile,),
            in_specs=[pl.BlockSpec((tile, width), lambda i, r: (i, side))] * 8,
            out_specs=pl.BlockSpec((tile, total), lambda i, r: (i, 0)),
        ),
        cost_estimate=estimate(flops=0, bytes_accessed=6 * n * total, transcendentals=0),
    )(rank_scalar(rank), *parts)


def place_rows(order, parts):
    n, d = parts[0].shape
    tile = min(n, 128)

    def kernel(order_ref, *refs):
        for p in range(4):
            refs[4][jnp.bitwise_xor(order_ref[0], p)] = refs[p][...].astype(F32)

    out = pl.pallas_call(
        kernel,
        out_shape=jax.ShapeDtypeStruct((4, n, d), F32),
        grid_spec=pltpu.PrefetchScalarGridSpec(
            num_scalar_prefetch=1,
            grid=(n // tile,),
            in_specs=[pl.BlockSpec((tile, d), lambda i, r: (i, 0))] * 4,
            out_specs=pl.BlockSpec((4, tile, d), lambda i, r: (0, i, 0)),
        ),
        cost_estimate=estimate(flops=0, bytes_accessed=24 * n * d, transcendentals=0),
    )(rank_scalar(order), *parts)
    return out.reshape(4 * n, d)


def place_attention(rank, parts):
    n, width = parts[0].shape
    h = HEAD_SIZE
    o = width - 2 * h
    tile = min(n, 128)

    def kernel(rank_ref, *refs):
        q_out, k_out, v_out, o_out = refs[8:]
        for p in range(8):
            t = jnp.bitwise_xor(rank_ref[0], p)
            j = t // 2
            core = t - 2 * j
            q_out[:, pl.ds(pl.multiple_of(t * h, 128), h)] = refs[p][:, :h].astype(F32)
            at = pl.ds(pl.multiple_of(j * h, 128), h)

            @pl.when(core == 0)
            def _():
                k_out[:, at] = refs[p][:, h : 2 * h].astype(F32)

            @pl.when(core == 1)
            def _():
                v_out[:, at] = refs[p][:, h : 2 * h].astype(F32)

            to = pl.multiple_of(core * 4 * o + j * o, 128)
            o_out[:, pl.ds(to, o)] = refs[p][:, 2 * h :].astype(F32)

    widths = (8 * h, 4 * h, 4 * h, 8 * o)
    return pl.pallas_call(
        kernel,
        out_shape=tuple(jax.ShapeDtypeStruct((n, w), F32) for w in widths),
        grid_spec=pltpu.PrefetchScalarGridSpec(
            num_scalar_prefetch=1,
            grid=(n // tile,),
            in_specs=[pl.BlockSpec((tile, width), lambda i, r: (i, 0))] * 8,
            out_specs=tuple(pl.BlockSpec((tile, w), lambda i, r: (i, 0)) for w in widths),
        ),
        cost_estimate=estimate(flops=0, bytes_accessed=48 * n * width, transcendentals=0),
    )(rank_scalar(rank), *parts)


def back_product(core, lefts, weight):
    m, k = lefts[0].shape
    n = weight.shape[1]
    tile = min(n // 2, 256)
    steps = n // 2 // tile

    def kernel(core_ref, a0, a1, l0, l1, r0, r1, left, right):
        left[...] = (mm_nt(a0[...], l0[...]) + mm_nt(a1[...], l1[...])).astype(BF16)
        right[...] = (mm_nt(a0[...], r0[...]) + mm_nt(a1[...], r1[...])).astype(BF16)

    whole = pl.BlockSpec((m, k), lambda i, r: (0, 0))
    out = pl.BlockSpec((m, tile), lambda i, r: (0, i))
    return pl.pallas_call(
        kernel,
        out_shape=(jax.ShapeDtypeStruct((m, n // 2), BF16),) * 2,
        grid_spec=pltpu.PrefetchScalarGridSpec(
            num_scalar_prefetch=1,
            grid=(steps,),
            in_specs=[
                whole,
                whole,
                pl.BlockSpec((None, tile, k), lambda i, r: (r[0], i, 0)),
                pl.BlockSpec((None, tile, k), lambda i, r: (1 - r[0], i, 0)),
                pl.BlockSpec((None, tile, k), lambda i, r: (r[0], i + steps, 0)),
                pl.BlockSpec((None, tile, k), lambda i, r: (1 - r[0], i + steps, 0)),
            ],
            out_specs=(out, out),
        ),
        cost_estimate=estimate(
            flops=4 * m * k * n, bytes_accessed=4 * (m + n) * k + 2 * m * n, transcendentals=0
        ),
    )(rank_scalar(core), *lefts, weight, weight, weight, weight)


def weight_product(left, right, other=None):
    m, k = left.shape
    n = right.shape[1]
    tile = 256

    def kernel(a, b, *refs):
        total = mm(a[...], b[...])
        if other is not None:
            total = total + refs[0][...]
        refs[-1][...] = total.astype(BF16)

    out = pl.BlockSpec((m, tile), lambda i: (0, i))
    more = () if other is None else (other,)
    return pl.pallas_call(
        kernel,
        out_shape=jax.ShapeDtypeStruct((m, n), BF16),
        grid=(n // tile,),
        in_specs=[
            pl.BlockSpec((m, k), lambda i: (0, 0)),
            pl.BlockSpec((k, tile), lambda i: (0, i)),
        ]
        + [out] * len(more),
        out_specs=out,
        cost_estimate=estimate(
            flops=2 * m * k * n,
            bytes_accessed=2 * (m * k + k * n + (1 + len(more)) * m * n),
            transcendentals=0,
        ),
    )(left, right, *more)


def ff_front(half, n2, weight):
    m, d = n2.shape
    f = weight.shape[2] // 2
    tile = 256
    steps = f // tile

    def kernel(half_ref, x, wg, wu, gate_out, up_out, act_out):
        gate = mm(x[...], wg[...])
        up = mm(x[...], wu[...])
        gate_out[...] = gate
        up_out[...] = up
        act_out[...] = (gate * jax.nn.sigmoid(gate) * up).astype(BF16)

    out = pl.BlockSpec((m, tile), lambda i, r: (0, i))
    return pl.pallas_call(
        kernel,
        out_shape=(
            jax.ShapeDtypeStruct((m, f), F32),
            jax.ShapeDtypeStruct((m, f), F32),
            jax.ShapeDtypeStruct((m, f), BF16),
        ),
        grid_spec=pltpu.PrefetchScalarGridSpec(
            num_scalar_prefetch=1,
            grid=(steps,),
            in_specs=[
                pl.BlockSpec((m, d), lambda i, r: (0, 0)),
                pl.BlockSpec((None, d, tile), lambda i, r: (r[0], 0, i)),
                pl.BlockSpec((None, d, tile), lambda i, r: (r[0], 0, i + steps)),
            ],
            out_specs=(out, out, out),
        ),
        cost_estimate=estimate(
            flops=4 * m * d * f, bytes_accessed=2 * m * d + 4 * d * f + 10 * m * f, transcendentals=m * f
        ),
    )(rank_scalar(half), n2, weight, weight)


def ff_back(half, d_in, weight, gate_pre, up_pre):
    m, d = d_in.shape
    f = weight.shape[1]
    tile = 256
    steps = f // tile

    def kernel(half_ref, g, w, gate_ref, up_ref, out, kept):
        i = pl.program_id(0)

        @pl.when(i < steps)
        def _():
            act_grad = mm_nt(g[...], w[...])
            gate = gate_ref[...]
            sig = jax.nn.sigmoid(gate)
            out[...] = (act_grad * up_ref[...] * sig * (1.0 + gate * (1.0 - sig))).astype(BF16)
            kept[i] = (act_grad * (gate * sig)).astype(BF16)

        @pl.when(i >= steps)
        def _():
            out[...] = kept[i - steps]

    last = steps - 1
    pre = pl.BlockSpec((m, tile), lambda i, r: (0, jnp.minimum(i, last)))
    return pl.pallas_call(
        kernel,
        out_shape=jax.ShapeDtypeStruct((m, 2 * f), BF16),
        grid_spec=pltpu.PrefetchScalarGridSpec(
            num_scalar_prefetch=1,
            grid=(2 * steps,),
            in_specs=[
                pl.BlockSpec((m, d), lambda i, r: (0, 0)),
                pl.BlockSpec((None, tile, d), lambda i, r: (r[0], jnp.minimum(i, last), 0)),
                pre,
                pre,
            ],
            out_specs=pl.BlockSpec((m, tile), lambda i, r: (0, i)),
            scratch_shapes=[pltpu.VMEM((steps, m, tile), BF16)],
        ),
        cost_estimate=estimate(
            flops=2 * m * d * f, bytes_accessed=2 * (m + f) * d + 12 * m * f, transcendentals=m * f
        ),
    )(rank_scalar(half), d_in, weight, gate_pre, up_pre)


def forward_product(core, lefts, weight):
    m, k = lefts[0].shape
    n = weight.shape[2]
    tile = 256
    steps = n // 2 // tile

    def kernel(core_ref, a0, a1, l0, l1, r0, r1, left, right):
        left[...] = (mm(a0[...], l0[...]) + mm(a1[...], l1[...])).astype(BF16)
        right[...] = (mm(a0[...], r0[...]) + mm(a1[...], r1[...])).astype(BF16)

    whole = pl.BlockSpec((m, k), lambda i, r: (0, 0))
    out = pl.BlockSpec((m, tile), lambda i, r: (0, i))
    return pl.pallas_call(
        kernel,
        out_shape=(jax.ShapeDtypeStruct((m, n // 2), BF16),) * 2,
        grid_spec=pltpu.PrefetchScalarGridSpec(
            num_scalar_prefetch=1,
            grid=(steps,),
            in_specs=[
                whole,
                whole,
                pl.BlockSpec((None, k, tile), lambda i, r: (r[0], 0, i)),
                pl.BlockSpec((None, k, tile), lambda i, r: (1 - r[0], 0, i)),
                pl.BlockSpec((None, k, tile), lambda i, r: (r[0], 0, i + steps)),
                pl.BlockSpec((None, k, tile), lambda i, r: (1 - r[0], 0, i + steps)),
            ],
            out_specs=(out, out),
        ),
        cost_estimate=estimate(
            flops=4 * m * k * n, bytes_accessed=4 * (m + n) * k + 2 * m * n, transcendentals=0
        ),
    )(rank_scalar(core), *lefts, weight, weight, weight, weight)


def send_blocks(slot, has, stream):
    groups = slot.shape[0]
    _, r, f = stream.shape
    count = 8

    def kernel(slot_ref, has_ref, *refs):
        for i in range(count):
            v = refs[i][0]
            keep = has_ref[pl.program_id(0) * count + i] > 0
            refs[count][i] = jnp.where(keep, v, jnp.zeros_like(v))

    return pl.pallas_call(
        kernel,
        out_shape=jax.ShapeDtypeStruct((groups, r, f), BF16),
        grid_spec=pltpu.PrefetchScalarGridSpec(
            num_scalar_prefetch=2,
            grid=(groups // count,),
            in_specs=[
                pl.BlockSpec((1, r, f), lambda g, s, h, i=i: (s[g * count + i], 0, 0))
                for i in range(count)
            ],
            out_specs=pl.BlockSpec((count, r, f), lambda g, s, h: (g, 0, 0)),
        ),
        cost_estimate=estimate(flops=0, bytes_accessed=4 * groups * r * f, transcendentals=0),
    )(slot, has, *[stream] * count)


def take_blocks(slot, has, got):
    slots = slot.shape[0]
    _, _, r, f = got.shape

    def kernel(slot_ref, has_ref, *refs):
        for i in range(slots):
            keep = has_ref[i] > 0
            for k in range(2):
                v = refs[i][0, k]
                refs[slots + k][i] = jnp.where(keep, v, jnp.zeros_like(v))

    out = pl.BlockSpec((slots, r, f), lambda g, s, h: (0, 0, 0))
    return pl.pallas_call(
        kernel,
        out_shape=(jax.ShapeDtypeStruct((slots, r, f), BF16),) * 2,
        grid_spec=pltpu.PrefetchScalarGridSpec(
            num_scalar_prefetch=2,
            grid=(1,),
            in_specs=[
                pl.BlockSpec((1, 2, r, f), lambda g, s, h, i=i: (s[i], 0, 0, 0))
                for i in range(slots)
            ],
            out_specs=(out, out),
        ),
        cost_estimate=estimate(flops=0, bytes_accessed=8 * slots * r * f, transcendentals=0),
    )(slot, has, *[got] * slots)


def assemble_rows(info, pieces, gain=None):
    _, _, r, f = pieces[0].shape
    width = 4 * f

    def block(i, n):
        return 2 * jnp.bitwise_xor(n[0], (i // 2) % 2) + i % 2

    def kernel(info_ref, *refs):
        own, ax, ay, dx, dy = refs[:5]
        i = pl.program_id(0)
        x = info_ref[0]
        near = i < 4
        low = block(i, info_ref) < 2
        same = jnp.where(near, own[0], ay[0])
        other = jnp.where(near, ax[0], jnp.where(low, dx[0], dy[0]))
        at = info_ref[2 + i] * r + lax.broadcasted_iota(jnp.int32, (r, f), 0)
        inside = at < info_ref[1]
        parts = []
        for h, v in ((x, same), (1 - x, other)):
            for c in range(2):
                t = jnp.where(inside, v[c].astype(F32), 0.0)
                parts.append((2 * h + c, t))
        if gain is None:
            for q, t in parts:
                refs[5][:, pl.ds(pl.multiple_of(q * f, 128), f)] = t.astype(BF16)
            return
        gain_ref, normed, rows = refs[5:]
        total = sum(jnp.sum(t * t, axis=1, keepdims=True) for _, t in parts)
        factor = lax.rsqrt(total * (1.0 / width) + EPS_NORM)
        for q, t in parts:
            g = gain_ref[pl.ds(q, 1), :]
            normed[:, pl.ds(pl.multiple_of(q * f, 128), f)] = (t * factor * g).astype(BF16)

        @pl.when(i < 2)
        def _():
            for q, t in parts:
                rows[:, pl.ds(pl.multiple_of(q * f, 128), f)] = t.astype(BF16)

    whole = pl.BlockSpec((1, 2, r, f), lambda i, n: (block(i, n), 0, 0, 0))
    specs = [
        whole,
        whole,
        whole,
        pl.BlockSpec((1, 2, r, f), lambda i, n: (jnp.minimum(block(i, n), 1), 0, 0, 0)),
        pl.BlockSpec((1, 2, r, f), lambda i, n: (jnp.maximum(block(i, n) - 2, 0), 0, 0, 0)),
    ]
    shape = [jax.ShapeDtypeStruct((8 * r, width), BF16)]
    outs = [pl.BlockSpec((r, width), lambda i, n: (i, 0))]
    args = list(pieces)
    if gain is not None:
        specs.append(pl.BlockSpec((4, f), lambda i, n: (0, 0)))
        args.append(gain)
        shape.append(jax.ShapeDtypeStruct((2 * r, width), BF16))
        outs.append(pl.BlockSpec((r, width), lambda i, n: (jnp.minimum(i, 1), 0)))
    got = pl.pallas_call(
        kernel,
        out_shape=tuple(shape),
        grid_spec=pltpu.PrefetchScalarGridSpec(
            num_scalar_prefetch=1, grid=(8,), in_specs=specs, out_specs=tuple(outs)
        ),
        cost_estimate=estimate(
            flops=16 * r * width, bytes_accessed=40 * r * width, transcendentals=0
        ),
    )(info, *args)
    return got[0] if gain is None else got


def turn(v, cos_t, sin_t, sign):
    h = v.shape[-1] // 2
    a, b = v[:, :h], v[:, h:]
    s = sin_t * sign
    return jnp.concatenate([a * cos_t - b * s, b * cos_t + a * s], axis=-1).astype(BF16)


def project(normed, w_attn, cos_t, sin_t):
    rows, width = normed.shape
    h = HEAD_SIZE
    tile = 256

    def kernel(x_ref, w_ref, c_ref, s_ref, q0, q1, k, v):
        even = mm(x_ref[...], w_ref[0])
        odd = mm(x_ref[...], w_ref[1])
        cos_t, sin_t = c_ref[...], s_ref[...]
        q0[...] = turn(even[:, :h], cos_t, sin_t, 1.0)
        k[...] = turn(even[:, h:], cos_t, sin_t, 1.0)
        q1[...] = turn(odd[:, :h], cos_t, sin_t, 1.0)
        v[...] = odd[:, h:].astype(BF16)

    out = pl.BlockSpec((tile, h), lambda i: (i, 0))
    table = pl.BlockSpec((tile, h // 2), lambda i: (i, 0))
    return pl.pallas_call(
        kernel,
        out_shape=(jax.ShapeDtypeStruct((rows, h), BF16),) * 4,
        grid=(rows // tile,),
        in_specs=[
            pl.BlockSpec((tile, width), lambda i: (i, 0)),
            pl.BlockSpec((2, width, 2 * h), lambda i: (0, 0, 0)),
            table,
            table,
        ],
        out_specs=(out,) * 4,
        cost_estimate=estimate(
            flops=8 * rows * width * h, bytes_accessed=2 * rows * width + 8 * width * h, transcendentals=0
        ),
    )(normed, w_attn, cos_t, sin_t)


def attend(q0, q1, keys, values, w_o, at_q, at_k):
    rows, h = q0.shape
    half = w_o.shape[2]
    tile = 256
    factor = 1.0 / math.sqrt(HEAD_SIZE)

    def kernel(q0_ref, q1_ref, k_ref, v_ref, w_ref, aq_ref, ak_ref, mixed, lse, left, right):
        allowed = ak_ref[...] <= aq_ref[...]
        for i, q_ref in enumerate((q0_ref, q1_ref)):
            scores = jnp.where(allowed, mm_nt(q_ref[...], k_ref[...]) * factor, MASK_FILL)
            top = jnp.max(scores, axis=-1, keepdims=True)
            e = jnp.exp(scores - top)
            total = jnp.sum(e, axis=-1, keepdims=True)
            probs = (e * (1.0 / total)).astype(BF16)
            mixed[:, i * h : (i + 1) * h] = mm(probs, v_ref[...]).astype(BF16)
            lse[i] = top + jnp.log(total)
        left[...] = mm(mixed[...], w_ref[0]).astype(BF16)
        right[...] = mm(mixed[...], w_ref[1]).astype(BF16)

    q_spec = pl.BlockSpec((tile, h), lambda i: (i, 0))
    kv_spec = pl.BlockSpec((rows, h), lambda i: (0, 0))
    out_spec = pl.BlockSpec((tile, half), lambda i: (i, 0))
    return pl.pallas_call(
        kernel,
        out_shape=(
            jax.ShapeDtypeStruct((rows, 2 * h), BF16),
            jax.ShapeDtypeStruct((2, rows, 1), F32),
            jax.ShapeDtypeStruct((rows, half), BF16),
            jax.ShapeDtypeStruct((rows, half), BF16),
        ),
        grid=(rows // tile,),
        in_specs=[
            q_spec,
            q_spec,
            kv_spec,
            kv_spec,
            pl.BlockSpec((2, 2 * h, half), lambda i: (0, 0, 0)),
            pl.BlockSpec((tile, 1), lambda i: (i, 0)),
            pl.BlockSpec((1, rows), lambda i: (0, 0)),
        ],
        out_specs=(
            pl.BlockSpec((tile, 2 * h), lambda i: (i, 0)),
            pl.BlockSpec((2, tile, 1), lambda i: (0, i, 0)),
            out_spec,
            out_spec,
        ),
        cost_estimate=estimate(
            flops=8 * rows * rows * h + 8 * rows * h * half,
            bytes_accessed=12 * rows * h + 8 * h * half + 4 * rows * half,
            transcendentals=2 * rows * rows,
        ),
    )(q0, q1, keys, values, w_o, at_q, at_k)


def attend_back(attn_in, w_o, q0, q1, keys, values, lse, at_q, at_k, cos_t, sin_t):
    rows, h = q0.shape
    half = w_o.shape[2]
    tile = 256
    steps = rows // tile
    factor = 1.0 / math.sqrt(HEAD_SIZE)

    def kernel(
        g_ref, w_ref, q0_ref, q1_ref, k_ref, v_ref, lse_ref, aq_ref, ak_ref, c_ref, s_ref, ca_ref,
        sa_ref, dq0, dq1, dk, dv, k_sum, v_sum,
    ):
        step = pl.program_id(0)

        @pl.when(step == 0)
        def _():
            k_sum[...] = jnp.zeros_like(k_sum)
            v_sum[...] = jnp.zeros_like(v_sum)

        g = g_ref[...]
        dmix = (mm_nt(g[:, :half], w_ref[0]) + mm_nt(g[:, half:], w_ref[1])).astype(BF16)
        allowed = ak_ref[...] <= aq_ref[...]
        for i, (q_ref, dq) in enumerate(((q0_ref, dq0), (q1_ref, dq1))):
            d = dmix[:, i * h : (i + 1) * h]
            scores = jnp.where(allowed, mm_nt(q_ref[...], k_ref[...]) * factor, MASK_FILL)
            probs = jnp.exp(scores - lse_ref[i])
            v_sum[...] += mm_tn(probs.astype(BF16), d)
            prob_grad = mm_nt(d, v_ref[...])
            inner = jnp.sum(prob_grad * probs, axis=-1, keepdims=True)
            score_grad = (probs * (prob_grad - inner)).astype(BF16)
            k_sum[...] += mm_tn(score_grad, q_ref[...])
            rot = (mm(score_grad, k_ref[...]) * factor).astype(BF16).astype(F32)
            dq[...] = turn(rot, c_ref[...], s_ref[...], -1.0)

        @pl.when(step == steps - 1)
        def _():
            rot = (k_sum[...] * factor).astype(BF16).astype(F32)
            dk[...] = turn(rot, ca_ref[...], sa_ref[...], -1.0)
            dv[...] = v_sum[...].astype(BF16)

    q_spec = pl.BlockSpec((tile, h), lambda i: (i, 0))
    kv_spec = pl.BlockSpec((rows, h), lambda i: (0, 0))
    table = pl.BlockSpec((tile, h // 2), lambda i: (i, 0))
    all_table = pl.BlockSpec((rows, h // 2), lambda i: (0, 0))
    return pl.pallas_call(
        kernel,
        out_shape=(jax.ShapeDtypeStruct((rows, h), BF16),) * 4,
        grid=(steps,),
        in_specs=[
            pl.BlockSpec((tile, 2 * half), lambda i: (i, 0)),
            pl.BlockSpec((2, 2 * h, half), lambda i: (0, 0, 0)),
            q_spec,
            q_spec,
            kv_spec,
            kv_spec,
            pl.BlockSpec((2, tile, 1), lambda i: (0, i, 0)),
            pl.BlockSpec((tile, 1), lambda i: (i, 0)),
            pl.BlockSpec((1, rows), lambda i: (0, 0)),
            table,
            table,
            all_table,
            all_table,
        ],
        out_specs=(q_spec, q_spec, kv_spec, kv_spec),
        scratch_shapes=[pltpu.VMEM((rows, h), F32), pltpu.VMEM((rows, h), F32)],
        cost_estimate=estimate(
            flops=20 * rows * rows * h + 8 * rows * h * half,
            bytes_accessed=20 * rows * h + 8 * h * half + 4 * rows * half,
            transcendentals=2 * rows * rows,
        ),
    )(attn_in, w_o, q0, q1, keys, values, lse, at_q, at_k, cos_t, sin_t, cos_t, sin_t)


def rope_tables(positions):
    half_dim = HEAD_SIZE // 2
    frequency = jnp.exp(jnp.arange(half_dim, dtype=F32) * (-2.0 * math.log(ROPE_BASE) / HEAD_SIZE))
    angles = positions.astype(F32)[:, None] * frequency[None, :]
    return jnp.cos(angles), jnp.sin(angles)


def norm_factor(hidden):
    return lax.rsqrt(jnp.mean(hidden * hidden, axis=-1, keepdims=True) + EPS_NORM)


def norm_backward(upstream, hidden, factor, gain_vec):
    scaled = upstream * gain_vec
    gain_part = jnp.sum(upstream * hidden * factor, axis=0)
    inner_sum = jnp.mean(scaled * hidden, axis=-1, keepdims=True)
    return (factor * scaled - hidden * (factor * factor * factor) * inner_sum, gain_part)


def make_body(planes):
    links = Links(planes)

    def body(
        tokens,
        cotangent,
        query_weight,
        key_matrix,
        value_matrix,
        output_weight,
        gate_weight,
        up_weight,
        down_weight,
        prenorm_gain,
        midnorm_gain,
        seq_len,
        stream_order,
    ):
        groups = 2 * planes
        z_me = lax.axis_index("z")
        y_me = lax.axis_index("y")
        x_me = lax.axis_index("x")
        c_me = lax.axis_index("c")
        slots, blk, quarter = tokens.shape
        width = 4 * quarter
        rank = 4 * y_me + 2 * x_me + c_me
        head = 2 * y_me + x_me
        shard = query_weight.shape[0]
        ff = gate_weight.shape[1]
        piece = ff // groups // 4

        nblk = (seq_len + blk - 1) // blk
        member = (stream_order[:, None] == jnp.arange(groups, dtype=jnp.int32)[None, :]).astype(
            jnp.int32
        )
        ordered = jnp.sum(member * nblk[None, :], axis=1)
        firsts = jnp.cumsum(ordered) - ordered
        seq_start = jnp.sum(member * firsts[:, None], axis=0)
        group_me = 2 * z_me + y_me
        offset = lax.rem(group_me - lax.rem(seq_start, groups) + groups, groups)
        has = offset < nblk
        slot_of = jnp.where(has, (seq_start + offset) // groups, 0)
        block_ids = jnp.arange(slots, dtype=jnp.int32) * groups + group_me
        ahead = block_ids[:, None] - seq_start[None, :]
        covers = ((ahead >= 0) & (ahead < nblk[None, :])).astype(jnp.int32)
        seq_of = jnp.sum(covers * jnp.arange(groups, dtype=jnp.int32)[None, :], axis=1)
        taken = jnp.sum(covers, axis=1)

        mine = 2 * z_me + c_me
        picked = jnp.arange(groups, dtype=jnp.int32) == mine
        my_start = jnp.sum(jnp.where(picked, seq_start, 0))
        my_len = jnp.sum(jnp.where(picked, seq_len, 0))

        def block_places(y):
            first = lax.rem(y + my_start, 2)
            plane = lax.rem((my_start + first) // 2, planes)
            k = jnp.arange(4, dtype=jnp.int32)
            if planes == 4:
                k = lax.rem(k - plane + planes, planes)
            return first + 2 * k, plane

        places_own, plane_own = block_places(y_me)
        places_far, _ = block_places(1 - y_me)

        def two_places(places, x):
            return lax.dynamic_slice(places, (2 * x,), (2,))

        places = jnp.concatenate(
            [
                two_places(places_own, x_me),
                two_places(places_own, 1 - x_me),
                two_places(places_far, x_me),
                two_places(places_far, 1 - x_me),
            ]
        )
        info = jnp.concatenate([jnp.stack([x_me, my_len]), places]).astype(jnp.int32)
        positions = (places[:, None] * blk + jnp.arange(blk, dtype=jnp.int32)[None, :]).reshape(-1)
        at_q = positions[:, None]
        at_k = jnp.where(positions < my_len, positions, 1 << 30)[None, :]
        rows = 2 * blk
        valid = (positions[:rows] < my_len).astype(F32)[:, None]

        def send_layout(out_rows):
            left, right = out_rows[:, : 2 * quarter], out_rows[:, 2 * quarter :]
            keep = jnp.where(x_me == 0, left, right)
            got = links.x(jnp.where(x_me == 0, right, left))
            send = pair(x_me, keep, got).reshape(4, blk, 2, quarter)
            send = jnp.transpose(send, (0, 2, 1, 3))
            if planes > 4:
                send = jnp.pad(send, ((0, planes - 4), (0, 0), (0, 0), (0, 0)))
                send = jnp.roll(send, plane_own, axis=0)
            return send.reshape(groups, blk, quarter)

        def own_and_other(g):
            n = g.shape[1]
            own = lax.dynamic_slice(g, (y_me * shard, 0), (shard, n))
            other = lax.dynamic_slice(g, ((1 - y_me) * shard, 0), (shard, n))
            return own, other

        def by_chip(own, other):
            return links.swap_chips([own, own, other, other])

        def by_rank(chips):
            return [links.c(chips[p // 2]) if p % 2 else chips[p // 2] for p in range(8)]

        def plane_rows(own_part, far_part):
            got = links.y(far_part)
            both = pair(y_me, own_part, got)
            return both.reshape(2 * own_part.shape[0], own_part.shape[1])

        def ff_columns(w, r):
            return jnp.concatenate(
                [
                    lax.dynamic_slice(w, (0, p * 8 * piece + r * piece), (shard, piece))
                    for p in range(planes)
                ],
                axis=1,
            )

        far = rank + 4 - 8 * y_me
        def attn_columns(r, ws):
            q = lax.dynamic_slice(ws[0], (0, r * HEAD_SIZE), (shard, HEAD_SIZE))
            j = r // 2
            k = lax.dynamic_slice(ws[1], (0, j * HEAD_SIZE), (shard, HEAD_SIZE))
            v = lax.dynamic_slice(ws[2], (0, j * HEAD_SIZE), (shard, HEAD_SIZE))
            at = lax.rem(r, 2) * (width // 2) + (r // 2) * (width // 8)
            o = lax.dynamic_slice(ws[3], (0, at), (shard, width // 8))
            return jnp.concatenate([q, jnp.where(c_me == 0, k, v), o], axis=1)

        gains = links.gather_gains(jnp.stack([prenorm_gain, midnorm_gain])).astype(F32)

        def to_sequences(stream):
            return send_blocks(slot_of, has.astype(jnp.int32), stream)

        def arranged(got):
            got = got.reshape(planes, 2, blk, quarter)
            if planes > 4:
                got = jnp.roll(got, -plane_own, axis=0)[:4]
            return got

        def exchange(send):
            return lax.all_to_all(send, ("z", "c"), split_axis=0, concat_axis=0, tiled=True)

        send_tokens = to_sequences(tokens)
        got_tokens = exchange(send_tokens)
        *attn_ws, gate_weight, up_weight, down_weight, _ = sync(
            query_weight,
            key_matrix,
            value_matrix,
            output_weight,
            gate_weight,
            up_weight,
            down_weight,
            send_tokens,
        )
        attn_share = plane_rows(attn_columns(rank, attn_ws), attn_columns(far, attn_ws))

        def ff_share(r):
            return jnp.concatenate([ff_columns(gate_weight, r), ff_columns(up_weight, r)], axis=1)

        ff_own, ff_far_rows = ff_share(rank), ff_share(far)
        down_share = lax.dynamic_slice(
            down_weight, ((2 * x_me + c_me) * piece, 0), (piece, width)
        )
        got_tokens, attn_share, ff_own, ff_far_rows, down_share, gains = sync(
            got_tokens, attn_share, ff_own, ff_far_rows, down_share, gains
        )
        w_attn = links.gather_planes(attn_share)
        own = arranged(got_tokens)
        ax, ay = sync(*links.gather_one(own))
        ff_two = plane_rows(ff_own, after(ff_far_rows, own))
        gain_pre, gain_mid = gains[0], gains[1]
        eighth = width // 8

        def spread(chunk_of):
            return links.swap_chips([chunk_of(jnp.bitwise_xor(head, p)) for p in range(4)])

        cos_t, sin_t = rope_tables(positions)
        dx, dy, cos_t, sin_t, ff_two = sync(*links.gather_two(ax, ay), cos_t, sin_t, ff_two)
        w_ff = links.gather_planes(ff_two)
        w_down = links.gather_planes(after(down_share, ff_two))
        normed, rows_in = assemble_rows(info, (own, ax, ay, dx, dy), gain_pre.reshape(4, quarter))
        send_cot = to_sequences(after(cotangent, dx))
        w_attn, normed, send_cot = sync(w_attn, normed, send_cot)
        got_cot = exchange(send_cot)
        w_o_cols = lax.dynamic_index_in_dim(w_attn, c_me, 0, keepdims=False)[:, 2 * HEAD_SIZE :]
        w_o = jnp.zeros((2 * HEAD_SIZE, 4 * eighth), BF16)
        for p, part in enumerate(
            spread(
                lambda t: lax.dynamic_slice(
                    w_o_cols, (t * 2 * HEAD_SIZE, 0), (2 * HEAD_SIZE, eighth)
                )
            )
        ):
            w_o = lax.dynamic_update_slice(w_o, part, (0, jnp.bitwise_xor(head, p) * eighth))
        w_o = pair(c_me, w_o, links.c(w_o))

        q0, q1, keys, values = project(normed, w_attn, cos_t, sin_t)
        mixed, lse, attn_left, attn_right = attend(q0, q1, keys, values, w_o, at_q, at_k)
        hidden_zero = rows_in.astype(F32)
        factor_pre = norm_factor(hidden_zero)
        gl, gr = sync(*links.scatter_one(attn_left, attn_right))
        l_far, r_far = sync(*links.scatter_two(attn_left, attn_right, gl, gr))
        hidden_one = hidden_zero + links.scatter_end(attn_left, attn_right, gl, gr, l_far, r_far)
        factor_mid = norm_factor(hidden_one)
        n_own = (hidden_one * factor_mid * gain_mid).astype(BF16)
        ax, ay, got_cot = sync(*links.gather_one(n_own), got_cot)
        dx, dy = sync(*links.gather_two(ax, ay))
        normed_two = jnp.concatenate([n_own, ax, ay, dx, dy], axis=0)
        own = after(arranged(got_cot), normed_two)
        n_ff = w_ff.shape[2] // 2
        far_gate, far_up, act_far = ff_front(1 - c_me, normed_two, w_ff)
        ax, ay, act_far = sync(*links.gather_one(own), act_far)
        own_gate, own_up, act_own = ff_front(c_me, after(normed_two, ax), w_ff)
        turned = sync(jnp.transpose(after(normed_two, act_own)))[0]
        dx, dy, act_own, turned = sync(*links.gather_two(ax, ay), act_own, turned)
        down_in = assemble_rows(info, (own, ax, ay, dx, dy))

        def far_part(left, right):
            return mm_tn(left, right).astype(BF16)

        def both_cores(left, right, got):
            return (mm_tn(left, right) + got).astype(BF16)

        def over_planes(g):
            return lax.psum_scatter(g, "z", scatter_dimension=0, tiled=True)

        half = width // 2
        down_far = far_part(act_far, down_in)
        sum_down = both_cores(act_own, down_in, links.c(down_far))
        g_down = over_planes(sum_down)
        w_down, d_in = sync(w_down, down_in, sum_down)[:2]
        ff_left, ff_right = forward_product(c_me, (act_own, act_far), w_down)
        ff_left, ff_right, d_in = sync(ff_left, ff_right, d_in)
        ff_l, ff_r = links.scatter_one(ff_left, ff_right)
        in_far = ff_back(1 - c_me, d_in, w_down, far_gate, far_up)
        ff_far = weight_product(turned, in_far)
        ff_l, ff_r, ff_far, in_far = sync(ff_l, ff_r, ff_far, in_far)
        ff_lf, ff_rf = links.scatter_two(ff_left, ff_right, ff_l, ff_r)
        in_own = ff_back(c_me, after(d_in, ff_far), w_down, own_gate, own_up)
        dn_left, dn_right = back_product(c_me, (in_own, in_far), w_ff)
        dn_left, dn_right, in_own, ff_lf, ff_rf, ff_got = sync(
            dn_left, dn_right, in_own, ff_lf, ff_rf, links.c(ff_far)
        )
        dn_l, dn_r = links.scatter_one(dn_left, dn_right)
        sum_ff = weight_product(turned, in_own, ff_got)
        dn_l, dn_r, sum_ff = sync(dn_l, dn_r, sum_ff)
        g_ff = over_planes(sum_ff)
        dn_lf, dn_rf = links.scatter_two(dn_left, dn_right, dn_l, dn_r)
        out_rows = (
            (hidden_one + links.scatter_end(ff_left, ff_right, ff_l, ff_r, ff_lf, ff_rf)) * valid
        ).astype(BF16)
        dn_lf, dn_rf, g_down, out_rows = sync(dn_lf, dn_rf, g_down, out_rows)
        normed_two_grad = links.scatter_end(dn_left, dn_right, dn_l, dn_r, dn_lf, dn_rf)

        mid_upstream, midnorm_part = norm_backward(normed_two_grad, hidden_one, factor_mid, gain_mid)
        hidden_one_grad = down_in[:rows].astype(F32) + mid_upstream
        a_own = hidden_one_grad.astype(BF16)
        ax, ay = sync(*links.gather_one(a_own))
        dx, dy = sync(*links.gather_two(ax, ay))
        attn_in = jnp.concatenate([a_own, ax, ay, dx, dy], axis=0)
        attn_in, g_down, out_rows = sync(attn_in, g_down, out_rows)
        out_send = send_layout(out_rows)
        down_x = links.x(g_down)
        first = c_me == 0
        g_both = mm_tn(mixed, attn_in)
        g_low, g_high = g_both[:, :half], g_both[:, half:]
        out_far = jnp.where(first, g_high, g_low).astype(BF16)
        out_own = jnp.where(first, g_low, g_high)
        dq0, dq1, dk, dv = attend_back(
            after(attn_in, out_far), w_o, q0, q1, keys, values, lse, at_q, at_k, cos_t, sin_t
        )
        g_out = (out_own + links.c(out_far)).astype(BF16)
        grad_even = jnp.concatenate([dq0, dk], axis=1)
        grad_odd = jnp.concatenate([dq1, dv], axis=1)
        normed_part = (
            mm_nt(after(grad_even, g_out), w_attn[0, :, : 2 * HEAD_SIZE])
            + mm_nt(grad_odd, w_attn[1, :, : 2 * HEAD_SIZE])
        ).astype(BF16)
        o_parts = spread(lambda t: lax.dynamic_slice(g_out, (0, t * eighth), (2 * HEAD_SIZE, eighth)))
        normed_part, grad_even, grad_odd, out_send, down_x, *o_parts = sync(
            normed_part, grad_even, grad_odd, out_send, down_x, *o_parts
        )
        np_left, np_right = normed_part[:, :half], normed_part[:, half:]
        np_l, np_r = links.scatter_one(np_left, np_right)
        g_o_cols = jnp.zeros((8 * HEAD_SIZE, eighth), BF16)
        for p, part in enumerate(o_parts):
            g_o_cols = lax.dynamic_update_slice(
                g_o_cols, part, (jnp.bitwise_xor(head, p) * 2 * HEAD_SIZE, 0)
            )
        d_own = jnp.where(first, grad_even, grad_odd)
        d_far = jnp.where(first, grad_odd, grad_even)
        g_qkv = both_cores(normed, d_own, links.c(far_part(normed, d_far)))
        attn_sum = jnp.concatenate([g_qkv, g_o_cols], axis=1)
        np_l, np_r, attn_sum, ff_own, ff_other = sync(
            np_l, np_r, attn_sum, *own_and_other(g_ff)
        )
        g_attn = over_planes(attn_sum)
        np_lf, np_rf = links.scatter_two(np_left, np_right, np_l, np_r)
        ff_x, ff_y = links.x(ff_own), links.y(ff_other)
        np_lf, np_rf = sync(np_lf, np_rf)
        normed_grad = links.scatter_end(np_left, np_right, np_l, np_r, np_lf, np_rf)
        pre_upstream, prenorm_part = norm_backward(normed_grad, hidden_zero, factor_pre, gain_pre)
        token_rows = ((hidden_one_grad + pre_upstream) * valid).astype(BF16)
        norm_plane = links.sum_plane(jnp.stack([prenorm_part, midnorm_part]))
        token_send, norm_plane, ff_x, ff_y, ff_own, ff_other = sync(
            send_layout(token_rows), norm_plane, ff_x, ff_y, ff_own, ff_other
        )
        got = exchange(jnp.stack([token_send, out_send], axis=1))
        ff_d, g_attn = sync(lax.ppermute(ff_other, AXES, links.pxy), g_attn)
        ff_chips = [ff_own, ff_x, ff_y, ff_d]
        attn_chips = by_chip(*own_and_other(g_attn))
        ff_parts = by_rank(ff_chips)
        down_gradient = place_rows(
            2 * x_me + c_me, [g_down, links.c(g_down), down_x, links.c(down_x)]
        )
        gate_gradient = place_columns(rank, ff_parts, planes, piece, 0)
        up_gradient = place_columns(rank, ff_parts, planes, piece, 1)
        *attn_chips, down_gradient, gate_gradient, up_gradient = sync(
            *attn_chips, down_gradient, gate_gradient, up_gradient
        )
        norm_parts = links.sum_planes(after(norm_plane, attn_chips[1]))
        query_gradient, key_gradient, value_gradient, output_gradient = place_attention(
            rank, by_rank(attn_chips)
        )
        grad_tokens, out_tokens = take_blocks(seq_of, taken, got)
        norm_own = lax.dynamic_slice(
            norm_parts, (0, group_me * prenorm_gain.shape[0]), (2, prenorm_gain.shape[0])
        )
        return (
            out_tokens,
            grad_tokens,
            query_gradient,
            key_gradient,
            value_gradient,
            output_gradient,
            gate_gradient,
            up_gradient,
            down_gradient,
            norm_own[0],
            norm_own[1],
        )

    return body


def solution(mesh):
    planes = mesh.shape["fsdp"] // 2
    grid = Mesh(mesh.devices.reshape(planes, 2, 2, 2), AXES)
    rows = ("z", "y")
    stream = P(None, rows, ("x", "c"))
    weight = P(rows, None)
    gain = P(rows)
    return jax.shard_map(
        make_body(planes),
        mesh=grid,
        in_specs=(stream, stream) + (weight,) * 7 + (gain, gain, P(), P()),
        out_specs=(stream, stream) + (weight,) * 7 + (gain, gain),
        check_vma=False,
    )
```

```python
import math

import jax
import jax.numpy as jnp
from jax import lax
from jax.experimental import pallas as pl
from jax.experimental.pallas import tpu as pltpu
from jax.sharding import Mesh
from jax.sharding import PartitionSpec as P

QUERY_HEADS = 8
KEY_VALUE_HEADS = 4
HEAD_SIZE = 256

EPS_NORM = 1e-06
ROPE_BASE = 1000042.0
MASK_FILL = -1e30
AXES = ("z", "y", "x", "c")
F32 = jnp.float32
BF16 = jnp.bfloat16


def dot(a, b, dims):
    return lax.dot_general(a, b, (dims, ((), ())), preferred_element_type=F32)


def mm(a, b):
    return dot(a, b, ((1,), (0,)))


def mm_nt(a, b):
    return dot(a, b, ((1,), (1,)))


def mm_tn(a, b):
    return dot(a, b, ((0,), (0,)))


def sync(*values):
    return lax.optimization_barrier(values)


def after(value, *others):
    return lax.optimization_barrier((value,) + others)[0]


class Links:
    def __init__(self, planes):
        self.planes = planes

        def pairs(move):
            out = []
            for z in range(planes):
                for y in range(2):
                    for x in range(2):
                        for c in range(2):
                            a, b, d, e = move(z, y, x, c)
                            out.append((((z * 2 + y) * 2 + x) * 2 + c, ((a * 2 + b) * 2 + d) * 2 + e))
            return out

        self.px = pairs(lambda z, y, x, c: (z, y, 1 - x, c))
        self.py = pairs(lambda z, y, x, c: (z, 1 - y, x, c))
        self.pxy = pairs(lambda z, y, x, c: (z, 1 - y, 1 - x, c))
        self.pc = pairs(lambda z, y, x, c: (z, y, x, 1 - c))
        self.pz = [
            pairs(lambda z, y, x, c, k=k: ((z + k) % planes, y, x, c)) for k in range(planes)
        ]
        self.pz_swap = []
        k = 1
        while k < planes:
            self.pz_swap.append(pairs(lambda z, y, x, c, k=k: (z ^ k, y, x, c)))
            k *= 2

    def x(self, a):
        return lax.ppermute(a, AXES, self.px)

    def y(self, a):
        return lax.ppermute(a, AXES, self.py)

    def c(self, a):
        return lax.ppermute(a, AXES, self.pc)

    def swap_chips(self, chunks):
        return [
            chunks[0],
            self.x(chunks[1]),
            self.y(chunks[2]),
            lax.ppermute(chunks[3], AXES, self.pxy),
        ]

    def sum_plane(self, a):
        for p in (self.pc, self.px, self.py):
            a = a + lax.ppermute(a, AXES, p)
        return a

    def sum_planes(self, a):
        for p in self.pz_swap:
            a = a + lax.ppermute(a, AXES, p)
        return a

    def gather_one(self, a):
        return self.x(a), self.y(a)

    def gather_two(self, ax, ay):
        m = ax.shape[0] // 2
        return self.x(ay[:m]), self.y(ax[m:])

    def scatter_one(self, p):
        return self.x(p[1]), self.y(p[3])

    def scatter_two(self, p, gl, gr):
        l_far = self.y((p[0][1].astype(F32) + gl[1]).astype(BF16))
        r_far = self.x((p[2][1].astype(F32) + gr[1]).astype(BF16))
        return l_far, r_far

    def scatter_end(self, p, gl, gr, l_far, r_far):
        gl, gr, l_far, r_far = sync(gl, gr, l_far, r_far)
        l_own = p[0][0].astype(F32) + gl[0] + l_far
        r_own = p[2][0].astype(F32) + gr[0] + r_far
        return jnp.concatenate([l_own, r_own], axis=1)

    def gather_planes(self, a):
        got = lax.all_gather(a, ("c", "z"), axis=0, tiled=True)
        return got.reshape(2, self.planes * a.shape[0], a.shape[1])

    def gather_gains(self, a):
        n = a.shape[1]
        y_me = lax.axis_index("y")
        z_me = lax.axis_index("z")
        two = pair(y_me, a, self.y(a))
        out = jnp.zeros((self.planes,) + two.shape, a.dtype)
        for k in range(self.planes):
            part = two if k == 0 else lax.ppermute(two, AXES, self.pz[k])
            at = lax.rem(z_me - k + self.planes, self.planes)
            out = lax.dynamic_update_slice(out, part[None], (at, 0, 0, 0))
        return jnp.transpose(out, (2, 0, 1, 3)).reshape(2, 2 * self.planes * n)


def pair(bit, own, other):
    return jnp.stack([jnp.where(bit == 0, own, other), jnp.where(bit == 0, other, own)])


def estimate(flops, bytes_accessed, transcendentals):
    return pl.CostEstimate(
        flops=flops, bytes_accessed=bytes_accessed, transcendentals=transcendentals
    )


def split_parts(left, right):
    n, h = left.shape[0] // 4, left.shape[1]
    l4, r4 = left.reshape(4, n, h), right.reshape(4, n, h)
    return (
        jnp.stack([l4[0], l4[2]]),
        jnp.stack([l4[1], l4[3]]),
        r4[:2],
        r4[2:],
    )


def store_parts(outs, left, right):
    n = left.shape[0] // 4
    for i in range(4):
        rows = slice(i * n, (i + 1) * n)
        outs[i % 2][i // 2] = left[rows]
        outs[2 + i // 2][i % 2] = right[rows]


def rank_scalar(rank):
    return jnp.reshape(rank, (1,)).astype(jnp.int32)


def place_columns(rank, parts, planes, piece, side):
    n = parts[0].shape[0]
    width = planes * piece
    total = 8 * width
    if piece % 128:
        parts = [t[:, side * width : (side + 1) * width] for t in parts]
        out = jnp.zeros((n, planes, 8, piece), F32)
        for p, part in enumerate(parts):
            part = part.reshape(n, planes, 1, piece).astype(F32)
            out = lax.dynamic_update_slice(out, part, (0, 0, jnp.bitwise_xor(rank, p), 0))
        return out.reshape(n, total)
    tile = min(n, 128)

    def kernel(rank_ref, *refs):
        out = refs[8]
        for p in range(8):
            t = jnp.bitwise_xor(rank_ref[0], p)
            for z in range(planes):
                at = pl.multiple_of(z * 8 * piece + t * piece, 128)
                out[:, pl.ds(at, piece)] = refs[p][:, z * piece : (z + 1) * piece].astype(F32)

    return pl.pallas_call(
        kernel,
        out_shape=jax.ShapeDtypeStruct((n, total), F32),
        grid_spec=pltpu.PrefetchScalarGridSpec(
            num_scalar_prefetch=1,
            grid=(n // tile,),
            in_specs=[pl.BlockSpec((tile, width), lambda i, r: (i, side))] * 8,
            out_specs=pl.BlockSpec((tile, total), lambda i, r: (i, 0)),
        ),
        cost_estimate=estimate(flops=0, bytes_accessed=6 * n * total, transcendentals=0),
    )(rank_scalar(rank), *parts)


def place_rows(order, parts):
    n, d = parts[0].shape
    tile = min(n, 128)

    def kernel(order_ref, *refs):
        for p in range(4):
            refs[4][jnp.bitwise_xor(order_ref[0], p)] = refs[p][...].astype(F32)

    out = pl.pallas_call(
        kernel,
        out_shape=jax.ShapeDtypeStruct((4, n, d), F32),
        grid_spec=pltpu.PrefetchScalarGridSpec(
            num_scalar_prefetch=1,
            grid=(n // tile,),
            in_specs=[pl.BlockSpec((tile, d), lambda i, r: (i, 0))] * 4,
            out_specs=pl.BlockSpec((4, tile, d), lambda i, r: (0, i, 0)),
        ),
        cost_estimate=estimate(flops=0, bytes_accessed=24 * n * d, transcendentals=0),
    )(rank_scalar(order), *parts)
    return out.reshape(4 * n, d)


def place_attention(rank, parts):
    n, width = parts[0].shape
    h = HEAD_SIZE
    o = width - 2 * h
    tile = min(n, 128)

    def kernel(rank_ref, *refs):
        q_out, k_out, v_out, o_out = refs[8:]
        for p in range(8):
            t = jnp.bitwise_xor(rank_ref[0], p)
            j = t // 2
            core = t - 2 * j
            q_out[:, pl.ds(pl.multiple_of(t * h, 128), h)] = refs[p][:, :h].astype(F32)
            at = pl.ds(pl.multiple_of(j * h, 128), h)

            @pl.when(core == 0)
            def _():
                k_out[:, at] = refs[p][:, h : 2 * h].astype(F32)

            @pl.when(core == 1)
            def _():
                v_out[:, at] = refs[p][:, h : 2 * h].astype(F32)

            to = pl.multiple_of(core * 4 * o + j * o, 128)
            o_out[:, pl.ds(to, o)] = refs[p][:, 2 * h :].astype(F32)

    widths = (8 * h, 4 * h, 4 * h, 8 * o)
    return pl.pallas_call(
        kernel,
        out_shape=tuple(jax.ShapeDtypeStruct((n, w), F32) for w in widths),
        grid_spec=pltpu.PrefetchScalarGridSpec(
            num_scalar_prefetch=1,
            grid=(n // tile,),
            in_specs=[pl.BlockSpec((tile, width), lambda i, r: (i, 0))] * 8,
            out_specs=tuple(pl.BlockSpec((tile, w), lambda i, r: (i, 0)) for w in widths),
        ),
        cost_estimate=estimate(flops=0, bytes_accessed=48 * n * width, transcendentals=0),
    )(rank_scalar(rank), *parts)


def back_product(core, lefts, weight):
    m, k = lefts[0].shape
    n = weight.shape[1]
    tile = min(n // 2, 256)
    steps = n // 2 // tile

    def kernel(core_ref, a0, a1, l0, l1, r0, r1, *outs):
        left = (mm_nt(a0[...], l0[...]) + mm_nt(a1[...], l1[...])).astype(BF16)
        right = (mm_nt(a0[...], r0[...]) + mm_nt(a1[...], r1[...])).astype(BF16)
        store_parts(outs, left, right)

    whole = pl.BlockSpec((m, k), lambda i, r: (0, 0))
    out = pl.BlockSpec((2, m // 4, tile), lambda i, r: (0, 0, i))
    return pl.pallas_call(
        kernel,
        out_shape=(jax.ShapeDtypeStruct((2, m // 4, n // 2), BF16),) * 4,
        grid_spec=pltpu.PrefetchScalarGridSpec(
            num_scalar_prefetch=1,
            grid=(steps,),
            in_specs=[
                whole,
                whole,
                pl.BlockSpec((None, tile, k), lambda i, r: (r[0], i, 0)),
                pl.BlockSpec((None, tile, k), lambda i, r: (1 - r[0], i, 0)),
                pl.BlockSpec((None, tile, k), lambda i, r: (r[0], i + steps, 0)),
                pl.BlockSpec((None, tile, k), lambda i, r: (1 - r[0], i + steps, 0)),
            ],
            out_specs=(out,) * 4,
        ),
        cost_estimate=estimate(
            flops=4 * m * k * n, bytes_accessed=4 * (m + n) * k + 2 * m * n, transcendentals=0
        ),
    )(rank_scalar(core), *lefts, weight, weight, weight, weight)


def weight_product(left, right, other=None):
    m, k = left.shape
    n = right.shape[1]
    tile = 256

    def kernel(a, b, *refs):
        total = mm(a[...], b[...])
        if other is not None:
            total = total + refs[0][...]
        refs[-1][...] = total.astype(BF16)

    out = pl.BlockSpec((m, tile), lambda i: (0, i))
    more = () if other is None else (other,)
    return pl.pallas_call(
        kernel,
        out_shape=jax.ShapeDtypeStruct((m, n), BF16),
        grid=(n // tile,),
        in_specs=[
            pl.BlockSpec((m, k), lambda i: (0, 0)),
            pl.BlockSpec((k, tile), lambda i: (0, i)),
        ]
        + [out] * len(more),
        out_specs=out,
        cost_estimate=estimate(
            flops=2 * m * k * n,
            bytes_accessed=2 * (m * k + k * n + (1 + len(more)) * m * n),
            transcendentals=0,
        ),
    )(left, right, *more)


def ff_front(half, n2, weight):
    m, d = n2.shape
    f = weight.shape[2] // 2
    tile = 256
    steps = f // tile

    def kernel(half_ref, x, wg, wu, gate_out, up_out, act_out):
        gate = mm(x[...], wg[...])
        up = mm(x[...], wu[...])
        gate_out[...] = gate
        up_out[...] = up
        act_out[...] = (gate * jax.nn.sigmoid(gate) * up).astype(BF16)

    out = pl.BlockSpec((m, tile), lambda i, r: (0, i))
    return pl.pallas_call(
        kernel,
        out_shape=(
            jax.ShapeDtypeStruct((m, f), F32),
            jax.ShapeDtypeStruct((m, f), F32),
            jax.ShapeDtypeStruct((m, f), BF16),
        ),
        grid_spec=pltpu.PrefetchScalarGridSpec(
            num_scalar_prefetch=1,
            grid=(steps,),
            in_specs=[
                pl.BlockSpec((m, d), lambda i, r: (0, 0)),
                pl.BlockSpec((None, d, tile), lambda i, r: (r[0], 0, i)),
                pl.BlockSpec((None, d, tile), lambda i, r: (r[0], 0, i + steps)),
            ],
            out_specs=(out, out, out),
        ),
        cost_estimate=estimate(
            flops=4 * m * d * f, bytes_accessed=2 * m * d + 4 * d * f + 10 * m * f, transcendentals=m * f
        ),
    )(rank_scalar(half), n2, weight, weight)


def ff_back(half, d_in, weight, gate_pre, up_pre):
    m, d = d_in.shape
    f = weight.shape[1]
    tile = 256
    steps = f // tile

    def kernel(half_ref, g, w, gate_ref, up_ref, out, kept):
        i = pl.program_id(0)

        @pl.when(i < steps)
        def _():
            act_grad = mm_nt(g[...], w[...])
            gate = gate_ref[...]
            sig = jax.nn.sigmoid(gate)
            out[...] = (act_grad * up_ref[...] * sig * (1.0 + gate * (1.0 - sig))).astype(BF16)
            kept[i] = (act_grad * (gate * sig)).astype(BF16)

        @pl.when(i >= steps)
        def _():
            out[...] = kept[i - steps]

    last = steps - 1
    pre = pl.BlockSpec((m, tile), lambda i, r: (0, jnp.minimum(i, last)))
    return pl.pallas_call(
        kernel,
        out_shape=jax.ShapeDtypeStruct((m, 2 * f), BF16),
        grid_spec=pltpu.PrefetchScalarGridSpec(
            num_scalar_prefetch=1,
            grid=(2 * steps,),
            in_specs=[
                pl.BlockSpec((m, d), lambda i, r: (0, 0)),
                pl.BlockSpec((None, tile, d), lambda i, r: (r[0], jnp.minimum(i, last), 0)),
                pre,
                pre,
            ],
            out_specs=pl.BlockSpec((m, tile), lambda i, r: (0, i)),
            scratch_shapes=[pltpu.VMEM((steps, m, tile), BF16)],
        ),
        cost_estimate=estimate(
            flops=2 * m * d * f, bytes_accessed=2 * (m + f) * d + 12 * m * f, transcendentals=m * f
        ),
    )(rank_scalar(half), d_in, weight, gate_pre, up_pre)


def forward_product(core, lefts, weight):
    m, k = lefts[0].shape
    n = weight.shape[2]
    tile = 256
    steps = n // 2 // tile

    def kernel(core_ref, a0, a1, l0, l1, r0, r1, *outs):
        left = (mm(a0[...], l0[...]) + mm(a1[...], l1[...])).astype(BF16)
        right = (mm(a0[...], r0[...]) + mm(a1[...], r1[...])).astype(BF16)
        store_parts(outs, left, right)

    whole = pl.BlockSpec((m, k), lambda i, r: (0, 0))
    out = pl.BlockSpec((2, m // 4, tile), lambda i, r: (0, 0, i))
    return pl.pallas_call(
        kernel,
        out_shape=(jax.ShapeDtypeStruct((2, m // 4, n // 2), BF16),) * 4,
        grid_spec=pltpu.PrefetchScalarGridSpec(
            num_scalar_prefetch=1,
            grid=(steps,),
            in_specs=[
                whole,
                whole,
                pl.BlockSpec((None, k, tile), lambda i, r: (r[0], 0, i)),
                pl.BlockSpec((None, k, tile), lambda i, r: (1 - r[0], 0, i)),
                pl.BlockSpec((None, k, tile), lambda i, r: (r[0], 0, i + steps)),
                pl.BlockSpec((None, k, tile), lambda i, r: (1 - r[0], 0, i + steps)),
            ],
            out_specs=(out,) * 4,
        ),
        cost_estimate=estimate(
            flops=4 * m * k * n, bytes_accessed=4 * (m + n) * k + 2 * m * n, transcendentals=0
        ),
    )(rank_scalar(core), *lefts, weight, weight, weight, weight)


def send_blocks(slot, has, stream):
    groups = slot.shape[0]
    _, r, f = stream.shape
    count = 8

    def kernel(slot_ref, has_ref, *refs):
        for i in range(count):
            v = refs[i][0]
            keep = has_ref[pl.program_id(0) * count + i] > 0
            refs[count][i] = jnp.where(keep, v, jnp.zeros_like(v))

    return pl.pallas_call(
        kernel,
        out_shape=jax.ShapeDtypeStruct((groups, r, f), BF16),
        grid_spec=pltpu.PrefetchScalarGridSpec(
            num_scalar_prefetch=2,
            grid=(groups // count,),
            in_specs=[
                pl.BlockSpec((1, r, f), lambda g, s, h, i=i: (s[g * count + i], 0, 0))
                for i in range(count)
            ],
            out_specs=pl.BlockSpec((count, r, f), lambda g, s, h: (g, 0, 0)),
        ),
        cost_estimate=estimate(flops=0, bytes_accessed=4 * groups * r * f, transcendentals=0),
    )(slot, has, *[stream] * count)


def take_blocks(slot, has, got):
    slots = slot.shape[0]
    _, _, r, f = got.shape

    def kernel(slot_ref, has_ref, *refs):
        for i in range(slots):
            keep = has_ref[i] > 0
            for k in range(2):
                v = refs[i][0, k]
                refs[slots + k][i] = jnp.where(keep, v, jnp.zeros_like(v))

    out = pl.BlockSpec((slots, r, f), lambda g, s, h: (0, 0, 0))
    return pl.pallas_call(
        kernel,
        out_shape=(jax.ShapeDtypeStruct((slots, r, f), BF16),) * 2,
        grid_spec=pltpu.PrefetchScalarGridSpec(
            num_scalar_prefetch=2,
            grid=(1,),
            in_specs=[
                pl.BlockSpec((1, 2, r, f), lambda g, s, h, i=i: (s[i], 0, 0, 0))
                for i in range(slots)
            ],
            out_specs=(out, out),
        ),
        cost_estimate=estimate(flops=0, bytes_accessed=8 * slots * r * f, transcendentals=0),
    )(slot, has, *[got] * slots)


def assemble_rows(info, pieces, gain=None):
    _, _, r, f = pieces[0].shape
    width = 4 * f

    def block(i, n):
        return 2 * jnp.bitwise_xor(n[0], (i // 2) % 2) + i % 2

    def kernel(info_ref, *refs):
        own, ax, ay, dx, dy = refs[:5]
        i = pl.program_id(0)
        x = info_ref[0]
        near = i < 4
        low = block(i, info_ref) < 2
        same = jnp.where(near, own[0], ay[0])
        other = jnp.where(near, ax[0], jnp.where(low, dx[0], dy[0]))
        at = info_ref[2 + i] * r + lax.broadcasted_iota(jnp.int32, (r, f), 0)
        inside = at < info_ref[1]
        parts = []
        for h, v in ((x, same), (1 - x, other)):
            for c in range(2):
                t = jnp.where(inside, v[c].astype(F32), 0.0)
                parts.append((2 * h + c, t))
        if gain is None:
            for q, t in parts:
                refs[5][:, pl.ds(pl.multiple_of(q * f, 128), f)] = t.astype(BF16)
            return
        gain_ref, normed, rows = refs[5:]
        total = sum(jnp.sum(t * t, axis=1, keepdims=True) for _, t in parts)
        factor = lax.rsqrt(total * (1.0 / width) + EPS_NORM)
        for q, t in parts:
            g = gain_ref[pl.ds(q, 1), :]
            normed[:, pl.ds(pl.multiple_of(q * f, 128), f)] = (t * factor * g).astype(BF16)

        @pl.when(i < 2)
        def _():
            for q, t in parts:
                rows[:, pl.ds(pl.multiple_of(q * f, 128), f)] = t.astype(BF16)

    whole = pl.BlockSpec((1, 2, r, f), lambda i, n: (block(i, n), 0, 0, 0))
    specs = [
        whole,
        whole,
        whole,
        pl.BlockSpec((1, 2, r, f), lambda i, n: (jnp.minimum(block(i, n), 1), 0, 0, 0)),
        pl.BlockSpec((1, 2, r, f), lambda i, n: (jnp.maximum(block(i, n) - 2, 0), 0, 0, 0)),
    ]
    shape = [jax.ShapeDtypeStruct((8 * r, width), BF16)]
    outs = [pl.BlockSpec((r, width), lambda i, n: (i, 0))]
    args = list(pieces)
    if gain is not None:
        specs.append(pl.BlockSpec((4, f), lambda i, n: (0, 0)))
        args.append(gain)
        shape.append(jax.ShapeDtypeStruct((2 * r, width), BF16))
        outs.append(pl.BlockSpec((r, width), lambda i, n: (jnp.minimum(i, 1), 0)))
    got = pl.pallas_call(
        kernel,
        out_shape=tuple(shape),
        grid_spec=pltpu.PrefetchScalarGridSpec(
            num_scalar_prefetch=1, grid=(8,), in_specs=specs, out_specs=tuple(outs)
        ),
        cost_estimate=estimate(
            flops=16 * r * width, bytes_accessed=40 * r * width, transcendentals=0
        ),
    )(info, *args)
    return got[0] if gain is None else got


def turn(v, cos_t, sin_t, sign):
    h = v.shape[-1] // 2
    a, b = v[:, :h], v[:, h:]
    s = sin_t * sign
    return jnp.concatenate([a * cos_t - b * s, b * cos_t + a * s], axis=-1).astype(BF16)


def project(normed, w_attn, cos_t, sin_t):
    rows, width = normed.shape
    h = HEAD_SIZE
    tile = 256

    def kernel(x_ref, w_ref, c_ref, s_ref, q0, q1, k, v):
        even = mm(x_ref[...], w_ref[0])
        odd = mm(x_ref[...], w_ref[1])
        cos_t, sin_t = c_ref[...], s_ref[...]
        q0[...] = turn(even[:, :h], cos_t, sin_t, 1.0)
        k[...] = turn(even[:, h:], cos_t, sin_t, 1.0)
        q1[...] = turn(odd[:, :h], cos_t, sin_t, 1.0)
        v[...] = odd[:, h:].astype(BF16)

    out = pl.BlockSpec((tile, h), lambda i: (i, 0))
    table = pl.BlockSpec((tile, h // 2), lambda i: (i, 0))
    return pl.pallas_call(
        kernel,
        out_shape=(jax.ShapeDtypeStruct((rows, h), BF16),) * 4,
        grid=(rows // tile,),
        in_specs=[
            pl.BlockSpec((tile, width), lambda i: (i, 0)),
            pl.BlockSpec((2, width, 2 * h), lambda i: (0, 0, 0)),
            table,
            table,
        ],
        out_specs=(out,) * 4,
        cost_estimate=estimate(
            flops=8 * rows * width * h, bytes_accessed=2 * rows * width + 8 * width * h, transcendentals=0
        ),
    )(normed, w_attn, cos_t, sin_t)


def attend(q0, q1, keys, values, w_o, at_q, at_k):
    rows, h = q0.shape
    half = w_o.shape[2]
    tile = 256
    factor = 1.0 / math.sqrt(HEAD_SIZE)

    def kernel(q0_ref, q1_ref, k_ref, v_ref, w_ref, aq_ref, ak_ref, mixed, lse, left, right):
        allowed = ak_ref[...] <= aq_ref[...]
        for i, q_ref in enumerate((q0_ref, q1_ref)):
            scores = jnp.where(allowed, mm_nt(q_ref[...], k_ref[...]) * factor, MASK_FILL)
            top = jnp.max(scores, axis=-1, keepdims=True)
            e = jnp.exp(scores - top)
            total = jnp.sum(e, axis=-1, keepdims=True)
            probs = (e * (1.0 / total)).astype(BF16)
            mixed[:, i * h : (i + 1) * h] = mm(probs, v_ref[...]).astype(BF16)
            lse[i] = top + jnp.log(total)
        left[...] = mm(mixed[...], w_ref[0]).astype(BF16)
        right[...] = mm(mixed[...], w_ref[1]).astype(BF16)

    q_spec = pl.BlockSpec((tile, h), lambda i: (i, 0))
    kv_spec = pl.BlockSpec((rows, h), lambda i: (0, 0))
    out_spec = pl.BlockSpec((tile, half), lambda i: (i, 0))
    return pl.pallas_call(
        kernel,
        out_shape=(
            jax.ShapeDtypeStruct((rows, 2 * h), BF16),
            jax.ShapeDtypeStruct((2, rows, 1), F32),
            jax.ShapeDtypeStruct((rows, half), BF16),
            jax.ShapeDtypeStruct((rows, half), BF16),
        ),
        grid=(rows // tile,),
        in_specs=[
            q_spec,
            q_spec,
            kv_spec,
            kv_spec,
            pl.BlockSpec((2, 2 * h, half), lambda i: (0, 0, 0)),
            pl.BlockSpec((tile, 1), lambda i: (i, 0)),
            pl.BlockSpec((1, rows), lambda i: (0, 0)),
        ],
        out_specs=(
            pl.BlockSpec((tile, 2 * h), lambda i: (i, 0)),
            pl.BlockSpec((2, tile, 1), lambda i: (0, i, 0)),
            out_spec,
            out_spec,
        ),
        cost_estimate=estimate(
            flops=8 * rows * rows * h + 8 * rows * h * half,
            bytes_accessed=12 * rows * h + 8 * h * half + 4 * rows * half,
            transcendentals=2 * rows * rows,
        ),
    )(q0, q1, keys, values, w_o, at_q, at_k)


def attend_back(attn_in, w_o, q0, q1, keys, values, lse, at_q, at_k, cos_t, sin_t):
    rows, h = q0.shape
    half = w_o.shape[2]
    tile = 256
    steps = rows // tile
    factor = 1.0 / math.sqrt(HEAD_SIZE)

    def kernel(
        g_ref, w_ref, q0_ref, q1_ref, k_ref, v_ref, lse_ref, aq_ref, ak_ref, c_ref, s_ref, ca_ref,
        sa_ref, dq0, dq1, dk, dv, k_sum, v_sum,
    ):
        step = pl.program_id(0)

        @pl.when(step == 0)
        def _():
            k_sum[...] = jnp.zeros_like(k_sum)
            v_sum[...] = jnp.zeros_like(v_sum)

        g = g_ref[...]
        dmix = (mm_nt(g[:, :half], w_ref[0]) + mm_nt(g[:, half:], w_ref[1])).astype(BF16)
        allowed = ak_ref[...] <= aq_ref[...]
        for i, (q_ref, dq) in enumerate(((q0_ref, dq0), (q1_ref, dq1))):
            d = dmix[:, i * h : (i + 1) * h]
            scores = jnp.where(allowed, mm_nt(q_ref[...], k_ref[...]) * factor, MASK_FILL)
            probs = jnp.exp(scores - lse_ref[i])
            v_sum[...] += mm_tn(probs.astype(BF16), d)
            prob_grad = mm_nt(d, v_ref[...])
            inner = jnp.sum(prob_grad * probs, axis=-1, keepdims=True)
            score_grad = (probs * (prob_grad - inner)).astype(BF16)
            k_sum[...] += mm_tn(score_grad, q_ref[...])
            rot = (mm(score_grad, k_ref[...]) * factor).astype(BF16).astype(F32)
            dq[...] = turn(rot, c_ref[...], s_ref[...], -1.0)

        @pl.when(step == steps - 1)
        def _():
            rot = (k_sum[...] * factor).astype(BF16).astype(F32)
            dk[...] = turn(rot, ca_ref[...], sa_ref[...], -1.0)
            dv[...] = v_sum[...].astype(BF16)

    q_spec = pl.BlockSpec((tile, h), lambda i: (i, 0))
    kv_spec = pl.BlockSpec((rows, h), lambda i: (0, 0))
    table = pl.BlockSpec((tile, h // 2), lambda i: (i, 0))
    all_table = pl.BlockSpec((rows, h // 2), lambda i: (0, 0))
    return pl.pallas_call(
        kernel,
        out_shape=(jax.ShapeDtypeStruct((rows, h), BF16),) * 4,
        grid=(steps,),
        in_specs=[
            pl.BlockSpec((tile, 2 * half), lambda i: (i, 0)),
            pl.BlockSpec((2, 2 * h, half), lambda i: (0, 0, 0)),
            q_spec,
            q_spec,
            kv_spec,
            kv_spec,
            pl.BlockSpec((2, tile, 1), lambda i: (0, i, 0)),
            pl.BlockSpec((tile, 1), lambda i: (i, 0)),
            pl.BlockSpec((1, rows), lambda i: (0, 0)),
            table,
            table,
            all_table,
            all_table,
        ],
        out_specs=(q_spec, q_spec, kv_spec, kv_spec),
        scratch_shapes=[pltpu.VMEM((rows, h), F32), pltpu.VMEM((rows, h), F32)],
        cost_estimate=estimate(
            flops=20 * rows * rows * h + 8 * rows * h * half,
            bytes_accessed=20 * rows * h + 8 * h * half + 4 * rows * half,
            transcendentals=2 * rows * rows,
        ),
    )(attn_in, w_o, q0, q1, keys, values, lse, at_q, at_k, cos_t, sin_t, cos_t, sin_t)


def rope_tables(positions):
    half_dim = HEAD_SIZE // 2
    frequency = jnp.exp(jnp.arange(half_dim, dtype=F32) * (-2.0 * math.log(ROPE_BASE) / HEAD_SIZE))
    angles = positions.astype(F32)[:, None] * frequency[None, :]
    return jnp.cos(angles), jnp.sin(angles)


def norm_factor(hidden):
    return lax.rsqrt(jnp.mean(hidden * hidden, axis=-1, keepdims=True) + EPS_NORM)


def norm_backward(upstream, hidden, factor, gain_vec):
    scaled = upstream * gain_vec
    gain_part = jnp.sum(upstream * hidden * factor, axis=0)
    inner_sum = jnp.mean(scaled * hidden, axis=-1, keepdims=True)
    return (factor * scaled - hidden * (factor * factor * factor) * inner_sum, gain_part)


def make_body(planes):
    links = Links(planes)

    def body(
        tokens,
        cotangent,
        query_weight,
        key_matrix,
        value_matrix,
        output_weight,
        gate_weight,
        up_weight,
        down_weight,
        prenorm_gain,
        midnorm_gain,
        seq_len,
        stream_order,
    ):
        groups = 2 * planes
        z_me = lax.axis_index("z")
        y_me = lax.axis_index("y")
        x_me = lax.axis_index("x")
        c_me = lax.axis_index("c")
        slots, blk, quarter = tokens.shape
        width = 4 * quarter
        rank = 4 * y_me + 2 * x_me + c_me
        head = 2 * y_me + x_me
        shard = query_weight.shape[0]
        ff = gate_weight.shape[1]
        piece = ff // groups // 4

        nblk = (seq_len + blk - 1) // blk
        member = (stream_order[:, None] == jnp.arange(groups, dtype=jnp.int32)[None, :]).astype(
            jnp.int32
        )
        ordered = jnp.sum(member * nblk[None, :], axis=1)
        firsts = jnp.cumsum(ordered) - ordered
        seq_start = jnp.sum(member * firsts[:, None], axis=0)
        group_me = 2 * z_me + y_me
        offset = lax.rem(group_me - lax.rem(seq_start, groups) + groups, groups)
        has = offset < nblk
        slot_of = jnp.where(has, (seq_start + offset) // groups, 0)
        block_ids = jnp.arange(slots, dtype=jnp.int32) * groups + group_me
        ahead = block_ids[:, None] - seq_start[None, :]
        covers = ((ahead >= 0) & (ahead < nblk[None, :])).astype(jnp.int32)
        seq_of = jnp.sum(covers * jnp.arange(groups, dtype=jnp.int32)[None, :], axis=1)
        taken = jnp.sum(covers, axis=1)

        mine = 2 * z_me + c_me
        picked = jnp.arange(groups, dtype=jnp.int32) == mine
        my_start = jnp.sum(jnp.where(picked, seq_start, 0))
        my_len = jnp.sum(jnp.where(picked, seq_len, 0))

        def block_places(y):
            first = lax.rem(y + my_start, 2)
            plane = lax.rem((my_start + first) // 2, planes)
            k = jnp.arange(4, dtype=jnp.int32)
            if planes == 4:
                k = lax.rem(k - plane + planes, planes)
            return first + 2 * k, plane

        places_own, plane_own = block_places(y_me)
        places_far, _ = block_places(1 - y_me)

        def two_places(places, x):
            return lax.dynamic_slice(places, (2 * x,), (2,))

        places = jnp.concatenate(
            [
                two_places(places_own, x_me),
                two_places(places_own, 1 - x_me),
                two_places(places_far, x_me),
                two_places(places_far, 1 - x_me),
            ]
        )
        info = jnp.concatenate([jnp.stack([x_me, my_len]), places]).astype(jnp.int32)
        positions = (places[:, None] * blk + jnp.arange(blk, dtype=jnp.int32)[None, :]).reshape(-1)
        at_q = positions[:, None]
        at_k = jnp.where(positions < my_len, positions, 1 << 30)[None, :]
        rows = 2 * blk
        valid = (positions[:rows] < my_len).astype(F32)[:, None]

        def send_layout(out_rows):
            left, right = out_rows[:, : 2 * quarter], out_rows[:, 2 * quarter :]
            keep = jnp.where(x_me == 0, left, right)
            got = links.x(jnp.where(x_me == 0, right, left))
            send = pair(x_me, keep, got).reshape(4, blk, 2, quarter)
            send = jnp.transpose(send, (0, 2, 1, 3))
            if planes > 4:
                send = jnp.pad(send, ((0, planes - 4), (0, 0), (0, 0), (0, 0)))
                send = jnp.roll(send, plane_own, axis=0)
            return send.reshape(groups, blk, quarter)

        def own_and_other(g):
            n = g.shape[1]
            own = lax.dynamic_slice(g, (y_me * shard, 0), (shard, n))
            other = lax.dynamic_slice(g, ((1 - y_me) * shard, 0), (shard, n))
            return own, other

        def by_chip(own, other):
            return links.swap_chips([own, own, other, other])

        def by_rank(chips):
            return [links.c(chips[p // 2]) if p % 2 else chips[p // 2] for p in range(8)]

        def plane_rows(own_part, far_part):
            got = links.y(far_part)
            both = pair(y_me, own_part, got)
            return both.reshape(2 * own_part.shape[0], own_part.shape[1])

        def ff_columns(w, r):
            return jnp.concatenate(
                [
                    lax.dynamic_slice(w, (0, p * 8 * piece + r * piece), (shard, piece))
                    for p in range(planes)
                ],
                axis=1,
            )

        far = rank + 4 - 8 * y_me
        def attn_columns(r, ws):
            q = lax.dynamic_slice(ws[0], (0, r * HEAD_SIZE), (shard, HEAD_SIZE))
            j = r // 2
            k = lax.dynamic_slice(ws[1], (0, j * HEAD_SIZE), (shard, HEAD_SIZE))
            v = lax.dynamic_slice(ws[2], (0, j * HEAD_SIZE), (shard, HEAD_SIZE))
            at = lax.rem(r, 2) * (width // 2) + (r // 2) * (width // 8)
            o = lax.dynamic_slice(ws[3], (0, at), (shard, width // 8))
            return jnp.concatenate([q, jnp.where(c_me == 0, k, v), o], axis=1)

        gains = links.gather_gains(jnp.stack([prenorm_gain, midnorm_gain])).astype(F32)

        def to_sequences(stream):
            return send_blocks(slot_of, has.astype(jnp.int32), stream)

        def arranged(got):
            got = got.reshape(planes, 2, blk, quarter)
            if planes > 4:
                got = jnp.roll(got, -plane_own, axis=0)[:4]
            return got

        def exchange(send):
            return lax.all_to_all(send, ("z", "c"), split_axis=0, concat_axis=0, tiled=True)

        send_tokens = to_sequences(tokens)
        got_tokens = exchange(send_tokens)
        *attn_ws, gate_weight, up_weight, down_weight, _ = sync(
            query_weight,
            key_matrix,
            value_matrix,
            output_weight,
            gate_weight,
            up_weight,
            down_weight,
            send_tokens,
        )
        attn_share = plane_rows(attn_columns(rank, attn_ws), attn_columns(far, attn_ws))

        def ff_share(r):
            return jnp.concatenate([ff_columns(gate_weight, r), ff_columns(up_weight, r)], axis=1)

        ff_own, ff_far_rows = ff_share(rank), ff_share(far)
        down_share = lax.dynamic_slice(
            down_weight, ((2 * x_me + c_me) * piece, 0), (piece, width)
        )
        got_tokens, attn_share, ff_own, ff_far_rows, down_share, gains = sync(
            got_tokens, attn_share, ff_own, ff_far_rows, down_share, gains
        )
        w_attn = links.gather_planes(attn_share)
        own = arranged(got_tokens)
        ax, ay = sync(*links.gather_one(own))
        ff_two = plane_rows(ff_own, after(ff_far_rows, own))
        gain_pre, gain_mid = gains[0], gains[1]
        eighth = width // 8

        def spread(chunk_of):
            return links.swap_chips([chunk_of(jnp.bitwise_xor(head, p)) for p in range(4)])

        cos_t, sin_t = rope_tables(positions)
        dx, dy, cos_t, sin_t, ff_two = sync(*links.gather_two(ax, ay), cos_t, sin_t, ff_two)
        w_ff = links.gather_planes(ff_two)
        w_down = links.gather_planes(after(down_share, ff_two))
        normed, rows_in = assemble_rows(info, (own, ax, ay, dx, dy), gain_pre.reshape(4, quarter))
        send_cot = to_sequences(after(cotangent, dx))
        w_attn, normed, send_cot = sync(w_attn, normed, send_cot)
        got_cot = exchange(send_cot)
        w_o_cols = lax.dynamic_index_in_dim(w_attn, c_me, 0, keepdims=False)[:, 2 * HEAD_SIZE :]
        w_o = jnp.zeros((2 * HEAD_SIZE, 4 * eighth), BF16)
        for p, part in enumerate(
            spread(
                lambda t: lax.dynamic_slice(
                    w_o_cols, (t * 2 * HEAD_SIZE, 0), (2 * HEAD_SIZE, eighth)
                )
            )
        ):
            w_o = lax.dynamic_update_slice(w_o, part, (0, jnp.bitwise_xor(head, p) * eighth))
        w_o = pair(c_me, w_o, links.c(w_o))

        q0, q1, keys, values = project(normed, w_attn, cos_t, sin_t)
        mixed, lse, attn_left, attn_right = attend(q0, q1, keys, values, w_o, at_q, at_k)
        hidden_zero = rows_in.astype(F32)
        factor_pre = norm_factor(hidden_zero)
        attn_p = split_parts(attn_left, attn_right)
        gl, gr = sync(*links.scatter_one(attn_p))
        l_far, r_far = sync(*links.scatter_two(attn_p, gl, gr))
        hidden_one = hidden_zero + links.scatter_end(attn_p, gl, gr, l_far, r_far)
        factor_mid = norm_factor(hidden_one)
        n_own = (hidden_one * factor_mid * gain_mid).astype(BF16)
        ax, ay, got_cot = sync(*links.gather_one(n_own), got_cot)
        dx, dy = sync(*links.gather_two(ax, ay))
        normed_two = jnp.concatenate([n_own, ax, ay, dx, dy], axis=0)
        own = after(arranged(got_cot), normed_two)
        n_ff = w_ff.shape[2] // 2
        far_gate, far_up, act_far = ff_front(1 - c_me, normed_two, w_ff)
        ax, ay, act_far = sync(*links.gather_one(own), act_far)
        own_gate, own_up, act_own = ff_front(c_me, after(normed_two, ax), w_ff)
        turned = sync(jnp.transpose(after(normed_two, act_own)))[0]
        dx, dy, act_own, turned = sync(*links.gather_two(ax, ay), act_own, turned)
        down_in = assemble_rows(info, (own, ax, ay, dx, dy))

        def far_part(left, right):
            return mm_tn(left, right).astype(BF16)

        def both_cores(left, right, got):
            return (mm_tn(left, right) + got).astype(BF16)

        def over_planes(g):
            return lax.psum_scatter(g, "z", scatter_dimension=0, tiled=True)

        half = width // 2
        down_far = far_part(act_far, down_in)
        sum_down = both_cores(act_own, down_in, links.c(down_far))
        g_down = over_planes(sum_down)
        w_down, d_in = sync(w_down, down_in, sum_down)[:2]
        *ff_p, d_in = sync(*forward_product(c_me, (act_own, act_far), w_down), d_in)
        ff_l, ff_r = links.scatter_one(ff_p)
        in_far = ff_back(1 - c_me, d_in, w_down, far_gate, far_up)
        ff_far = weight_product(turned, in_far)
        ff_l, ff_r, ff_far, in_far = sync(ff_l, ff_r, ff_far, in_far)
        ff_lf, ff_rf = links.scatter_two(ff_p, ff_l, ff_r)
        in_own = ff_back(c_me, after(d_in, ff_far), w_down, own_gate, own_up)
        dn_p = back_product(c_me, (in_own, in_far), w_ff)
        in_own, ff_lf, ff_rf, ff_got, *dn_p = sync(in_own, ff_lf, ff_rf, links.c(ff_far), *dn_p)
        dn_l, dn_r = links.scatter_one(dn_p)
        sum_ff = weight_product(turned, in_own, ff_got)
        dn_l, dn_r, sum_ff = sync(dn_l, dn_r, sum_ff)
        g_ff = over_planes(sum_ff)
        dn_lf, dn_rf = links.scatter_two(dn_p, dn_l, dn_r)
        out_rows = (
            (hidden_one + links.scatter_end(ff_p, ff_l, ff_r, ff_lf, ff_rf)) * valid
        ).astype(BF16)
        dn_lf, dn_rf, g_down, out_rows = sync(dn_lf, dn_rf, g_down, out_rows)
        normed_two_grad = links.scatter_end(dn_p, dn_l, dn_r, dn_lf, dn_rf)

        mid_upstream, midnorm_part = norm_backward(normed_two_grad, hidden_one, factor_mid, gain_mid)
        hidden_one_grad = down_in[:rows].astype(F32) + mid_upstream
        a_own = hidden_one_grad.astype(BF16)
        ax, ay = sync(*links.gather_one(a_own))
        dx, dy = sync(*links.gather_two(ax, ay))
        attn_in = jnp.concatenate([a_own, ax, ay, dx, dy], axis=0)
        attn_in, g_down, out_rows = sync(attn_in, g_down, out_rows)
        out_send = send_layout(out_rows)
        down_x = links.x(g_down)
        first = c_me == 0
        g_both = mm_tn(mixed, attn_in)
        g_low, g_high = g_both[:, :half], g_both[:, half:]
        out_far = jnp.where(first, g_high, g_low).astype(BF16)
        out_own = jnp.where(first, g_low, g_high)
        dq0, dq1, dk, dv = attend_back(
            after(attn_in, out_far), w_o, q0, q1, keys, values, lse, at_q, at_k, cos_t, sin_t
        )
        g_out = (out_own + links.c(out_far)).astype(BF16)
        grad_even = jnp.concatenate([dq0, dk], axis=1)
        grad_odd = jnp.concatenate([dq1, dv], axis=1)
        normed_part = (
            mm_nt(after(grad_even, g_out), w_attn[0, :, : 2 * HEAD_SIZE])
            + mm_nt(grad_odd, w_attn[1, :, : 2 * HEAD_SIZE])
        ).astype(BF16)
        o_parts = spread(lambda t: lax.dynamic_slice(g_out, (0, t * eighth), (2 * HEAD_SIZE, eighth)))
        normed_part, grad_even, grad_odd, out_send, down_x, *o_parts = sync(
            normed_part, grad_even, grad_odd, out_send, down_x, *o_parts
        )
        np_p = split_parts(normed_part[:, :half], normed_part[:, half:])
        np_l, np_r = links.scatter_one(np_p)
        g_o_cols = jnp.zeros((8 * HEAD_SIZE, eighth), BF16)
        for p, part in enumerate(o_parts):
            g_o_cols = lax.dynamic_update_slice(
                g_o_cols, part, (jnp.bitwise_xor(head, p) * 2 * HEAD_SIZE, 0)
            )
        d_own = jnp.where(first, grad_even, grad_odd)
        d_far = jnp.where(first, grad_odd, grad_even)
        g_qkv = both_cores(normed, d_own, links.c(far_part(normed, d_far)))
        attn_sum = jnp.concatenate([g_qkv, g_o_cols], axis=1)
        np_l, np_r, attn_sum, ff_own, ff_other = sync(
            np_l, np_r, attn_sum, *own_and_other(g_ff)
        )
        g_attn = over_planes(attn_sum)
        np_lf, np_rf = links.scatter_two(np_p, np_l, np_r)
        ff_x, ff_y = links.x(ff_own), links.y(ff_other)
        np_lf, np_rf = sync(np_lf, np_rf)
        normed_grad = links.scatter_end(np_p, np_l, np_r, np_lf, np_rf)
        pre_upstream, prenorm_part = norm_backward(normed_grad, hidden_zero, factor_pre, gain_pre)
        token_rows = ((hidden_one_grad + pre_upstream) * valid).astype(BF16)
        norm_plane = links.sum_plane(jnp.stack([prenorm_part, midnorm_part]))
        token_send, norm_plane, ff_x, ff_y, ff_own, ff_other = sync(
            send_layout(token_rows), norm_plane, ff_x, ff_y, ff_own, ff_other
        )
        got = exchange(jnp.stack([token_send, out_send], axis=1))
        ff_d, g_attn = sync(lax.ppermute(ff_other, AXES, links.pxy), g_attn)
        ff_chips = [ff_own, ff_x, ff_y, ff_d]
        attn_chips = by_chip(*own_and_other(g_attn))
        ff_parts = by_rank(ff_chips)
        down_gradient = place_rows(
            2 * x_me + c_me, [g_down, links.c(g_down), down_x, links.c(down_x)]
        )
        gate_gradient = place_columns(rank, ff_parts, planes, piece, 0)
        up_gradient = place_columns(rank, ff_parts, planes, piece, 1)
        *attn_chips, down_gradient, gate_gradient, up_gradient = sync(
            *attn_chips, down_gradient, gate_gradient, up_gradient
        )
        norm_parts = links.sum_planes(after(norm_plane, attn_chips[1]))
        query_gradient, key_gradient, value_gradient, output_gradient = place_attention(
            rank, by_rank(attn_chips)
        )
        grad_tokens, out_tokens = take_blocks(seq_of, taken, got)
        norm_own = lax.dynamic_slice(
            norm_parts, (0, group_me * prenorm_gain.shape[0]), (2, prenorm_gain.shape[0])
        )
        return (
            out_tokens,
            grad_tokens,
            query_gradient,
            key_gradient,
            value_gradient,
            output_gradient,
            gate_gradient,
            up_gradient,
            down_gradient,
            norm_own[0],
            norm_own[1],
        )

    return body


def solution(mesh):
    planes = mesh.shape["fsdp"] // 2
    grid = Mesh(mesh.devices.reshape(planes, 2, 2, 2), AXES)
    rows = ("z", "y")
    stream = P(None, rows, ("x", "c"))
    weight = P(rows, None)
    gain = P(rows)
    return jax.shard_map(
        make_body(planes),
        mesh=grid,
        in_specs=(stream, stream) + (weight,) * 7 + (gain, gain, P(), P()),
        out_specs=(stream, stream) + (weight,) * 7 + (gain, gain),
        check_vma=False,
    )
```
